32 devices in a mesh: meet: 2 (over x), tm: 16 (over z, y, core).
Axes of the slice: x: 2, y: 2, z: 4, core: 2. Of those that a mesh axis runs over, the one named last changes fastest.
Arguments:
- waveform: bfloat16 [8, 327680], P(None, ('meet', 'tm')), parts along dimension 1, may hold values from -16 to 16
- masks: int32 [2, 2048, 257], P(None, ('meet', 'tm')), parts along dimension 1, may hold values from 0 to 255, as said below
- valid: int32 [2], P('meet'), parts along dimension 0, may hold values from 512 to 1024, as said below
- ref_mic: int32 [2], P('meet'), parts along dimension 0, may hold values from 0 to 7
- conv1_w: bfloat16 [9, 256], replicated, may hold values from -2 to 2
- conv1_b: float32 [256], replicated, may hold values from -4 to 4
- conv2_w: bfloat16 [9, 256, 256], replicated, may hold values from -0.125 to 0.125
- conv2_b: float32 [256], replicated, may hold values from -4 to 4
- proj_w: bfloat16 [4864, 256], replicated, may hold values from -0.078125 to 0.078125
- proj_b: float32 [256], replicated, may hold values from -4 to 4
Outputs:
- features: bfloat16 [1, 512, 256], P(None, ('meet', 'tm')), parts along dimension 1
The draws below stay inside these ranges and needn't reach their ends.
There are 2 independent parts, one for each index of `meet`. The reference program is written for one: setup_inputs(seed, part) draws one part's arguments, and reference() takes and returns one part's arrays. A program takes and returns all parts, laid end to end along the dimension named above; an argument that names none is the same for every part. Nothing has to cross between parts.
Inputs may be any that keep to these rules, and one draw needn't show every extreme that they name: `masks`: mask levels; level / 255 is the weight of a time-frequency cell for a speaker or, in the last row, for the noise. `valid`: frames of the meeting that hold speech data; all 1024 in some meetings.
All inputs are finite; a program needn't handle non-finite values.
Results may differ from the reference program's by a relative error of at most 0.003.
The reference program's roundings to bfloat16 on the way count: a program that leaves them out, or rounds other values in their place, can miss the bound.
Values may be sent and summed in bfloat16 or wider, within the bound.
A program may use at most 64 MiB of HBM per device.

```python
import math
import jax
import jax.numpy as jnp
from jax import lax

MICS = 8
NFFT = 512
HOP = 160
BINS = 257
MELS = 80
SPK = 1
CHANNELS = 256
D = 256
F_DEV = 64
FRAMES = 1024
Q2 = 19
OUTF = 256
N_TM = 16


block_frames = 16


echo_count = 3


def speaker_blocks(key):
    picker = jax.random.fold_in(key, 101)
    return jax.random.randint(picker, (FRAMES // block_frames,), 0, SPK + 1)


def draw_masks(key, part):
    owner = jnp.repeat(speaker_blocks(key), block_frames)
    high_key, low_key = jax.random.split(jax.random.fold_in(key, 102))
    strong = jax.random.randint(high_key, (SPK + 1, FRAMES, BINS), 128, 256)
    faint = jax.random.randint(low_key, (SPK + 1, FRAMES, BINS), 0, 96)
    chosen = jnp.arange(SPK + 1)[:, None, None] == owner[None, :, None]
    return jnp.where(chosen, strong, faint).astype(jnp.int32)


def draw_valid(key, part):
    cutoff = jax.random.randint(jax.random.fold_in(key, 104), (1,), 0, FRAMES // 2 + 1)
    return (FRAMES - cutoff * (1 - part % 2)).astype(jnp.int32)


def delayed_copy(signal, delays):
    length = signal.shape[0]
    positions = jnp.arange(length, dtype=jnp.int32)[None, :] - delays[:, None]
    picked = jnp.take(signal, jnp.clip(positions, 0, length - 1), axis=0)
    return jnp.where(positions >= 0, picked, 0.0)


def draw_waveform(key, part):
    length = FRAMES * HOP
    reach = NFFT // 4
    owner = jnp.repeat(speaker_blocks(key), block_frames * HOP)
    subkeys = jax.random.split(jax.random.fold_in(key, 103), 11)
    source = jax.random.normal(subkeys[0], (length,), jnp.float32)
    sensor = jax.random.normal(subkeys[1], (MICS, length), jnp.float32)
    shared = jax.random.normal(subkeys[2], (length,), jnp.float32)
    direct_delay = jax.random.randint(subkeys[3], (SPK, MICS), 0, reach + 1).astype(jnp.int32)
    echo_delay = jax.random.randint(subkeys[7], (SPK, echo_count, MICS), 0, reach + 1).astype(jnp.int32)
    noise_delay = jax.random.randint(subkeys[8], (MICS,), 0, reach + 1).astype(jnp.int32)
    direct_gain = jax.random.uniform(subkeys[9], (SPK, MICS), jnp.float32, 0.6, 1.2)
    echo_gain = jax.random.normal(subkeys[10], (SPK, echo_count, MICS), jnp.float32) * 0.35
    block_gain = jnp.exp(jax.random.uniform(subkeys[4], (FRAMES // block_frames,), jnp.float32, -0.7, 0.7))
    ramp = 1.0 + 2.0 * jnp.arange(length, dtype=jnp.float32) / length
    loudness = ramp * jnp.repeat(block_gain, block_frames * HOP) * 0.6
    speech = jnp.zeros((MICS, length), jnp.float32)
    for talker in range(SPK):
        imaged = direct_gain[talker][:, None] * delayed_copy(source, direct_delay[talker])
        for echo in range(echo_count):
            imaged = imaged + echo_gain[talker, echo][:, None] * delayed_copy(source, echo_delay[talker, echo])
        speech = jnp.where(owner[None, :] == talker, imaged, 0.0)
    sensor_gain = jnp.exp(jax.random.uniform(subkeys[5], (MICS,), jnp.float32, -1.6, -0.5))
    mixing = jax.random.normal(subkeys[6], (MICS,), jnp.float32) * 0.5
    noises = sensor_gain[:, None] * sensor + mixing[:, None] * delayed_copy(shared, noise_delay)
    combined = speech * loudness[None, :] + noises
    return jnp.clip(combined, -16.0, 16.0).astype(jnp.bfloat16)


def centred(own_key, dims, deviation, most, held_as=jnp.bfloat16):
    array = jax.random.normal(own_key, dims, jnp.float32) * deviation
    return jnp.minimum(jnp.maximum(array, -most), most).astype(held_as)


def setup_inputs(seed: int = 0, part: int = 0) -> dict:
    splits = jax.random.split(jax.random.key(seed), 11)
    own_keys = jax.random.split(jax.random.fold_in(splits[10], part), 11)
    waveform = draw_waveform(jax.random.fold_in(jax.random.fold_in(splits[10], part), 71), part)
    masks = draw_masks(jax.random.fold_in(jax.random.fold_in(splits[10], part), 71), part)
    valid = draw_valid(jax.random.fold_in(jax.random.fold_in(splits[10], part), 71), part)
    ref_mic = jax.random.randint(own_keys[3], (1,), 0, MICS).astype(jnp.int32)
    conv1_w = centred(splits[4], (9, CHANNELS), 9 ** -0.5, 2.0)
    conv1_b = centred(splits[5], (CHANNELS,), 1.0, 4.0, jnp.float32)
    conv2_w = centred(splits[6], (9, CHANNELS, CHANNELS), (9 * CHANNELS) ** -0.5, 0.125)
    conv2_b = centred(splits[7], (CHANNELS,), 1.0, 4.0, jnp.float32)
    proj_w = centred(splits[8], (Q2 * CHANNELS, D), (Q2 * CHANNELS) ** -0.5, 0.078125)
    proj_b = centred(splits[9], (D,), 1.0, 4.0, jnp.float32)
    return {"waveform": waveform, "masks": masks, "valid": valid, "ref_mic": ref_mic, "conv1_w": conv1_w, "conv1_b": conv1_b, "conv2_w": conv2_w, "conv2_b": conv2_b, "proj_w": proj_w, "proj_b": proj_b}


loading = 0.03
epsilon = 1e-6
sample_rate = 16000.0


def dft_tables(fft_len, bin_count):
    sample_pos = jnp.arange(fft_len, dtype=jnp.int32)
    bin_pos = jnp.arange(bin_count, dtype=jnp.int32)
    product = (sample_pos[:, None] * bin_pos[None, :]) % fft_len
    phase = product.astype(jnp.float32) * (2.0 * math.pi / fft_len)
    window = 0.5 - 0.5 * jnp.cos(sample_pos.astype(jnp.float32) * (2.0 * math.pi / fft_len))
    cosine_table = (window[:, None] * jnp.cos(phase)).astype(jnp.bfloat16)
    sine_table = (-window[:, None] * jnp.sin(phase)).astype(jnp.bfloat16)
    return cosine_table, sine_table


def mel_bank(bin_count, mel_count):
    mel_top = 2595.0 * math.log10(1.0 + sample_rate / 2.0 / 700.0)
    points = jnp.arange(mel_count + 2, dtype=jnp.float32) * (mel_top / (mel_count + 1))
    edges_hz = 700.0 * (jnp.power(10.0, points / 2595.0) - 1.0)
    freq_hz = jnp.arange(bin_count, dtype=jnp.float32) * (sample_rate / 2.0 / (bin_count - 1))
    lower_hz = edges_hz[:-2]
    centre_hz = edges_hz[1:-1]
    upper_hz = edges_hz[2:]
    rising = (freq_hz[:, None] - lower_hz[None, :]) / (centre_hz - lower_hz)[None, :]
    falling = (upper_hz[None, :] - freq_hz[:, None]) / (upper_hz - centre_hz)[None, :]
    return jnp.maximum(jnp.minimum(rising, falling), 0.0)


def spectra(extended, frames, hop_len, cosine_table, sine_table):
    mic_count = extended.shape[0]
    fft_len = cosine_table.shape[0]
    block_count = -(-fft_len // hop_len)
    pieces = extended.reshape(mic_count, frames + block_count - 1, hop_len)
    framed = jnp.concatenate([pieces[:, offset:offset + frames] for offset in range(block_count)], axis=2)
    framed = framed[:, :, :fft_len].reshape(mic_count * frames, fft_len)
    spec_re = jnp.dot(framed, cosine_table, preferred_element_type=jnp.float32)
    spec_im = jnp.dot(framed, sine_table, preferred_element_type=jnp.float32)
    return spec_re.reshape(mic_count, frames, -1), spec_im.reshape(mic_count, frames, -1)


def cov_partial(spec_re, spec_im, weight):
    highest = lax.Precision.HIGHEST
    scaled_re = weight[:, None] * spec_re[None]
    scaled_im = weight[:, None] * spec_im[None]

    def paired(left_part, right_part):
        return jnp.einsum('kmtf,ntf->kmnf', left_part, right_part, precision=highest)

    stats_re = paired(scaled_re, spec_re) + paired(scaled_im, spec_im)
    stats_im = paired(scaled_im, spec_re) - paired(scaled_re, spec_im)
    return stats_re, stats_im


def solve_beams(stats_re, stats_im, ref_mic):
    mic_count = stats_re.shape[1]
    identity = jnp.eye(mic_count, dtype=jnp.float32)[None, :, :, None]
    target_re = stats_re[:-1]
    target_im = stats_im[:-1]
    other_re = jnp.sum(stats_re, axis=0)[None] - target_re
    other_im = jnp.sum(stats_im, axis=0)[None] - target_im
    spread = jnp.sum(other_re * identity, axis=(1, 2))
    ridge = loading * spread / mic_count + epsilon
    matrix_re = other_re + ridge[:, None, None, :] * identity
    matrix_im = other_im
    answer_re = target_re
    answer_im = target_im
    row_index = jnp.arange(mic_count, dtype=jnp.int32)
    for pivot in range(mic_count):
        pivot_re = matrix_re[:, pivot, pivot]
        pivot_im = matrix_im[:, pivot, pivot]
        modulus = pivot_re * pivot_re + pivot_im * pivot_im
        inverse_re = (pivot_re / modulus)[:, None]
        inverse_im = (-pivot_im / modulus)[:, None]
        lead_re = matrix_re[:, pivot] * inverse_re - matrix_im[:, pivot] * inverse_im
        lead_im = matrix_re[:, pivot] * inverse_im + matrix_im[:, pivot] * inverse_re
        head_re = answer_re[:, pivot] * inverse_re - answer_im[:, pivot] * inverse_im
        head_im = answer_re[:, pivot] * inverse_im + answer_im[:, pivot] * inverse_re
        column_re = matrix_re[:, :, pivot][:, :, None]
        column_im = matrix_im[:, :, pivot][:, :, None]
        on_pivot = (row_index == pivot)[None, :, None, None]
        matrix_re, matrix_im = (
            jnp.where(on_pivot, lead_re[:, None], matrix_re - (column_re * lead_re[:, None] - column_im * lead_im[:, None])),
            jnp.where(on_pivot, lead_im[:, None], matrix_im - (column_re * lead_im[:, None] + column_im * lead_re[:, None])))
        answer_re, answer_im = (
            jnp.where(on_pivot, head_re[:, None], answer_re - (column_re * head_re[:, None] - column_im * head_im[:, None])),
            jnp.where(on_pivot, head_im[:, None], answer_im - (column_re * head_im[:, None] + column_im * head_re[:, None])))
    trace_ratio = jnp.sum(answer_re * identity, axis=(1, 2))
    chosen = (row_index == ref_mic[0]).astype(jnp.float32)[None, None, :, None]
    scale_by = 1.0 / (trace_ratio + epsilon)
    beam_re = jnp.sum(answer_re * chosen, axis=2) * scale_by[:, None, :]
    beam_im = jnp.sum(answer_im * chosen, axis=2) * scale_by[:, None, :]
    return beam_re, beam_im


def beam_logmel(spec_re, spec_im, beam_re, beam_im, melbank, live_rows):
    highest = lax.Precision.HIGHEST

    def mixed(beam_part, spec_part):
        return jnp.einsum('kmf,mtf->ktf', beam_part, spec_part, precision=highest)

    beamed_re = mixed(beam_re, spec_re) + mixed(beam_im, spec_im)
    beamed_im = mixed(beam_re, spec_im) - mixed(beam_im, spec_re)
    power_sum = beamed_re * beamed_re + beamed_im * beamed_im
    melspec = jnp.einsum('ktf,fj->ktj', power_sum, melbank, precision=highest)
    return (jnp.log(melspec + epsilon) * live_rows[None, :, None]).astype(jnp.bfloat16)


def stem(extended, row_live, out_live, conv1_w, conv1_b, conv2_w, conv2_b, proj_w, proj_b):
    streams, span, mel_count = extended.shape
    frames = span - 3
    halves = frames // 2 + 1
    quarter = frames // 4
    q_first = (mel_count - 3) // 2 + 1
    q_second = (q_first - 3) // 2 + 1
    channels = conv1_w.shape[1]
    kernel_one = conv1_w.astype(jnp.float32)
    layer_one = jnp.zeros((streams, halves, q_first, channels), jnp.float32)
    for shift_t in range(3):
        for shift_f in range(3):
            tap = extended[:, shift_t:shift_t + 2 * halves - 1:2, shift_f:shift_f + 2 * q_first - 1:2]
            layer_one = layer_one + tap.astype(jnp.float32)[..., None] * kernel_one[3 * shift_t + shift_f]
    layer_one = (jax.nn.relu(layer_one + conv1_b) * row_live[None, :, None, None]).astype(jnp.bfloat16)
    summed = jnp.zeros((streams * quarter * q_second, channels), jnp.float32)
    for shift_t in range(3):
        for shift_f in range(3):
            window = layer_one[:, shift_t:shift_t + 2 * quarter - 1:2, shift_f:shift_f + 2 * q_second - 1:2]
            summed = summed + jnp.dot(window.reshape(-1, channels), conv2_w[3 * shift_t + shift_f],
                                      preferred_element_type=jnp.float32)
    layer_two = jax.nn.relu(summed + conv2_b).astype(jnp.bfloat16).reshape(streams * quarter, q_second * channels)
    projected = jnp.dot(layer_two, proj_w, preferred_element_type=jnp.float32) + proj_b
    projected = projected.reshape(streams, quarter, -1) * out_live[None, :, None]
    return projected.astype(jnp.bfloat16)


def reference(waveform, masks, valid, ref_mic, conv1_w, conv1_b, conv2_w, conv2_b, proj_w, proj_b):
    mic_count = waveform.shape[0]
    block_count = -(-NFFT // HOP)
    cosine_table, sine_table = dft_tables(NFFT, BINS)
    melbank = mel_bank(BINS, MELS)
    padded = jnp.concatenate([waveform, jnp.zeros((mic_count, (block_count - 1) * HOP), waveform.dtype)], axis=1)
    shard_ids = jnp.arange(N_TM, dtype=jnp.int32)

    def shard_spectra(shard):
        extended = lax.dynamic_slice_in_dim(padded, (shard * (F_DEV * HOP)).astype(jnp.int32),
                                            (F_DEV + block_count - 1) * HOP, 1)
        return spectra(extended, F_DEV, HOP, cosine_table, sine_table)

    def shard_live(shard):
        return (shard * F_DEV + jnp.arange(F_DEV, dtype=jnp.int32) < valid[0]).astype(jnp.float32)

    def add_shard(carry, shard):
        spec_re, spec_im = shard_spectra(shard)
        shard_mask = lax.dynamic_slice_in_dim(masks, (shard * F_DEV).astype(jnp.int32), F_DEV, 1)
        weight = shard_mask.astype(jnp.float32) * shard_live(shard)[None, :, None] / 255.0
        part_re, part_im = cov_partial(spec_re, spec_im, weight)
        return (carry[0] + part_re, carry[1] + part_im), None

    zeros_cov = jnp.zeros((SPK + 1, mic_count, mic_count, BINS), jnp.float32)
    (stats_re, stats_im), _ = lax.scan(add_shard, (zeros_cov, zeros_cov), shard_ids)
    beam_re, beam_im = solve_beams(stats_re, stats_im, ref_mic)

    def shard_logmel(shard):
        spec_re, spec_im = shard_spectra(shard)
        return beam_logmel(spec_re, spec_im, beam_re, beam_im, melbank, shard_live(shard))

    logmel = lax.map(shard_logmel, shard_ids)
    logmel = jnp.transpose(logmel, (1, 0, 2, 3)).reshape(SPK, FRAMES, MELS)
    ext_all = jnp.concatenate([jnp.zeros((SPK, 3, MELS), logmel.dtype), logmel], axis=1)

    def shard_stem(shard):
        extended = lax.dynamic_slice_in_dim(ext_all, (shard * F_DEV).astype(jnp.int32), F_DEV + 3, 1)
        row_live = (shard * (F_DEV // 2) + jnp.arange(F_DEV // 2 + 1, dtype=jnp.int32) >= 1).astype(jnp.float32)
        quarter = F_DEV // 4
        out_live = (4 * (shard * quarter + jnp.arange(quarter, dtype=jnp.int32)) < valid[0]).astype(jnp.float32)
        return stem(extended, row_live, out_live, conv1_w, conv1_b, conv2_w, conv2_b, proj_w, proj_b)

    features = lax.map(shard_stem, shard_ids)
    return jnp.transpose(features, (1, 0, 2, 3)).reshape(SPK, OUTF, -1)
```

```python
import functools
import math

import jax
import jax.numpy as jnp
import numpy as np
from jax import lax
from jax.experimental import pallas as pl
from jax.experimental.pallas import tpu as pltpu
from jax.sharding import PartitionSpec as P

NFFT = 512
HOP = 160
MELS = 80
BINS = NFFT // 2 + 1
LANES = 128
MAIN = BINS - 1
PADDED = MAIN + LANES
SPECTRUM = 2 * MAIN + LANES
GROUP = 4
SPAN = GROUP * HOP
WINDOW = 1024

loading = 0.03
epsilon = 1e-06
sample_rate = 16000.0


def dft_table():
    sample_pos = np.arange(NFFT)
    phase = (sample_pos[:, None] * np.arange(BINS)[None, :] % NFFT).astype(np.float32)
    phase = phase * np.float32(2.0 * math.pi / NFFT)
    ramp = sample_pos.astype(np.float32) * np.float32(2.0 * math.pi / NFFT)
    window = np.float32(0.5) - np.float32(0.5) * np.cos(ramp)
    cosines = window[:, None] * np.cos(phase)
    sines = -window[:, None] * np.sin(phase)
    table = np.zeros((NFFT, SPECTRUM), np.float32)
    table[:, :MAIN] = cosines[:, :MAIN]
    table[:, MAIN : 2 * MAIN] = sines[:, :MAIN]
    table[:, 2 * MAIN :] = cosines[:, MAIN:]
    return table.astype(jnp.bfloat16)


def mel_bank():
    mel_top = 2595.0 * math.log10(1.0 + sample_rate / 2.0 / 700.0)
    points = np.arange(MELS + 2) * (mel_top / (MELS + 1))
    edges_hz = 700.0 * (np.power(10.0, points / 2595.0) - 1.0)
    freq_hz = np.arange(BINS) * (sample_rate / 2.0 / (BINS - 1))
    lower, centre, upper = edges_hz[:-2], edges_hz[1:-1], edges_hz[2:]
    rising = (freq_hz[:, None] - lower[None, :]) / (centre - lower)[None, :]
    falling = (upper[None, :] - freq_hz[:, None]) / (upper - centre)[None, :]
    bank = np.zeros((PADDED, LANES), np.float32)
    bank[:BINS, :MELS] = np.maximum(np.minimum(rising, falling), 0.0)
    return bank


def repeat_table():
    table = np.zeros((LANES, MELS * 8), np.float32)
    for mel in range(MELS):
        table[mel, mel * 8 : mel * 8 + 8] = 1.0
    return table.astype(jnp.bfloat16)


def kernel(
    n,
    valid_ref,
    mic_ref,
    wave_hbm,
    masks_hbm,
    table_hbm,
    bank_hbm,
    repeat_hbm,
    conv1_w_hbm,
    conv1_b_hbm,
    conv2_hbm,
    conv2_b_hbm,
    proj_hbm,
    proj_b_hbm,
    out_ref,
    conv1_w,
    conv1_b,
    conv2_b,
    proj_b,
    wave,
    masks,
    table,
    ext,
    weight,
    spec,
    left,
    right,
    cov,
    part,
    landed,
    packed,
    gathered,
    full,
    bank,
    repeat,
    conv2_w,
    proj_w,
    beam,
    power,
    spread,
    lined,
    kernel_one,
    patches,
    first,
    nearby_send,
    nearby_recv,
    send_one,
    recv_one,
    send_two,
    recv_two,
    loads,
):
    rows, frames = masks.shape[0], masks.shape[1]
    mics, own = wave.shape
    groups = frames // GROUP + 1
    reach = right.shape[1]
    me = lax.axis_index("tm")
    load_wave = pltpu.make_async_copy(wave_hbm, wave, loads.at[0])
    load_table = pltpu.make_async_copy(table_hbm, table, loads.at[1])
    load_masks = pltpu.make_async_copy(masks_hbm, masks, loads.at[2])
    load_wave.start()
    load_table.start()
    load_masks.start()
    load_conv2 = pltpu.make_async_copy(conv2_hbm, conv2_w, loads.at[3])
    load_proj = pltpu.make_async_copy(proj_hbm, proj_w, loads.at[4])
    load_bank = pltpu.make_async_copy(bank_hbm, bank, loads.at[5])
    load_repeat = pltpu.make_async_copy(repeat_hbm, repeat, loads.at[6])
    barrier = pltpu.get_barrier_semaphore()
    for j in range(1, n):
        pl.semaphore_signal(
            barrier,
            inc=1,
            device_id={"tm": lax.rem(me + j, n)},
            device_id_type=pl.DeviceIdType.MESH,
        )

    def transform(chosen):
        spans = jnp.concatenate(
            [ext[:, g * SPAN : g * SPAN + WINDOW] for g in chosen], axis=0
        )
        framed = jnp.concatenate(
            [
                (spans if r == 0 else pltpu.roll(spans, WINDOW - r * HOP, axis=1))[:, :NFFT]
                for r in range(GROUP)
            ],
            axis=0,
        ).astype(jnp.bfloat16)
        return jnp.dot(framed, table[...], preferred_element_type=jnp.float32)

    load_wave.wait()
    ext[:, SPAN : SPAN + own] = wave[...].astype(jnp.float32)
    load_table.wait()
    inner = list(range(1, groups - 1))
    found = transform(inner)
    width = len(inner) * mics
    for r in range(GROUP):
        spec[(r * groups + 1) * mics : (r * groups + 1) * mics + width, :] = found[
            r * width : (r + 1) * width
        ]

    pl.semaphore_wait(barrier, n - 1)
    to_right = pltpu.make_async_remote_copy(
        src_ref=wave_hbm.at[:, own - SPAN :],
        dst_ref=left,
        send_sem=nearby_send.at[0],
        recv_sem=nearby_recv.at[0],
        device_id={"tm": lax.rem(me + 1, n)},
        device_id_type=pl.DeviceIdType.MESH,
    )
    to_left = pltpu.make_async_remote_copy(
        src_ref=wave_hbm.at[:, :reach],
        dst_ref=right,
        send_sem=nearby_send.at[1],
        recv_sem=nearby_recv.at[1],
        device_id={"tm": lax.rem(me + n - 1, n)},
        device_id_type=pl.DeviceIdType.MESH,
    )
    to_right.start()
    to_left.start()
    small = [
        pltpu.make_async_copy(source, held, loads.at[7 + i])
        for i, (source, held) in enumerate(
            (
                (conv1_w_hbm, conv1_w),
                (conv1_b_hbm, conv1_b),
                (conv2_b_hbm, conv2_b),
                (proj_b_hbm, proj_b),
            )
        )
    ]
    for load in small:
        load.start()
    load_bank.start()
    load_repeat.start()
    load_conv2.start()
    load_proj.start()

    load_masks.wait()
    limit = valid_ref[0] - me * frames
    alive = lax.broadcasted_iota(jnp.int32, (frames, MAIN), 0) < limit
    for k in range(rows):
        level = masks[k].astype(jnp.float32) * (1.0 / 255.0)
        weight[k, :, :MAIN] = jnp.where(alive, level[:, :MAIN], 0.0)
        weight[k, :, MAIN:] = jnp.where(
            alive[:, :LANES], jnp.broadcast_to(level[:, MAIN:], (frames, LANES)), 0.0
        )

    half = mics // 2
    low = lax.broadcasted_iota(jnp.int32, (mics, LANES), 0) < half

    def frames_of(h):
        first_row = h * 2 * GROUP
        if not isinstance(h, int):
            first_row = pl.multiple_of(first_row, 2 * GROUP)
        places = []
        for i in range(2 * GROUP):
            at = ((i % GROUP) * groups + 1 + 2 * h + i // GROUP) * mics
            if not isinstance(h, int):
                at = pl.multiple_of(at, mics)
            places.append(pl.ds(at, mics))
        return pl.ds(first_row, 2 * GROUP), places

    def add_block(h, totals, block):
        totals = list(totals)
        lanes = pl.ds(block * LANES, LANES)
        lanes_im = pl.ds(MAIN + block * LANES, LANES)
        span, places = frames_of(h)
        held = [weight[k, span, lanes] for k in range(rows)]
        for i, at in enumerate(places):
            re = spec[at, lanes]
            im = spec[at, lanes_im]
            w = [held[k][i : i + 1] for k in range(rows)]
            place = 0
            for d in range(half + 1):
                if d == 0:
                    products = [re * re + im * im]
                else:
                    re_n = pltpu.roll(re, mics - d, axis=0)
                    im_n = pltpu.roll(im, mics - d, axis=0)
                    real = re * re_n + im * im_n
                    imag = im * re_n - re * im_n
                    products = [real, imag] if d < half else [jnp.where(low, real, imag)]
                for product in products:
                    for k in range(rows):
                        slot = k * mics + place
                        totals[slot] = totals[slot] + w[k] * product
                    place += 1
        return tuple(totals)

    def add_last_bin(h, totals):
        totals = list(totals)
        span, places = frames_of(h)
        held = [weight[k, span, pl.ds(MAIN, LANES)] for k in range(rows)]
        for i, at in enumerate(places):
            re = spec[at, pl.ds(2 * MAIN, LANES)]
            for d in range(half + 1):
                product = re * (re if d == 0 else pltpu.roll(re, mics - d, axis=0))
                for k in range(rows):
                    slot = k * (half + 1) + d
                    totals[slot] = totals[slot] + held[k][i : i + 1] * product
        return tuple(totals)

    blocks = frames // (2 * GROUP)
    tiles = MAIN // LANES
    planes = rows * mics
    extra = rows * (half + 1)
    adders = [functools.partial(add_block, block=block) for block in range(tiles)]
    adders.append(add_last_bin)
    counts = [planes] * tiles + [extra]
    for block in range(tiles + 1):
        zeros = tuple(jnp.zeros((mics, LANES), jnp.float32) for _ in range(counts[block]))
        totals = lax.fori_loop(0, blocks - 1, adders[block], zeros)
        for slot in range(counts[block]):
            cov[block, slot] = totals[slot]

    to_right.wait_recv()
    to_left.wait_recv()
    ext[:, :SPAN] = jnp.where(me > 0, left[...].astype(jnp.float32), 0.0)
    ext[:, SPAN + own :] = jnp.where(me < n - 1, right[...].astype(jnp.float32), 0.0)
    found = transform([0, groups - 1])
    for r in range(GROUP):
        for i, g in enumerate((0, groups - 1)):
            at = (r * 2 + i) * mics
            spec[(r * groups + g) * mics : (r * groups + g + 1) * mics, :] = found[at : at + mics]

    lane = lax.broadcasted_iota(jnp.int32, (mics, LANES), 1)
    sub = lax.broadcasted_iota(jnp.int32, (mics, LANES), 0)
    width = MAIN // n
    per_tile = LANES // width
    deep = -(-planes // per_tile)

    def turned(value, amount):
        amount = amount % LANES
        return pltpu.roll(value, amount, axis=1) if amount else value

    totals = add_last_bin(blocks - 1, tuple(cov[tiles, slot] for slot in range(extra)))
    line = jnp.zeros((mics, LANES), jnp.float32)
    for slot in range(extra):
        line = jnp.where(lane == mics * slot + sub, totals[slot], line)
    line = jnp.sum(line, axis=0, keepdims=True)
    for to in range(n):
        part[to, deep * mics : deep * mics + 1, :] = line
    for block in range(tiles):
        totals = adders[block](blocks - 1, tuple(cov[block, slot] for slot in range(planes)))
        for slot in range(planes):
            cov[block, slot] = totals[slot]
        for to in range(block * per_tile, (block + 1) * per_tile):
            for tile in range(deep):
                packing = jnp.zeros((mics, LANES), jnp.float32)
                for i in range(min(per_tile, planes - tile * per_tile)):
                    moved = turned(cov[block, tile * per_tile + i], (i - to % per_tile) * width)
                    packing = moved if i == 0 else jnp.where(lane // width == i, moved, packing)
                part[to, tile * mics : (tile + 1) * mics, :] = packing

    sent_one = []
    for j in range(1, n):
        to = lax.rem(me + j, n)
        copy = pltpu.make_async_remote_copy(
            src_ref=part.at[to],
            dst_ref=landed.at[j],
            send_sem=send_one.at[j],
            recv_sem=recv_one.at[j],
            device_id={"tm": to},
            device_id_type=pl.DeviceIdType.MESH,
        )
        copy.start()
        sent_one.append(copy)

    for load in small:
        load.wait()
    channels = conv1_w.shape[1]
    kernel_one[...] = jnp.zeros_like(kernel_one)
    for a in range(3):
        for b in range(3):
            tap = conv1_w[3 * a + b : 3 * a + b + 1, :].astype(jnp.float32)
            for late in range(3):
                at = b * 8 + 2 * late + a
                kernel_one[at : at + 1, late * channels : (late + 1) * channels] = tap
    power[...] = jnp.zeros_like(power)
    lined[...] = jnp.zeros_like(lined)

    total = part[me]
    for j in range(1, n):
        sent_one[j - 1].wait_recv()
        total = total + landed[j]
    line = total[deep * mics : deep * mics + 1]
    lasts = [
        jnp.sum(jnp.where(lane == mics * slot + sub, line, 0.0), axis=1, keepdims=True)
        for slot in range(extra)
    ]
    whole = []
    for slot in range(planes):
        tile = slot // per_tile
        plane = turned(total[tile * mics : (tile + 1) * mics], -(slot % per_tile) * width)
        k, place = slot // mics, slot % mics
        d = (place + 1) // 2
        if place == 0 or (place % 2 == 1 and d < half):
            at_last = lasts[k * (half + 1) + d]
        elif d == half:
            at_last = jnp.where(low, lasts[k * (half + 1) + d], 0.0)
        else:
            at_last = jnp.zeros((mics, LANES), jnp.float32)
        whole.append(jnp.where(lane == width, at_last, plane))
    solved = solve(whole, mics, full, mic_ref[0])
    for i in range(2):
        value = jnp.where(lane < width, solved[i], 0.0)
        for step in (1, 2, 4):
            value = value + turned(value, step * width)
        value = jnp.where(lane // width == sub, value, 0.0)
        packed[i : i + 1, :] = jnp.sum(value, axis=0, keepdims=True)
    sent_two = []
    for j in range(1, n):
        copy = pltpu.make_async_remote_copy(
            src_ref=packed,
            dst_ref=gathered.at[me],
            send_sem=send_two.at[j],
            recv_sem=recv_two.at[j],
            device_id={"tm": lax.rem(me + j, n)},
            device_id_type=pl.DeviceIdType.MESH,
        )
        copy.start()
        sent_two.append(copy)
    gathered[me] = packed[...]
    for i in range(2):
        at_last = jnp.sum(jnp.where(lane == width, solved[i], 0.0), axis=1, keepdims=True)
        beam[i, :, MAIN:] = jnp.broadcast_to(at_last, (mics, LANES))
    to_right.wait_send()
    to_left.wait_send()
    for j in range(1, n):
        sent_two[j - 1].wait_recv()
    for i in range(2):
        for block in range(tiles):
            joined = jnp.zeros((mics, LANES), jnp.float32)
            for t in range(per_tile):
                row = gathered[block * per_tile + t, i : i + 1, :]
                value = jnp.where(lane // width == sub, row, 0.0)
                for step in (1, 2, 4):
                    value = value + turned(value, step * width)
                if mics * width < LANES:
                    value = turned(value, (t - mics + 1) * width)
                joined = jnp.where(lane // width == t, value, joined)
            beam[i, :, block * LANES : (block + 1) * LANES] = joined

    load_bank.wait()
    load_repeat.wait()
    stem(
        valid_ref[0],
        spec,
        bank,
        repeat,
        conv1_b,
        load_conv2,
        conv2_w,
        conv2_b,
        load_proj,
        proj_w,
        proj_b,
        out_ref,
        beam,
        power,
        spread,
        lined,
        kernel_one,
        patches,
        first,
    )
    for j in range(1, n):
        sent_one[j - 1].wait_send()
        sent_two[j - 1].wait_send()


def solve(planes, mics, full, ref):
    half = mics // 2
    for k in range(2):
        for m in range(mics):
            for d in range(half + 1):
                n = (m + d) % mics
                if d == half and m >= half:
                    continue

                def row(plane, at):
                    return planes[k * mics + plane][at : at + 1]

                if d == 0:
                    full[2 * k, m, m : m + 1, :] = row(0, m)
                    full[2 * k + 1, m, m : m + 1, :] = jnp.zeros((1, LANES), jnp.float32)
                    continue
                if d < half:
                    real, imag = row(2 * d - 1, m), row(2 * d, m)
                else:
                    real, imag = row(2 * d - 1, m), -row(2 * d - 1, m + half)
                full[2 * k, m, n : n + 1, :] = real
                full[2 * k + 1, m, n : n + 1, :] = imag
                full[2 * k, n, m : m + 1, :] = real
                full[2 * k + 1, n, m : m + 1, :] = -imag
    answer_re = [full[0, m] for m in range(mics)]
    answer_im = [full[1, m] for m in range(mics)]
    matrix_re = [full[2, m] for m in range(mics)]
    matrix_im = [full[3, m] for m in range(mics)]
    index = lax.broadcasted_iota(jnp.int32, (mics, LANES), 0)
    spread = matrix_re[0][0:1]
    for m in range(1, mics):
        spread = spread + matrix_re[m][m : m + 1]
    ridge = loading * spread / mics + epsilon
    matrix_re = [
        jnp.where(index == m, matrix_re[m] + ridge, matrix_re[m]) for m in range(mics)
    ]
    for p in range(mics):
        pivot_re, pivot_im = matrix_re[p][p : p + 1], matrix_im[p][p : p + 1]
        scale = 1.0 / (pivot_re * pivot_re + pivot_im * pivot_im)
        inverse_re, inverse_im = pivot_re * scale, -pivot_im * scale
        lead_re = matrix_re[p] * inverse_re - matrix_im[p] * inverse_im
        lead_im = matrix_re[p] * inverse_im + matrix_im[p] * inverse_re
        head_re = answer_re[p] * inverse_re - answer_im[p] * inverse_im
        head_im = answer_re[p] * inverse_im + answer_im[p] * inverse_re
        for m in range(mics):
            if m == p:
                continue
            column_re, column_im = matrix_re[m][p : p + 1], matrix_im[m][p : p + 1]
            matrix_re[m] = matrix_re[m] - (column_re * lead_re - column_im * lead_im)
            matrix_im[m] = matrix_im[m] - (column_re * lead_im + column_im * lead_re)
            answer_re[m] = answer_re[m] - (column_re * head_re - column_im * head_im)
            answer_im[m] = answer_im[m] - (column_re * head_im + column_im * head_re)
        matrix_re[p], matrix_im[p] = lead_re, lead_im
        answer_re[p], answer_im[p] = head_re, head_im
    trace = answer_re[0][0:1]
    for m in range(1, mics):
        trace = trace + answer_re[m][m : m + 1]
    scale = 1.0 / (trace + epsilon)
    picked = index == ref
    beam_re = jnp.zeros((mics, LANES), jnp.float32)
    beam_im = jnp.zeros((mics, LANES), jnp.float32)
    for m in range(mics):
        real = jnp.sum(jnp.where(picked, answer_re[m], 0.0), axis=0, keepdims=True)
        imag = jnp.sum(jnp.where(picked, answer_im[m], 0.0), axis=0, keepdims=True)
        beam_re = jnp.where(index == m, real * scale, beam_re)
        beam_im = jnp.where(index == m, imag * scale, beam_im)
    return beam_re, beam_im


def row_sums(values):
    count = len(values)
    sub = lax.broadcasted_iota(jnp.int32, values[0].shape, 0)
    step = count // 2
    while step:
        upper = sub // step % 2 == 1
        values = [
            jnp.where(
                upper,
                values[i + step] + pltpu.roll(values[i + step], step, axis=0),
                values[i] + pltpu.roll(values[i], count - step, axis=0),
            )
            for i in range(step)
        ]
        step //= 2
    return values[0]


def stem(
    valid,
    spec,
    bank,
    repeat,
    conv1_b,
    load_conv2,
    conv2_w,
    conv2_b,
    load_proj,
    proj_w,
    proj_b,
    out_ref,
    beam,
    power,
    spread,
    lined,
    kernel_one,
    patches,
    first,
):
    mics = beam.shape[1]
    quarter = out_ref.shape[0]
    groups = quarter + 1
    frames = quarter * GROUP
    stride = power.shape[0] // GROUP
    channels = conv2_w.shape[1]
    q_first = (MELS - 3) // 2 + 1
    q_second = (q_first - 3) // 2 + 1
    position = lax.axis_index("tm")
    for block in range(PADDED // LANES):
        lanes = pl.ds(block * LANES, LANES)
        beam_re = beam[0, :, lanes]
        beam_im = beam[1, :, lanes]

        def products(r, g):
            at = slice((r * groups + g) * mics, (r * groups + g + 1) * mics)
            if block < MAIN // LANES:
                re = spec[at, lanes]
                im = spec[at, pl.ds(MAIN + block * LANES, LANES)]
                return beam_re * re + beam_im * im, beam_re * im - beam_im * re
            re = spec[at, pl.ds(2 * MAIN, LANES)]
            return beam_re * re, -beam_im * re

        for r in range(GROUP):
            for g in range(0, groups - mics + 1, mics):
                pairs = [products(r, g + i) for i in range(mics)]
                real = row_sums([pair[0] for pair in pairs])
                imag = row_sums([pair[1] for pair in pairs])
                at = r * stride + g
                power[at : at + mics, lanes] = real * real + imag * imag
            for g in range(groups - groups % mics, groups):
                real, imag = products(r, g)
                real = jnp.sum(real, axis=0, keepdims=True)
                imag = jnp.sum(imag, axis=0, keepdims=True)
                at = r * stride + g
                power[at : at + 1, lanes] = real * real + imag * imag

    melspec = (
        jnp.dot(
            power[:, :MAIN],
            bank[:MAIN, :],
            preferred_element_type=jnp.float32,
            precision=lax.Precision.HIGHEST,
        )
        + power[:, MAIN:] * bank[MAIN : MAIN + 1, :]
    )
    row = lax.broadcasted_iota(jnp.int32, melspec.shape, 0)
    frame = position * frames + (row % stride - 1) * GROUP + row // stride
    alive = (frame >= 0) & (frame < valid)
    logmel = jnp.where(alive, jnp.log(melspec + epsilon), 0.0).astype(jnp.bfloat16)
    spread[...] = jnp.dot(logmel, repeat[...], preferred_element_type=jnp.float32)
    width = spread.shape[1]
    phase = lax.broadcasted_iota(jnp.int32, (quarter, width), 1) % 8
    mixed = jnp.zeros((quarter, width), jnp.float32)
    for u in range(7):
        start = (u + 1) % GROUP * stride + (u + 1) // GROUP
        mixed = jnp.where(phase == u, spread[start : start + quarter, :], mixed)
    lined[:, :width] = mixed
    order = list(range(0, q_first, 2)) + list(range(1, q_first, 2))
    for place, q in enumerate(order):
        base = 16 * q // LANES * LANES
        shift = 16 * q - base
        two = lined[:, base : base + 2 * LANES]
        if shift:
            two = pltpu.roll(two, 2 * LANES - shift, axis=1)
        patches[place * quarter : (place + 1) * quarter, :] = two[:, :LANES].astype(jnp.bfloat16)

    kernel_bf = kernel_one[...].astype(jnp.bfloat16)
    for late in range(3):
        lanes = slice(late * channels, (late + 1) * channels)
        one = jnp.dot(patches[...], kernel_bf[:, lanes], preferred_element_type=jnp.float32)
        one = jnp.maximum(one + conv1_b[...], 0.0)
        if late == 0:
            step = lax.broadcasted_iota(jnp.int32, one.shape, 0) % quarter
            one = jnp.where((step == 0) & (position == 0), 0.0, one)
        first[:, lanes] = one.astype(jnp.bfloat16)

    load_conv2.wait()
    evens = (q_first + 1) // 2
    summed = jnp.zeros((q_second * quarter, channels), jnp.float32)
    for b in range(3):
        start = {0: 0, 1: evens, 2: 1}[b] * quarter
        for late in range(3):
            summed = summed + jnp.dot(
                first[start : start + q_second * quarter, late * channels : (late + 1) * channels],
                conv2_w[3 * late + b],
                preferred_element_type=jnp.float32,
            )
    second = jnp.maximum(summed + conv2_b[...], 0.0).astype(jnp.bfloat16)
    load_proj.wait()
    out = jnp.zeros((quarter, out_ref.shape[1]), jnp.float32)
    for r in range(q_second):
        out = out + jnp.dot(
            second[r * quarter : (r + 1) * quarter],
            proj_w[r * channels : (r + 1) * channels, :],
            preferred_element_type=jnp.float32,
        )
    out_row = lax.broadcasted_iota(jnp.int32, out.shape, 0) + position * quarter
    out = jnp.where(GROUP * out_row < valid, out + proj_b[...], 0.0)
    out_ref[...] = out


def per_device(
    n, waveform, masks, valid, ref_mic, conv1_w, conv1_b, conv2_w, conv2_b, proj_w, proj_b
):
    mics, own = waveform.shape
    rows, frames = masks.shape[0], masks.shape[1]
    groups = frames // GROUP + 1
    quarter = frames // GROUP
    channels = conv1_w.shape[1]
    model = proj_w.shape[1]
    reach = WINDOW - SPAN
    vmem = pl.BlockSpec(memory_space=pltpu.VMEM)
    smem = pl.BlockSpec(memory_space=pltpu.SMEM)
    anywhere = pl.BlockSpec(memory_space=pltpu.HBM)
    planes = rows * mics
    deep = -(-planes * (MAIN // n) // LANES)
    tall = deep * mics + 1
    stride = -(-groups // 8) * 8
    q_first = (MELS - 3) // 2 + 1
    q_count = q_first * quarter
    features = pl.pallas_call(
        functools.partial(kernel, n),
        out_shape=jax.ShapeDtypeStruct((quarter, model), jnp.float32),
        in_specs=[smem] * 2 + [anywhere] * 5 + [anywhere, anywhere, anywhere, anywhere, anywhere, anywhere],
        out_specs=vmem,
        scratch_shapes=[
            pltpu.VMEM(conv1_w.shape, conv1_w.dtype),
            pltpu.VMEM((1, channels), jnp.float32),
            pltpu.VMEM((1, channels), jnp.float32),
            pltpu.VMEM((1, model), jnp.float32),
            pltpu.VMEM(waveform.shape, waveform.dtype),
            pltpu.VMEM(masks.shape, masks.dtype),
            pltpu.VMEM((NFFT, SPECTRUM), jnp.bfloat16),
            pltpu.VMEM((mics, SPAN + own + reach), jnp.float32),
            pltpu.VMEM((rows, frames, PADDED), jnp.float32),
            pltpu.VMEM((GROUP * groups * mics, SPECTRUM), jnp.float32),
            pltpu.VMEM((mics, SPAN), waveform.dtype),
            pltpu.VMEM((mics, reach), waveform.dtype),
            pltpu.VMEM((PADDED // LANES, planes, mics, LANES), jnp.float32),
            pltpu.VMEM((n, tall, LANES), jnp.float32),
            pltpu.VMEM((n, tall, LANES), jnp.float32),
            pltpu.VMEM((2, LANES), jnp.float32),
            pltpu.VMEM((n, 2, LANES), jnp.float32),
            pltpu.VMEM((4, mics, mics, LANES), jnp.float32),
            pltpu.VMEM((PADDED, LANES), jnp.float32),
            pltpu.VMEM((LANES, MELS * 8), jnp.bfloat16),
            pltpu.VMEM(conv2_w.shape, jnp.bfloat16),
            pltpu.VMEM(proj_w.shape, jnp.bfloat16),
            pltpu.VMEM((2, mics, PADDED), jnp.float32),
            pltpu.VMEM((GROUP * stride, PADDED), jnp.float32),
            pltpu.VMEM((GROUP * stride, MELS * 8), jnp.float32),
            pltpu.VMEM((quarter, MELS * 8 + LANES), jnp.float32),
            pltpu.VMEM((LANES, 3 * channels), jnp.float32),
            pltpu.VMEM((q_count, LANES), jnp.bfloat16),
            pltpu.VMEM((q_count, 3 * channels), jnp.bfloat16),
            pltpu.SemaphoreType.DMA((2,)),
            pltpu.SemaphoreType.DMA((2,)),
            pltpu.SemaphoreType.DMA((n,)),
            pltpu.SemaphoreType.DMA((n,)),
            pltpu.SemaphoreType.DMA((n,)),
            pltpu.SemaphoreType.DMA((n,)),
            pltpu.SemaphoreType.DMA((11,)),
        ],
        compiler_params=pltpu.CompilerParams(
            collective_id=0, has_side_effects=True, vmem_limit_bytes=16 << 20
        ),
    )(
        valid,
        ref_mic,
        *(
            pltpu.with_memory_space_constraint(held, pltpu.HBM)
            for held in (
                waveform,
                masks,
                jnp.asarray(dft_table()),
                jnp.asarray(mel_bank()),
                jnp.asarray(repeat_table()),
                conv1_w,
                conv1_b[None],
                conv2_w,
                conv2_b[None],
                proj_w,
                proj_b[None],
            )
        ),
    )
    return features.astype(jnp.bfloat16)[None]


def solution(mesh):
    return jax.shard_map(
        functools.partial(per_device, mesh.shape["tm"]),
        mesh=mesh,
        in_specs=(
            P(None, ("meet", "tm")),
            P(None, ("meet", "tm"), None),
            P("meet"),
            P("meet"),
            P(),
            P(),
            P(),
            P(),
            P(),
            P(),
        ),
        out_specs=P(None, ("meet", "tm"), None),
        check_vma=False,
    )
```

```python
import functools
import math

import jax
import jax.numpy as jnp
import numpy as np
from jax import lax
from jax.experimental import pallas as pl
from jax.experimental.pallas import tpu as pltpu
from jax.sharding import PartitionSpec as P

NFFT = 512
HOP = 160
MELS = 80
BINS = NFFT // 2 + 1
LANES = 128
MAIN = BINS - 1
PADDED = MAIN + LANES
SPECTRUM = 2 * MAIN + LANES
GROUP = 4
SPAN = GROUP * HOP
WINDOW = 1024
SOLVERS = 8

loading = 0.03
epsilon = 1e-06
sample_rate = 16000.0


def dft_table():
    sample_pos = np.arange(NFFT)
    phase = (sample_pos[:, None] * np.arange(BINS)[None, :] % NFFT).astype(np.float32)
    phase = phase * np.float32(2.0 * math.pi / NFFT)
    ramp = sample_pos.astype(np.float32) * np.float32(2.0 * math.pi / NFFT)
    window = np.float32(0.5) - np.float32(0.5) * np.cos(ramp)
    cosines = window[:, None] * np.cos(phase)
    sines = -window[:, None] * np.sin(phase)
    table = np.zeros((NFFT, SPECTRUM), np.float32)
    table[:, :MAIN] = cosines[:, :MAIN]
    table[:, MAIN : 2 * MAIN] = sines[:, :MAIN]
    table[:, 2 * MAIN :] = cosines[:, MAIN:]
    return table.astype(jnp.bfloat16)


def mel_bank():
    mel_top = 2595.0 * math.log10(1.0 + sample_rate / 2.0 / 700.0)
    points = np.arange(MELS + 2) * (mel_top / (MELS + 1))
    edges_hz = 700.0 * (np.power(10.0, points / 2595.0) - 1.0)
    freq_hz = np.arange(BINS) * (sample_rate / 2.0 / (BINS - 1))
    lower, centre, upper = edges_hz[:-2], edges_hz[1:-1], edges_hz[2:]
    rising = (freq_hz[:, None] - lower[None, :]) / (centre - lower)[None, :]
    falling = (upper[None, :] - freq_hz[:, None]) / (upper - centre)[None, :]
    bank = np.zeros((PADDED, LANES), np.float32)
    bank[:BINS, :MELS] = np.maximum(np.minimum(rising, falling), 0.0)
    return bank


def repeat_table():
    table = np.zeros((LANES, MELS * 8), np.float32)
    for mel in range(MELS):
        table[mel, mel * 8 : mel * 8 + 8] = 1.0
    return table.astype(jnp.bfloat16)


def kernel(
    n,
    valid_ref,
    mic_ref,
    wave_hbm,
    masks_hbm,
    table_hbm,
    bank_hbm,
    repeat_hbm,
    conv1_w_hbm,
    conv1_b_hbm,
    conv2_hbm,
    conv2_b_hbm,
    proj_hbm,
    proj_b_hbm,
    out_ref,
    conv1_w,
    conv1_b,
    conv2_b,
    proj_b,
    wave,
    masks,
    table,
    ext,
    weight,
    spec,
    left,
    right,
    cov,
    part,
    landed,
    packed,
    gathered,
    full,
    bank,
    repeat,
    conv2_w,
    proj_w,
    beam,
    power,
    spread,
    lined,
    kernel_one,
    patches,
    first,
    nearby_send,
    nearby_recv,
    send_one,
    recv_one,
    send_two,
    recv_two,
    loads,
):
    rows, frames = masks.shape[0], masks.shape[1]
    mics, own = wave.shape
    groups = frames // GROUP + 1
    reach = right.shape[1]
    me = lax.axis_index("tm")
    solvers = part.shape[0]
    base = (n - solvers) // 2
    solving = (me >= base) & (me < base + solvers)
    load_wave = pltpu.make_async_copy(wave_hbm, wave, loads.at[0])
    load_table = pltpu.make_async_copy(table_hbm, table, loads.at[1])
    load_masks = pltpu.make_async_copy(masks_hbm, masks, loads.at[2])
    load_wave.start()
    load_table.start()
    load_masks.start()
    load_conv2 = pltpu.make_async_copy(conv2_hbm, conv2_w, loads.at[3])
    load_proj = pltpu.make_async_copy(proj_hbm, proj_w, loads.at[4])
    load_bank = pltpu.make_async_copy(bank_hbm, bank, loads.at[5])
    load_repeat = pltpu.make_async_copy(repeat_hbm, repeat, loads.at[6])
    barrier = pltpu.get_barrier_semaphore()

    def greet(to):
        pl.semaphore_signal(
            barrier,
            inc=1,
            device_id={"tm": to},
            device_id_type=pl.DeviceIdType.MESH,
        )

    @pl.when(solving)
    def _():
        for j in range(1, n):
            greet(lax.rem(me + j, n))

    @pl.when((me > 0) & jnp.logical_not(solving))
    def _():
        greet(me - 1)

    @pl.when((me < n - 1) & jnp.logical_not(solving))
    def _():
        greet(me + 1)

    def counted(here):
        return jnp.where(here, 1, 0).astype(jnp.int32)

    greeted = (
        solvers
        - counted(solving)
        + counted((me > 0) & ((me - 1 < base) | (me - 1 >= base + solvers)))
        + counted((me < n - 1) & ((me + 1 < base) | (me + 1 >= base + solvers)))
    )
    to_right = pltpu.make_async_remote_copy(
        src_ref=wave_hbm.at[:, own - SPAN :],
        dst_ref=left,
        send_sem=nearby_send.at[0],
        recv_sem=nearby_recv.at[0],
        device_id={"tm": lax.rem(me + 1, n)},
        device_id_type=pl.DeviceIdType.MESH,
    )
    to_left = pltpu.make_async_remote_copy(
        src_ref=wave_hbm.at[:, :reach],
        dst_ref=right,
        send_sem=nearby_send.at[1],
        recv_sem=nearby_recv.at[1],
        device_id={"tm": lax.rem(me + n - 1, n)},
        device_id_type=pl.DeviceIdType.MESH,
    )

    def meet():
        pl.semaphore_wait(barrier, greeted)

        @pl.when(me > 0)
        def _():
            to_left.start()

        @pl.when(me < n - 1)
        def _():
            to_right.start()

    late = me >= n // 2

    @pl.when(late)
    def _():
        meet()

    def transform(chosen):
        spans = jnp.concatenate(
            [ext[:, g * SPAN : g * SPAN + WINDOW] for g in chosen], axis=0
        )
        framed = jnp.concatenate(
            [
                (spans if r == 0 else pltpu.roll(spans, WINDOW - r * HOP, axis=1))[:, :NFFT]
                for r in range(GROUP)
            ],
            axis=0,
        ).astype(jnp.bfloat16)
        return jnp.dot(framed, table[...], preferred_element_type=jnp.float32)

    load_wave.wait()
    ext[:, SPAN : SPAN + own] = wave[...].astype(jnp.float32)
    load_table.wait()
    inner = list(range(1, groups - 1))
    found = transform(inner)
    width = len(inner) * mics
    for r in range(GROUP):
        spec[(r * groups + 1) * mics : (r * groups + 1) * mics + width, :] = found[
            r * width : (r + 1) * width
        ]

    @pl.when(jnp.logical_not(late))
    def _():
        meet()

    small = [
        pltpu.make_async_copy(source, held, loads.at[7 + i])
        for i, (source, held) in enumerate(
            (
                (conv1_w_hbm, conv1_w),
                (conv1_b_hbm, conv1_b),
                (conv2_b_hbm, conv2_b),
                (proj_b_hbm, proj_b),
            )
        )
    ]
    for load in small:
        load.start()
    load_bank.start()
    load_repeat.start()
    load_conv2.start()
    load_proj.start()

    load_masks.wait()
    limit = valid_ref[0] - me * frames
    alive = lax.broadcasted_iota(jnp.int32, (frames, MAIN), 0) < limit
    for k in range(rows):
        level = masks[k].astype(jnp.float32) * (1.0 / 255.0)
        weight[k, :, :MAIN] = jnp.where(alive, level[:, :MAIN], 0.0)
        weight[k, :, MAIN:] = jnp.where(
            alive[:, :LANES], jnp.broadcast_to(level[:, MAIN:], (frames, LANES)), 0.0
        )

    half = mics // 2
    low = lax.broadcasted_iota(jnp.int32, (mics, LANES), 0) < half

    def frames_of(h):
        first_row = h * 2 * GROUP
        if not isinstance(h, int):
            first_row = pl.multiple_of(first_row, 2 * GROUP)
        places = []
        for i in range(2 * GROUP):
            at = ((i % GROUP) * groups + 1 + 2 * h + i // GROUP) * mics
            if not isinstance(h, int):
                at = pl.multiple_of(at, mics)
            places.append(pl.ds(at, mics))
        return pl.ds(first_row, 2 * GROUP), places

    def add_block(h, totals, block):
        totals = list(totals)
        lanes = pl.ds(block * LANES, LANES)
        lanes_im = pl.ds(MAIN + block * LANES, LANES)
        span, places = frames_of(h)
        held = [weight[k, span, lanes] for k in range(rows)]
        for i, at in enumerate(places):
            re = spec[at, lanes]
            im = spec[at, lanes_im]
            w = [held[k][i : i + 1] for k in range(rows)]
            place = 0
            for d in range(half + 1):
                if d == 0:
                    products = [re * re + im * im]
                else:
                    re_n = pltpu.roll(re, mics - d, axis=0)
                    im_n = pltpu.roll(im, mics - d, axis=0)
                    real = re * re_n + im * im_n
                    imag = im * re_n - re * im_n
                    products = [real, imag] if d < half else [jnp.where(low, real, imag)]
                for product in products:
                    for k in range(rows):
                        slot = k * mics + place
                        totals[slot] = totals[slot] + w[k] * product
                    place += 1
        return tuple(totals)

    def add_last_bin(h, totals):
        totals = list(totals)
        span, places = frames_of(h)
        held = [weight[k, span, pl.ds(MAIN, LANES)] for k in range(rows)]
        for i, at in enumerate(places):
            re = spec[at, pl.ds(2 * MAIN, LANES)]
            for d in range(half + 1):
                product = re * (re if d == 0 else pltpu.roll(re, mics - d, axis=0))
                for k in range(rows):
                    slot = k * (half + 1) + d
                    totals[slot] = totals[slot] + held[k][i : i + 1] * product
        return tuple(totals)

    blocks = frames // (2 * GROUP)
    tiles = MAIN // LANES
    planes = rows * mics
    extra = rows * (half + 1)
    adders = [functools.partial(add_block, block=block) for block in range(tiles)]
    adders.append(add_last_bin)
    counts = [planes] * tiles + [extra]
    for block in range(tiles + 1):
        zeros = tuple(jnp.zeros((mics, LANES), jnp.float32) for _ in range(counts[block]))
        totals = lax.fori_loop(0, blocks - 1, adders[block], zeros)
        for slot in range(counts[block]):
            cov[block, slot] = totals[slot]

    @pl.when(me > 0)
    def _():
        to_right.wait_recv()
        ext[:, :SPAN] = left[...].astype(jnp.float32)

    @pl.when(me == 0)
    def _():
        ext[:, :SPAN] = jnp.zeros((mics, SPAN), jnp.float32)

    @pl.when(me < n - 1)
    def _():
        to_left.wait_recv()
        ext[:, SPAN + own :] = right[...].astype(jnp.float32)

    @pl.when(me == n - 1)
    def _():
        ext[:, SPAN + own :] = jnp.zeros((mics, reach), jnp.float32)

    found = transform([0, groups - 1])
    for r in range(GROUP):
        for i, g in enumerate((0, groups - 1)):
            at = (r * 2 + i) * mics
            spec[(r * groups + g) * mics : (r * groups + g + 1) * mics, :] = found[at : at + mics]

    lane = lax.broadcasted_iota(jnp.int32, (mics, LANES), 1)
    sub = lax.broadcasted_iota(jnp.int32, (mics, LANES), 0)
    width = MAIN // solvers
    per_tile = LANES // width
    deep = -(-planes // per_tile)

    def turned(value, amount):
        amount = amount % LANES
        return pltpu.roll(value, amount, axis=1) if amount else value

    totals = add_last_bin(blocks - 1, tuple(cov[tiles, slot] for slot in range(extra)))
    line = jnp.zeros((mics, LANES), jnp.float32)
    for slot in range(extra):
        line = jnp.where(lane == mics * slot + sub, totals[slot], line)
    line = jnp.sum(line, axis=0, keepdims=True)
    for to in range(solvers):
        part[to, deep * mics : deep * mics + 1, :] = line
    for block in range(tiles):
        totals = adders[block](blocks - 1, tuple(cov[block, slot] for slot in range(planes)))
        for slot in range(planes):
            cov[block, slot] = totals[slot]
        for to in range(block * per_tile, (block + 1) * per_tile):
            for tile in range(deep):
                packing = jnp.zeros((mics, LANES), jnp.float32)
                for i in range(min(per_tile, planes - tile * per_tile)):
                    moved = turned(cov[block, tile * per_tile + i], (i - to % per_tile) * width)
                    packing = moved if i == 0 else jnp.where(lane // width == i, moved, packing)
                part[to, tile * mics : (tile + 1) * mics, :] = packing

    def parcel(to, offset):
        return pltpu.make_async_remote_copy(
            src_ref=part.at[to],
            dst_ref=landed.at[offset],
            send_sem=send_one.at[to],
            recv_sem=recv_one.at[offset],
            device_id={"tm": base + to},
            device_id_type=pl.DeviceIdType.MESH,
        )

    for to in range(solvers):

        @pl.when(me != base + to)
        def _():
            parcel(to, lax.rem(base + to + n - me, n)).start()

    for load in small:
        load.wait()
    channels = conv1_w.shape[1]
    kernel_one[...] = jnp.zeros_like(kernel_one)
    for a in range(3):
        for b in range(3):
            tap = conv1_w[3 * a + b : 3 * a + b + 1, :].astype(jnp.float32)
            for late in range(3):
                at = b * 8 + 2 * late + a
                kernel_one[at : at + 1, late * channels : (late + 1) * channels] = tap
    power[...] = jnp.zeros_like(power)
    lined[...] = jnp.zeros_like(lined)

    upper = mics // 2

    def folded(value):
        return jnp.where(
            lane < 2 * width,
            value,
            turned(pltpu.roll(value, mics - upper, axis=0), 2 * width),
        )

    def answer(offset, to, tall):
        return pltpu.make_async_remote_copy(
            src_ref=packed.at[:tall],
            dst_ref=gathered.at[me - base, :tall],
            send_sem=send_two.at[offset],
            recv_sem=recv_two.at[me - base],
            device_id={"tm": to},
            device_id_type=pl.DeviceIdType.MESH,
        )

    def answers(act):
        @pl.when(me == base)
        def _():
            for j in range(1, n):
                act(answer(j, lax.rem(me + j, n), mics))

        @pl.when(solving & (me != base))
        def _():
            for j in range(1, n):
                act(answer(j, lax.rem(me + j, n), upper))

    @pl.when(solving)
    def _():
        total = part[me - base]
        for j in range(1, n):
            parcel(0, j).wait_recv()
            total = total + landed[j]
        line = total[deep * mics : deep * mics + 1]
        lasts = [
            jnp.sum(jnp.where(lane == mics * slot + sub, line, 0.0), axis=1, keepdims=True)
            for slot in range(extra)
        ]
        whole = []
        for slot in range(planes):
            tile = slot // per_tile
            plane = turned(total[tile * mics : (tile + 1) * mics], -(slot % per_tile) * width)
            k, place = slot // mics, slot % mics
            d = (place + 1) // 2
            if place == 0 or (place % 2 == 1 and d < half):
                at_last = lasts[k * (half + 1) + d]
            elif d == half:
                at_last = jnp.where(low, lasts[k * (half + 1) + d], 0.0)
            else:
                at_last = jnp.zeros((mics, LANES), jnp.float32)
            whole.append(jnp.where(lane == width, at_last, plane))
        real, imag = solve(whole, mics, full, mic_ref[0])
        main = folded(jnp.where(lane < width, real, turned(imag, width)))
        rest = folded(jnp.where(lane < width, turned(real, -width), imag))
        sent = jnp.where(sub < upper, main, pltpu.roll(rest, upper, axis=0))
        packed[...] = sent
        gathered[me - base] = sent

    answers(lambda copy: copy.start())

    @pl.when(me < n - 1)
    def _():
        to_right.wait_send()

    @pl.when(me > 0)
    def _():
        to_left.wait_send()

    for to in range(solvers):

        @pl.when(me != base + to)
        def _():
            pltpu.make_async_copy(
                packed.at[: mics if to == 0 else upper],
                gathered.at[to, : mics if to == 0 else upper],
                recv_two.at[to],
            ).wait()

    def unfolded(value):
        return jnp.where(
            sub < upper, value, turned(pltpu.roll(value, upper, axis=0), -2 * width)
        )

    for block in range(tiles):
        joined = [jnp.zeros((mics, LANES), jnp.float32)] * 2
        for t in range(per_tile):
            value = unfolded(gathered[block * per_tile + t])
            for i in range(2):
                moved = turned(value, (t - i) * width)
                joined[i] = moved if t == 0 else jnp.where(lane // width == t, moved, joined[i])
        for i in range(2):
            beam[i, :, block * LANES : (block + 1) * LANES] = joined[i]
    rest = unfolded(pltpu.roll(gathered[0], mics - upper, axis=0))
    for i in range(2):
        at_last = jnp.sum(jnp.where(lane == i * width, rest, 0.0), axis=1, keepdims=True)
        beam[i, :, MAIN:] = jnp.broadcast_to(at_last, (mics, LANES))

    load_bank.wait()
    load_repeat.wait()
    stem(
        valid_ref[0],
        spec,
        bank,
        repeat,
        conv1_b,
        load_conv2,
        conv2_w,
        conv2_b,
        load_proj,
        proj_w,
        proj_b,
        out_ref,
        beam,
        power,
        spread,
        lined,
        kernel_one,
        patches,
        first,
    )
    for to in range(solvers):

        @pl.when(me != base + to)
        def _():
            parcel(to, lax.rem(base + to + n - me, n)).wait_send()

    answers(lambda copy: copy.wait_send())


def solve(planes, mics, full, ref):
    half = mics // 2
    for k in range(2):
        for m in range(mics):
            for d in range(half + 1):
                n = (m + d) % mics
                if d == half and m >= half:
                    continue

                def row(plane, at):
                    return planes[k * mics + plane][at : at + 1]

                if d == 0:
                    full[2 * k, m, m : m + 1, :] = row(0, m)
                    full[2 * k + 1, m, m : m + 1, :] = jnp.zeros((1, LANES), jnp.float32)
                    continue
                if d < half:
                    real, imag = row(2 * d - 1, m), row(2 * d, m)
                else:
                    real, imag = row(2 * d - 1, m), -row(2 * d - 1, m + half)
                full[2 * k, m, n : n + 1, :] = real
                full[2 * k + 1, m, n : n + 1, :] = imag
                full[2 * k, n, m : m + 1, :] = real
                full[2 * k + 1, n, m : m + 1, :] = -imag
    answer_re = [full[0, m] for m in range(mics)]
    answer_im = [full[1, m] for m in range(mics)]
    matrix_re = [full[2, m] for m in range(mics)]
    matrix_im = [full[3, m] for m in range(mics)]
    index = lax.broadcasted_iota(jnp.int32, (mics, LANES), 0)
    spread = matrix_re[0][0:1]
    for m in range(1, mics):
        spread = spread + matrix_re[m][m : m + 1]
    ridge = loading * spread / mics + epsilon
    matrix_re = [
        jnp.where(index == m, matrix_re[m] + ridge, matrix_re[m]) for m in range(mics)
    ]
    for p in range(mics):
        pivot_re, pivot_im = matrix_re[p][p : p + 1], matrix_im[p][p : p + 1]
        scale = 1.0 / (pivot_re * pivot_re + pivot_im * pivot_im)
        inverse_re, inverse_im = pivot_re * scale, -pivot_im * scale
        lead_re = matrix_re[p] * inverse_re - matrix_im[p] * inverse_im
        lead_im = matrix_re[p] * inverse_im + matrix_im[p] * inverse_re
        head_re = answer_re[p] * inverse_re - answer_im[p] * inverse_im
        head_im = answer_re[p] * inverse_im + answer_im[p] * inverse_re
        for m in range(mics):
            if m == p:
                continue
            column_re, column_im = matrix_re[m][p : p + 1], matrix_im[m][p : p + 1]
            matrix_re[m] = matrix_re[m] - (column_re * lead_re - column_im * lead_im)
            matrix_im[m] = matrix_im[m] - (column_re * lead_im + column_im * lead_re)
            answer_re[m] = answer_re[m] - (column_re * head_re - column_im * head_im)
            answer_im[m] = answer_im[m] - (column_re * head_im + column_im * head_re)
        matrix_re[p], matrix_im[p] = lead_re, lead_im
        answer_re[p], answer_im[p] = head_re, head_im
    trace = answer_re[0][0:1]
    for m in range(1, mics):
        trace = trace + answer_re[m][m : m + 1]
    scale = 1.0 / (trace + epsilon)
    picked = index == ref
    beam_re = jnp.zeros((mics, LANES), jnp.float32)
    beam_im = jnp.zeros((mics, LANES), jnp.float32)
    for m in range(mics):
        real = jnp.sum(jnp.where(picked, answer_re[m], 0.0), axis=0, keepdims=True)
        imag = jnp.sum(jnp.where(picked, answer_im[m], 0.0), axis=0, keepdims=True)
        beam_re = jnp.where(index == m, real * scale, beam_re)
        beam_im = jnp.where(index == m, imag * scale, beam_im)
    return beam_re, beam_im


def row_sums(values):
    count = len(values)
    sub = lax.broadcasted_iota(jnp.int32, values[0].shape, 0)
    step = count // 2
    while step:
        upper = sub // step % 2 == 1
        values = [
            jnp.where(
                upper,
                values[i + step] + pltpu.roll(values[i + step], step, axis=0),
                values[i] + pltpu.roll(values[i], count - step, axis=0),
            )
            for i in range(step)
        ]
        step //= 2
    return values[0]


def stem(
    valid,
    spec,
    bank,
    repeat,
    conv1_b,
    load_conv2,
    conv2_w,
    conv2_b,
    load_proj,
    proj_w,
    proj_b,
    out_ref,
    beam,
    power,
    spread,
    lined,
    kernel_one,
    patches,
    first,
):
    mics = beam.shape[1]
    quarter = out_ref.shape[0]
    groups = quarter + 1
    frames = quarter * GROUP
    stride = power.shape[0] // GROUP
    channels = conv2_w.shape[1]
    q_first = (MELS - 3) // 2 + 1
    q_second = (q_first - 3) // 2 + 1
    position = lax.axis_index("tm")
    for block in range(PADDED // LANES):
        lanes = pl.ds(block * LANES, LANES)
        beam_re = beam[0, :, lanes]
        beam_im = beam[1, :, lanes]

        def products(r, g):
            at = slice((r * groups + g) * mics, (r * groups + g + 1) * mics)
            if block < MAIN // LANES:
                re = spec[at, lanes]
                im = spec[at, pl.ds(MAIN + block * LANES, LANES)]
                return beam_re * re + beam_im * im, beam_re * im - beam_im * re
            re = spec[at, pl.ds(2 * MAIN, LANES)]
            return beam_re * re, -beam_im * re

        for r in range(GROUP):
            for g in range(0, groups - mics + 1, mics):
                pairs = [products(r, g + i) for i in range(mics)]
                real = row_sums([pair[0] for pair in pairs])
                imag = row_sums([pair[1] for pair in pairs])
                at = r * stride + g
                power[at : at + mics, lanes] = real * real + imag * imag
            for g in range(groups - groups % mics, groups):
                real, imag = products(r, g)
                real = jnp.sum(real, axis=0, keepdims=True)
                imag = jnp.sum(imag, axis=0, keepdims=True)
                at = r * stride + g
                power[at : at + 1, lanes] = real * real + imag * imag

    melspec = (
        jnp.dot(
            power[:, :MAIN],
            bank[:MAIN, :],
            preferred_element_type=jnp.float32,
            precision=lax.Precision.HIGHEST,
        )
        + power[:, MAIN:] * bank[MAIN : MAIN + 1, :]
    )
    row = lax.broadcasted_iota(jnp.int32, melspec.shape, 0)
    frame = position * frames + (row % stride - 1) * GROUP + row // stride
    alive = (frame >= 0) & (frame < valid)
    logmel = jnp.where(alive, jnp.log(melspec + epsilon), 0.0).astype(jnp.bfloat16)
    spread[...] = jnp.dot(logmel, repeat[...], preferred_element_type=jnp.float32)
    width = spread.shape[1]
    phase = lax.broadcasted_iota(jnp.int32, (quarter, width), 1) % 8
    mixed = jnp.zeros((quarter, width), jnp.float32)
    for u in range(7):
        start = (u + 1) % GROUP * stride + (u + 1) // GROUP
        mixed = jnp.where(phase == u, spread[start : start + quarter, :], mixed)
    lined[:, :width] = mixed
    order = list(range(0, q_first, 2)) + list(range(1, q_first, 2))
    for place, q in enumerate(order):
        base = 16 * q // LANES * LANES
        shift = 16 * q - base
        two = lined[:, base : base + 2 * LANES]
        if shift:
            two = pltpu.roll(two, 2 * LANES - shift, axis=1)
        patches[place * quarter : (place + 1) * quarter, :] = two[:, :LANES].astype(jnp.bfloat16)

    kernel_bf = kernel_one[...].astype(jnp.bfloat16)
    for late in range(3):
        lanes = slice(late * channels, (late + 1) * channels)
        one = jnp.dot(patches[...], kernel_bf[:, lanes], preferred_element_type=jnp.float32)
        one = jnp.maximum(one + conv1_b[...], 0.0)
        if late == 0:
            step = lax.broadcasted_iota(jnp.int32, one.shape, 0) % quarter
            one = jnp.where((step == 0) & (position == 0), 0.0, one)
        first[:, lanes] = one.astype(jnp.bfloat16)

    load_conv2.wait()
    evens = (q_first + 1) // 2
    summed = jnp.zeros((q_second * quarter, channels), jnp.float32)
    for b in range(3):
        start = {0: 0, 1: evens, 2: 1}[b] * quarter
        for late in range(3):
            summed = summed + jnp.dot(
                first[start : start + q_second * quarter, late * channels : (late + 1) * channels],
                conv2_w[3 * late + b],
                preferred_element_type=jnp.float32,
            )
    second = jnp.maximum(summed + conv2_b[...], 0.0).astype(jnp.bfloat16)
    load_proj.wait()
    out = jnp.zeros((quarter, out_ref.shape[1]), jnp.float32)
    for r in range(q_second):
        out = out + jnp.dot(
            second[r * quarter : (r + 1) * quarter],
            proj_w[r * channels : (r + 1) * channels, :],
            preferred_element_type=jnp.float32,
        )
    out_row = lax.broadcasted_iota(jnp.int32, out.shape, 0) + position * quarter
    out = jnp.where(GROUP * out_row < valid, out + proj_b[...], 0.0)
    out_ref[...] = out


def per_device(
    n, waveform, masks, valid, ref_mic, conv1_w, conv1_b, conv2_w, conv2_b, proj_w, proj_b
):
    mics, own = waveform.shape
    rows, frames = masks.shape[0], masks.shape[1]
    groups = frames // GROUP + 1
    quarter = frames // GROUP
    channels = conv1_w.shape[1]
    model = proj_w.shape[1]
    reach = WINDOW - SPAN
    vmem = pl.BlockSpec(memory_space=pltpu.VMEM)
    smem = pl.BlockSpec(memory_space=pltpu.SMEM)
    anywhere = pl.BlockSpec(memory_space=pltpu.HBM)
    planes = rows * mics
    solvers = min(SOLVERS, n)
    deep = -(-planes * (MAIN // solvers) // LANES)
    tall = deep * mics + 1
    stride = -(-groups // 8) * 8
    q_first = (MELS - 3) // 2 + 1
    q_count = q_first * quarter
    features = pl.pallas_call(
        functools.partial(kernel, n),
        out_shape=jax.ShapeDtypeStruct((quarter, model), jnp.float32),
        in_specs=[smem] * 2 + [anywhere] * 5 + [anywhere, anywhere, anywhere, anywhere, anywhere, anywhere],
        out_specs=vmem,
        scratch_shapes=[
            pltpu.VMEM(conv1_w.shape, conv1_w.dtype),
            pltpu.VMEM((1, channels), jnp.float32),
            pltpu.VMEM((1, channels), jnp.float32),
            pltpu.VMEM((1, model), jnp.float32),
            pltpu.VMEM(waveform.shape, waveform.dtype),
            pltpu.VMEM(masks.shape, masks.dtype),
            pltpu.VMEM((NFFT, SPECTRUM), jnp.bfloat16),
            pltpu.VMEM((mics, SPAN + own + reach), jnp.float32),
            pltpu.VMEM((rows, frames, PADDED), jnp.float32),
            pltpu.VMEM((GROUP * groups * mics, SPECTRUM), jnp.float32),
            pltpu.VMEM((mics, SPAN), waveform.dtype),
            pltpu.VMEM((mics, reach), waveform.dtype),
            pltpu.VMEM((PADDED // LANES, planes, mics, LANES), jnp.float32),
            pltpu.VMEM((solvers, tall, LANES), jnp.float32),
            pltpu.VMEM((n, tall, LANES), jnp.float32),
            pltpu.VMEM((mics, LANES), jnp.float32),
            pltpu.VMEM((solvers, mics, LANES), jnp.float32),
            pltpu.VMEM((4, mics, mics, LANES), jnp.float32),
            pltpu.VMEM((PADDED, LANES), jnp.float32),
            pltpu.VMEM((LANES, MELS * 8), jnp.bfloat16),
            pltpu.VMEM(conv2_w.shape, jnp.bfloat16),
            pltpu.VMEM(proj_w.shape, jnp.bfloat16),
            pltpu.VMEM((2, mics, PADDED), jnp.float32),
            pltpu.VMEM((GROUP * stride, PADDED), jnp.float32),
            pltpu.VMEM((GROUP * stride, MELS * 8), jnp.float32),
            pltpu.VMEM((quarter, MELS * 8 + LANES), jnp.float32),
            pltpu.VMEM((LANES, 3 * channels), jnp.float32),
            pltpu.VMEM((q_count, LANES), jnp.bfloat16),
            pltpu.VMEM((q_count, 3 * channels), jnp.bfloat16),
            pltpu.SemaphoreType.DMA((2,)),
            pltpu.SemaphoreType.DMA((2,)),
            pltpu.SemaphoreType.DMA((n,)),
            pltpu.SemaphoreType.DMA((n,)),
            pltpu.SemaphoreType.DMA((n,)),
            pltpu.SemaphoreType.DMA((n,)),
            pltpu.SemaphoreType.DMA((11,)),
        ],
        compiler_params=pltpu.CompilerParams(
            collective_id=0, has_side_effects=True, vmem_limit_bytes=16 << 20
        ),
    )(
        valid,
        ref_mic,
        *(
            pltpu.with_memory_space_constraint(held, pltpu.HBM)
            for held in (
                waveform,
                masks,
                jnp.asarray(dft_table()),
                jnp.asarray(mel_bank()),
                jnp.asarray(repeat_table()),
                conv1_w,
                conv1_b[None],
                conv2_w,
                conv2_b[None],
                proj_w,
                proj_b[None],
            )
        ),
    )
    return features.astype(jnp.bfloat16)[None]


def solution(mesh):
    return jax.shard_map(
        functools.partial(per_device, mesh.shape["tm"]),
        mesh=mesh,
        in_specs=(
            P(None, ("meet", "tm")),
            P(None, ("meet", "tm"), None),
            P("meet"),
            P("meet"),
            P(),
            P(),
            P(),
            P(),
            P(),
            P(),
        ),
        out_specs=P(None, ("meet", "tm"), None),
        check_vma=False,
    )
```

```python
import functools
import math

import jax
import jax.numpy as jnp
import numpy as np
from jax import lax
from jax.experimental import pallas as pl
from jax.experimental.pallas import tpu as pltpu
from jax.sharding import PartitionSpec as P

NFFT = 512
HOP = 160
MELS = 80
BINS = NFFT // 2 + 1
LANES = 128
MAIN = BINS - 1
PADDED = MAIN + LANES
SPECTRUM = 2 * MAIN + LANES
GROUP = 4
SPAN = GROUP * HOP
WINDOW = 1024
SOLVERS = 8
LEVEL = 32000.0
TINY = 1e-30

loading = 0.03
epsilon = 1e-06
sample_rate = 16000.0


def dft_table():
    sample_pos = np.arange(NFFT)
    phase = (sample_pos[:, None] * np.arange(BINS)[None, :] % NFFT).astype(np.float32)
    phase = phase * np.float32(2.0 * math.pi / NFFT)
    ramp = sample_pos.astype(np.float32) * np.float32(2.0 * math.pi / NFFT)
    window = np.float32(0.5) - np.float32(0.5) * np.cos(ramp)
    cosines = window[:, None] * np.cos(phase)
    sines = -window[:, None] * np.sin(phase)
    table = np.zeros((NFFT, SPECTRUM), np.float32)
    table[:, :MAIN] = cosines[:, :MAIN]
    table[:, MAIN : 2 * MAIN] = sines[:, :MAIN]
    table[:, 2 * MAIN :] = cosines[:, MAIN:]
    return table.astype(jnp.bfloat16)


def mel_bank():
    mel_top = 2595.0 * math.log10(1.0 + sample_rate / 2.0 / 700.0)
    points = np.arange(MELS + 2) * (mel_top / (MELS + 1))
    edges_hz = 700.0 * (np.power(10.0, points / 2595.0) - 1.0)
    freq_hz = np.arange(BINS) * (sample_rate / 2.0 / (BINS - 1))
    lower, centre, upper = edges_hz[:-2], edges_hz[1:-1], edges_hz[2:]
    rising = (freq_hz[:, None] - lower[None, :]) / (centre - lower)[None, :]
    falling = (upper[None, :] - freq_hz[:, None]) / (upper - centre)[None, :]
    bank = np.zeros((PADDED, LANES), np.float32)
    bank[:BINS, :MELS] = np.maximum(np.minimum(rising, falling), 0.0)
    return bank


def repeat_table():
    table = np.zeros((LANES, MELS * 8), np.float32)
    for mel in range(MELS):
        table[mel, mel * 8 : mel * 8 + 8] = 1.0
    return table.astype(jnp.bfloat16)


def kernel(
    n,
    valid_ref,
    mic_ref,
    wave_hbm,
    masks_hbm,
    table_hbm,
    bank_hbm,
    repeat_hbm,
    conv1_w_hbm,
    conv1_b_hbm,
    conv2_hbm,
    conv2_b_hbm,
    proj_hbm,
    proj_b_hbm,
    out_ref,
    conv1_w,
    conv1_b,
    conv2_b,
    proj_b,
    wave,
    masks,
    table,
    ext,
    weight,
    spec,
    left,
    right,
    cov,
    part,
    notes,
    landed,
    noted,
    packed,
    gathered,
    full,
    bank,
    repeat,
    conv2_w,
    proj_w,
    beam,
    power,
    spread,
    lined,
    kernel_one,
    patches,
    first,
    nearby_send,
    nearby_recv,
    send_one,
    recv_one,
    send_note,
    recv_note,
    send_two,
    recv_two,
    loads,
):
    rows, frames = masks.shape[0], masks.shape[1]
    mics, own = wave.shape
    groups = frames // GROUP + 1
    reach = right.shape[1]
    me = lax.axis_index("tm")
    solvers = part.shape[0]
    base = (n - solvers) // 2
    solving = (me >= base) & (me < base + solvers)
    load_wave = pltpu.make_async_copy(wave_hbm, wave, loads.at[0])
    load_table = pltpu.make_async_copy(table_hbm, table, loads.at[1])
    load_masks = pltpu.make_async_copy(masks_hbm, masks, loads.at[2])
    load_wave.start()
    load_table.start()
    load_masks.start()
    load_conv2 = pltpu.make_async_copy(conv2_hbm, conv2_w, loads.at[3])
    load_proj = pltpu.make_async_copy(proj_hbm, proj_w, loads.at[4])
    load_bank = pltpu.make_async_copy(bank_hbm, bank, loads.at[5])
    load_repeat = pltpu.make_async_copy(repeat_hbm, repeat, loads.at[6])
    barrier = pltpu.get_barrier_semaphore()

    def greet(to):
        pl.semaphore_signal(
            barrier,
            inc=1,
            device_id={"tm": to},
            device_id_type=pl.DeviceIdType.MESH,
        )

    @pl.when(solving)
    def _():
        for j in range(1, n):
            greet(lax.rem(me + j, n))

    @pl.when((me > 0) & jnp.logical_not(solving))
    def _():
        greet(me - 1)

    @pl.when((me < n - 1) & jnp.logical_not(solving))
    def _():
        greet(me + 1)

    def counted(here):
        return jnp.where(here, 1, 0).astype(jnp.int32)

    greeted = (
        solvers
        - counted(solving)
        + counted((me > 0) & ((me - 1 < base) | (me - 1 >= base + solvers)))
        + counted((me < n - 1) & ((me + 1 < base) | (me + 1 >= base + solvers)))
    )
    to_right = pltpu.make_async_remote_copy(
        src_ref=wave_hbm.at[:, own - SPAN :],
        dst_ref=left,
        send_sem=nearby_send.at[0],
        recv_sem=nearby_recv.at[0],
        device_id={"tm": lax.rem(me + 1, n)},
        device_id_type=pl.DeviceIdType.MESH,
    )
    to_left = pltpu.make_async_remote_copy(
        src_ref=wave_hbm.at[:, :reach],
        dst_ref=right,
        send_sem=nearby_send.at[1],
        recv_sem=nearby_recv.at[1],
        device_id={"tm": lax.rem(me + n - 1, n)},
        device_id_type=pl.DeviceIdType.MESH,
    )

    def meet():
        pl.semaphore_wait(barrier, greeted)

        @pl.when(me > 0)
        def _():
            to_left.start()

        @pl.when(me < n - 1)
        def _():
            to_right.start()

    late = me >= base + solvers

    @pl.when(late)
    def _():
        meet()

    def transform(chosen):
        spans = jnp.concatenate(
            [ext[:, g * SPAN : g * SPAN + WINDOW] for g in chosen], axis=0
        )
        framed = jnp.concatenate(
            [
                (spans if r == 0 else pltpu.roll(spans, WINDOW - r * HOP, axis=1))[:, :NFFT]
                for r in range(GROUP)
            ],
            axis=0,
        ).astype(jnp.bfloat16)
        return jnp.dot(framed, table[...], preferred_element_type=jnp.float32)

    load_wave.wait()
    ext[:, SPAN : SPAN + own] = wave[...].astype(jnp.float32)
    load_table.wait()
    inner = list(range(1, groups - 1))
    found = transform(inner)
    width = len(inner) * mics
    for r in range(GROUP):
        spec[(r * groups + 1) * mics : (r * groups + 1) * mics + width, :] = found[
            r * width : (r + 1) * width
        ]

    @pl.when(jnp.logical_not(late))
    def _():
        meet()

    small = [
        pltpu.make_async_copy(source, held, loads.at[7 + i])
        for i, (source, held) in enumerate(
            (
                (conv1_w_hbm, conv1_w),
                (conv1_b_hbm, conv1_b),
                (conv2_b_hbm, conv2_b),
                (proj_b_hbm, proj_b),
            )
        )
    ]
    for load in small:
        load.start()
    load_bank.start()
    load_repeat.start()
    load_conv2.start()
    load_proj.start()

    load_masks.wait()
    limit = valid_ref[0] - me * frames
    alive = lax.broadcasted_iota(jnp.int32, (frames, MAIN), 0) < limit
    for k in range(rows):
        level = masks[k].astype(jnp.float32) * (1.0 / 255.0)
        weight[k, :, :MAIN] = jnp.where(alive, level[:, :MAIN], 0.0)
        weight[k, :, MAIN:] = jnp.where(
            alive[:, :LANES], jnp.broadcast_to(level[:, MAIN:], (frames, LANES)), 0.0
        )

    half = mics // 2
    low = lax.broadcasted_iota(jnp.int32, (mics, LANES), 0) < half

    def frames_of(h):
        first_row = h * 2 * GROUP
        if not isinstance(h, int):
            first_row = pl.multiple_of(first_row, 2 * GROUP)
        places = []
        for i in range(2 * GROUP):
            at = ((i % GROUP) * groups + 1 + 2 * h + i // GROUP) * mics
            if not isinstance(h, int):
                at = pl.multiple_of(at, mics)
            places.append(pl.ds(at, mics))
        return pl.ds(first_row, 2 * GROUP), places

    def add_block(h, totals, block):
        totals = list(totals)
        lanes = pl.ds(block * LANES, LANES)
        lanes_im = pl.ds(MAIN + block * LANES, LANES)
        span, places = frames_of(h)
        held = [weight[k, span, lanes] for k in range(rows)]
        for i, at in enumerate(places):
            re = spec[at, lanes]
            im = spec[at, lanes_im]
            w = [held[k][i : i + 1] for k in range(rows)]
            place = 0
            for d in range(half + 1):
                if d == 0:
                    products = [re * re + im * im]
                else:
                    re_n = pltpu.roll(re, mics - d, axis=0)
                    im_n = pltpu.roll(im, mics - d, axis=0)
                    real = re * re_n + im * im_n
                    imag = im * re_n - re * im_n
                    products = [real, imag] if d < half else [jnp.where(low, real, imag)]
                for product in products:
                    for k in range(rows):
                        slot = k * mics + place
                        totals[slot] = totals[slot] + w[k] * product
                    place += 1
        return tuple(totals)

    def add_last_bin(h, totals):
        totals = list(totals)
        span, places = frames_of(h)
        held = [weight[k, span, pl.ds(MAIN, LANES)] for k in range(rows)]
        for i, at in enumerate(places):
            re = spec[at, pl.ds(2 * MAIN, LANES)]
            for d in range(half + 1):
                product = re * (re if d == 0 else pltpu.roll(re, mics - d, axis=0))
                for k in range(rows):
                    slot = k * (half + 1) + d
                    totals[slot] = totals[slot] + held[k][i : i + 1] * product
        return tuple(totals)

    blocks = frames // (2 * GROUP)
    tiles = MAIN // LANES
    planes = rows * mics
    extra = rows * (half + 1)
    adders = [functools.partial(add_block, block=block) for block in range(tiles)]
    adders.append(add_last_bin)
    counts = [planes] * tiles + [extra]
    for block in range(tiles + 1):
        zeros = tuple(jnp.zeros((mics, LANES), jnp.float32) for _ in range(counts[block]))
        totals = lax.fori_loop(0, blocks - 1, adders[block], zeros)
        for slot in range(counts[block]):
            cov[block, slot] = totals[slot]

    @pl.when(me > 0)
    def _():
        to_right.wait_recv()
        ext[:, :SPAN] = left[...].astype(jnp.float32)

    @pl.when(me == 0)
    def _():
        ext[:, :SPAN] = jnp.zeros((mics, SPAN), jnp.float32)

    @pl.when(me < n - 1)
    def _():
        to_left.wait_recv()
        ext[:, SPAN + own :] = right[...].astype(jnp.float32)

    @pl.when(me == n - 1)
    def _():
        ext[:, SPAN + own :] = jnp.zeros((mics, reach), jnp.float32)

    found = transform([0, groups - 1])
    for r in range(GROUP):
        for i, g in enumerate((0, groups - 1)):
            at = (r * 2 + i) * mics
            spec[(r * groups + g) * mics : (r * groups + g + 1) * mics, :] = found[at : at + mics]

    lane = lax.broadcasted_iota(jnp.int32, (mics, LANES), 1)
    sub = lax.broadcasted_iota(jnp.int32, (mics, LANES), 0)
    width = MAIN // solvers
    per_tile = LANES // width
    deep = -(-planes // per_tile)

    def turned(value, amount):
        amount = amount % LANES
        return pltpu.roll(value, amount, axis=1) if amount else value

    totals = add_last_bin(blocks - 1, tuple(cov[tiles, slot] for slot in range(extra)))
    line = jnp.zeros((mics, LANES), jnp.float32)
    for slot in range(extra):
        line = jnp.where(lane == mics * slot + sub, totals[slot], line)
    line = jnp.sum(line, axis=0, keepdims=True)
    for to in range(solvers):
        notes[to, rows : rows + 1, :] = line
    group = lane // width

    def packed_for(to, values):
        packing = values[0]
        for i in range(1, per_tile):
            packing = jnp.where(group == (to + i) % per_tile, values[i], packing)
        return packing

    for block in range(tiles):
        totals = adders[block](blocks - 1, tuple(cov[block, slot] for slot in range(planes)))
        turns = []
        for k in range(rows):
            peak = jnp.maximum(jnp.max(totals[k * mics], axis=0, keepdims=True), TINY)
            peak = jnp.broadcast_to(peak, (mics, LANES))
            turns.append([turned(peak * (1.0 / LEVEL), i * width) for i in range(per_tile)])
            scale = LEVEL / peak
            for slot in range(k * mics, (k + 1) * mics):
                cov[block, slot] = turned(totals[slot] * scale, slot % per_tile * width)
        for to in range(block * per_tile, (block + 1) * per_tile):
            for k in range(rows):
                notes[to, k : k + 1, :] = packed_for(to, turns[k])[:1]
            for tile in range(deep):
                values = [cov[block, tile * per_tile + i] for i in range(per_tile)]
                whole = jnp.round(packed_for(to, values)).astype(jnp.int32)
                part[to, tile * mics : (tile + 1) * mics, :] = whole.astype(jnp.int16)

    def parcel(to, offset):
        return pltpu.make_async_remote_copy(
            src_ref=part.at[to],
            dst_ref=landed.at[offset],
            send_sem=send_one.at[to],
            recv_sem=recv_one.at[offset],
            device_id={"tm": base + to},
            device_id_type=pl.DeviceIdType.MESH,
        )

    def note(to, offset):
        return pltpu.make_async_remote_copy(
            src_ref=notes.at[to],
            dst_ref=noted.at[offset],
            send_sem=send_note.at[to],
            recv_sem=recv_note.at[offset],
            device_id={"tm": base + to},
            device_id_type=pl.DeviceIdType.MESH,
        )

    for to in range(solvers):

        @pl.when(me != base + to)
        def _():
            offset = lax.rem(base + to + n - me, n)
            parcel(to, offset).start()
            note(to, offset).start()

    for load in small:
        load.wait()
    channels = conv1_w.shape[1]
    kernel_one[...] = jnp.zeros_like(kernel_one)
    for a in range(3):
        for b in range(3):
            tap = conv1_w[3 * a + b : 3 * a + b + 1, :].astype(jnp.float32)
            for late in range(3):
                at = b * 8 + 2 * late + a
                kernel_one[at : at + 1, late * channels : (late + 1) * channels] = tap
    power[...] = jnp.zeros_like(power)
    lined[...] = jnp.zeros_like(lined)

    upper = mics // 2

    def folded(value):
        return jnp.where(
            lane < 2 * width,
            value,
            turned(pltpu.roll(value, mics - upper, axis=0), 2 * width),
        )

    def answer(offset, to, tall):
        return pltpu.make_async_remote_copy(
            src_ref=packed.at[:tall],
            dst_ref=gathered.at[me - base, :tall],
            send_sem=send_two.at[offset],
            recv_sem=recv_two.at[me - base],
            device_id={"tm": to},
            device_id_type=pl.DeviceIdType.MESH,
        )

    def answers(act):
        @pl.when(me == base)
        def _():
            for j in range(1, n):
                act(answer(j, lax.rem(me + j, n), mics))

        @pl.when(solving & (me != base))
        def _():
            for j in range(1, n):
                act(answer(j, lax.rem(me + j, n), upper))

    @pl.when(solving)
    def _():
        def levels(codes, held):
            codes = codes.astype(jnp.int32).astype(jnp.float32)
            return [
                codes[tile * mics : (tile + 1) * mics]
                * held[tile * per_tile // mics : tile * per_tile // mics + 1]
                for tile in range(deep)
            ]

        total = levels(part[me - base], notes[me - base])
        line = notes[me - base, rows : rows + 1]
        for j in range(1, n):
            parcel(0, j).wait_recv()
            note(0, j).wait_recv()
            total = [a + b for a, b in zip(total, levels(landed[j], noted[j]))]
            line = line + noted[j, rows : rows + 1]
        back = lax.rem(per_tile - lax.rem(me - base, per_tile), per_tile) * width
        total = [pltpu.roll(value, back, axis=1) for value in total]
        lasts = [
            jnp.sum(jnp.where(lane == mics * slot + sub, line, 0.0), axis=1, keepdims=True)
            for slot in range(extra)
        ]
        whole = []
        for slot in range(planes):
            tile = slot // per_tile
            plane = turned(total[tile], -(slot % per_tile) * width)
            k, place = slot // mics, slot % mics
            d = (place + 1) // 2
            if place == 0 or (place % 2 == 1 and d < half):
                at_last = lasts[k * (half + 1) + d]
            elif d == half:
                at_last = jnp.where(low, lasts[k * (half + 1) + d], 0.0)
            else:
                at_last = jnp.zeros((mics, LANES), jnp.float32)
            whole.append(jnp.where(lane == width, at_last, plane))
        real, imag = solve(whole, mics, full, mic_ref[0])
        main = folded(jnp.where(lane < width, real, turned(imag, width)))
        rest = folded(jnp.where(lane < width, turned(real, -width), imag))
        sent = jnp.where(sub < upper, main, pltpu.roll(rest, upper, axis=0))
        packed[...] = sent
        gathered[me - base] = sent

    answers(lambda copy: copy.start())

    @pl.when(me < n - 1)
    def _():
        to_right.wait_send()

    @pl.when(me > 0)
    def _():
        to_left.wait_send()

    for to in range(solvers):

        @pl.when(me != base + to)
        def _():
            pltpu.make_async_copy(
                packed.at[: mics if to == 0 else upper],
                gathered.at[to, : mics if to == 0 else upper],
                recv_two.at[to],
            ).wait()

    def unfolded(value):
        return jnp.where(
            sub < upper, value, turned(pltpu.roll(value, upper, axis=0), -2 * width)
        )

    for block in range(tiles):
        joined = [jnp.zeros((mics, LANES), jnp.float32)] * 2
        for t in range(per_tile):
            value = unfolded(gathered[block * per_tile + t])
            for i in range(2):
                moved = turned(value, (t - i) * width)
                joined[i] = moved if t == 0 else jnp.where(lane // width == t, moved, joined[i])
        for i in range(2):
            beam[i, :, block * LANES : (block + 1) * LANES] = joined[i]
    rest = unfolded(pltpu.roll(gathered[0], mics - upper, axis=0))
    for i in range(2):
        at_last = jnp.sum(jnp.where(lane == i * width, rest, 0.0), axis=1, keepdims=True)
        beam[i, :, MAIN:] = jnp.broadcast_to(at_last, (mics, LANES))

    load_bank.wait()
    load_repeat.wait()
    stem(
        valid_ref[0],
        spec,
        bank,
        repeat,
        conv1_b,
        load_conv2,
        conv2_w,
        conv2_b,
        load_proj,
        proj_w,
        proj_b,
        out_ref,
        beam,
        power,
        spread,
        lined,
        kernel_one,
        patches,
        first,
    )
    for to in range(solvers):

        @pl.when(me != base + to)
        def _():
            parcel(to, 0).wait_send()
            note(to, 0).wait_send()

    answers(lambda copy: copy.wait_send())


def solve(planes, mics, full, ref):
    half = mics // 2
    for k in range(2):
        for m in range(mics):
            for d in range(half + 1):
                n = (m + d) % mics
                if d == half and m >= half:
                    continue

                def row(plane, at):
                    return planes[k * mics + plane][at : at + 1]

                if d == 0:
                    full[2 * k, m, m : m + 1, :] = row(0, m)
                    full[2 * k + 1, m, m : m + 1, :] = jnp.zeros((1, LANES), jnp.float32)
                    continue
                if d < half:
                    real, imag = row(2 * d - 1, m), row(2 * d, m)
                else:
                    real, imag = row(2 * d - 1, m), -row(2 * d - 1, m + half)
                full[2 * k, m, n : n + 1, :] = real
                full[2 * k + 1, m, n : n + 1, :] = imag
                full[2 * k, n, m : m + 1, :] = real
                full[2 * k + 1, n, m : m + 1, :] = -imag
    answer_re = [full[0, m] for m in range(mics)]
    answer_im = [full[1, m] for m in range(mics)]
    matrix_re = [full[2, m] for m in range(mics)]
    matrix_im = [full[3, m] for m in range(mics)]
    index = lax.broadcasted_iota(jnp.int32, (mics, LANES), 0)
    spread = matrix_re[0][0:1]
    for m in range(1, mics):
        spread = spread + matrix_re[m][m : m + 1]
    ridge = loading * spread / mics + epsilon
    matrix_re = [
        jnp.where(index == m, matrix_re[m] + ridge, matrix_re[m]) for m in range(mics)
    ]
    for p in range(mics):
        pivot_re, pivot_im = matrix_re[p][p : p + 1], matrix_im[p][p : p + 1]
        scale = 1.0 / (pivot_re * pivot_re + pivot_im * pivot_im)
        inverse_re, inverse_im = pivot_re * scale, -pivot_im * scale
        lead_re = matrix_re[p] * inverse_re - matrix_im[p] * inverse_im
        lead_im = matrix_re[p] * inverse_im + matrix_im[p] * inverse_re
        head_re = answer_re[p] * inverse_re - answer_im[p] * inverse_im
        head_im = answer_re[p] * inverse_im + answer_im[p] * inverse_re
        for m in range(mics):
            if m == p:
                continue
            column_re, column_im = matrix_re[m][p : p + 1], matrix_im[m][p : p + 1]
            matrix_re[m] = matrix_re[m] - (column_re * lead_re - column_im * lead_im)
            matrix_im[m] = matrix_im[m] - (column_re * lead_im + column_im * lead_re)
            answer_re[m] = answer_re[m] - (column_re * head_re - column_im * head_im)
            answer_im[m] = answer_im[m] - (column_re * head_im + column_im * head_re)
        matrix_re[p], matrix_im[p] = lead_re, lead_im
        answer_re[p], answer_im[p] = head_re, head_im
    trace = answer_re[0][0:1]
    for m in range(1, mics):
        trace = trace + answer_re[m][m : m + 1]
    scale = 1.0 / (trace + epsilon)
    picked = index == ref
    beam_re = jnp.zeros((mics, LANES), jnp.float32)
    beam_im = jnp.zeros((mics, LANES), jnp.float32)
    for m in range(mics):
        real = jnp.sum(jnp.where(picked, answer_re[m], 0.0), axis=0, keepdims=True)
        imag = jnp.sum(jnp.where(picked, answer_im[m], 0.0), axis=0, keepdims=True)
        beam_re = jnp.where(index == m, real * scale, beam_re)
        beam_im = jnp.where(index == m, imag * scale, beam_im)
    return beam_re, beam_im


def row_sums(values):
    count = len(values)
    sub = lax.broadcasted_iota(jnp.int32, values[0].shape, 0)
    step = count // 2
    while step:
        upper = sub // step % 2 == 1
        values = [
            jnp.where(
                upper,
                values[i + step] + pltpu.roll(values[i + step], step, axis=0),
                values[i] + pltpu.roll(values[i], count - step, axis=0),
            )
            for i in range(step)
        ]
        step //= 2
    return values[0]


def stem(
    valid,
    spec,
    bank,
    repeat,
    conv1_b,
    load_conv2,
    conv2_w,
    conv2_b,
    load_proj,
    proj_w,
    proj_b,
    out_ref,
    beam,
    power,
    spread,
    lined,
    kernel_one,
    patches,
    first,
):
    mics = beam.shape[1]
    quarter = out_ref.shape[0]
    groups = quarter + 1
    frames = quarter * GROUP
    stride = power.shape[0] // GROUP
    channels = conv2_w.shape[1]
    q_first = (MELS - 3) // 2 + 1
    q_second = (q_first - 3) // 2 + 1
    position = lax.axis_index("tm")
    for block in range(PADDED // LANES):
        lanes = pl.ds(block * LANES, LANES)
        beam_re = beam[0, :, lanes]
        beam_im = beam[1, :, lanes]

        def products(r, g):
            at = slice((r * groups + g) * mics, (r * groups + g + 1) * mics)
            if block < MAIN // LANES:
                re = spec[at, lanes]
                im = spec[at, pl.ds(MAIN + block * LANES, LANES)]
                return beam_re * re + beam_im * im, beam_re * im - beam_im * re
            re = spec[at, pl.ds(2 * MAIN, LANES)]
            return beam_re * re, -beam_im * re

        for r in range(GROUP):
            for g in range(0, groups - mics + 1, mics):
                pairs = [products(r, g + i) for i in range(mics)]
                real = row_sums([pair[0] for pair in pairs])
                imag = row_sums([pair[1] for pair in pairs])
                at = r * stride + g
                power[at : at + mics, lanes] = real * real + imag * imag
            for g in range(groups - groups % mics, groups):
                real, imag = products(r, g)
                real = jnp.sum(real, axis=0, keepdims=True)
                imag = jnp.sum(imag, axis=0, keepdims=True)
                at = r * stride + g
                power[at : at + 1, lanes] = real * real + imag * imag

    melspec = (
        jnp.dot(
            power[:, :MAIN],
            bank[:MAIN, :],
            preferred_element_type=jnp.float32,
            precision=lax.Precision.HIGHEST,
        )
        + power[:, MAIN:] * bank[MAIN : MAIN + 1, :]
    )
    row = lax.broadcasted_iota(jnp.int32, melspec.shape, 0)
    frame = position * frames + (row % stride - 1) * GROUP + row // stride
    alive = (frame >= 0) & (frame < valid)
    logmel = jnp.where(alive, jnp.log(melspec + epsilon), 0.0).astype(jnp.bfloat16)
    spread[...] = jnp.dot(logmel, repeat[...], preferred_element_type=jnp.float32)
    width = spread.shape[1]
    phase = lax.broadcasted_iota(jnp.int32, (quarter, width), 1) % 8
    mixed = jnp.zeros((quarter, width), jnp.float32)
    for u in range(7):
        start = (u + 1) % GROUP * stride + (u + 1) // GROUP
        mixed = jnp.where(phase == u, spread[start : start + quarter, :], mixed)
    lined[:, :width] = mixed
    order = list(range(0, q_first, 2)) + list(range(1, q_first, 2))
    for place, q in enumerate(order):
        base = 16 * q // LANES * LANES
        shift = 16 * q - base
        two = lined[:, base : base + 2 * LANES]
        if shift:
            two = pltpu.roll(two, 2 * LANES - shift, axis=1)
        patches[place * quarter : (place + 1) * quarter, :] = two[:, :LANES].astype(jnp.bfloat16)

    kernel_bf = kernel_one[...].astype(jnp.bfloat16)
    for late in range(3):
        lanes = slice(late * channels, (late + 1) * channels)
        one = jnp.dot(patches[...], kernel_bf[:, lanes], preferred_element_type=jnp.float32)
        one = jnp.maximum(one + conv1_b[...], 0.0)
        if late == 0:
            step = lax.broadcasted_iota(jnp.int32, one.shape, 0) % quarter
            one = jnp.where((step == 0) & (position == 0), 0.0, one)
        first[:, lanes] = one.astype(jnp.bfloat16)

    load_conv2.wait()
    evens = (q_first + 1) // 2
    summed = jnp.zeros((q_second * quarter, channels), jnp.float32)
    for b in range(3):
        start = {0: 0, 1: evens, 2: 1}[b] * quarter
        for late in range(3):
            summed = summed + jnp.dot(
                first[start : start + q_second * quarter, late * channels : (late + 1) * channels],
                conv2_w[3 * late + b],
                preferred_element_type=jnp.float32,
            )
    second = jnp.maximum(summed + conv2_b[...], 0.0).astype(jnp.bfloat16)
    load_proj.wait()
    out = jnp.zeros((quarter, out_ref.shape[1]), jnp.float32)
    for r in range(q_second):
        out = out + jnp.dot(
            second[r * quarter : (r + 1) * quarter],
            proj_w[r * channels : (r + 1) * channels, :],
            preferred_element_type=jnp.float32,
        )
    out_row = lax.broadcasted_iota(jnp.int32, out.shape, 0) + position * quarter
    out = jnp.where(GROUP * out_row < valid, out + proj_b[...], 0.0)
    out_ref[...] = out


def per_device(
    n, waveform, masks, valid, ref_mic, conv1_w, conv1_b, conv2_w, conv2_b, proj_w, proj_b
):
    mics, own = waveform.shape
    rows, frames = masks.shape[0], masks.shape[1]
    groups = frames // GROUP + 1
    quarter = frames // GROUP
    channels = conv1_w.shape[1]
    model = proj_w.shape[1]
    reach = WINDOW - SPAN
    vmem = pl.BlockSpec(memory_space=pltpu.VMEM)
    smem = pl.BlockSpec(memory_space=pltpu.SMEM)
    anywhere = pl.BlockSpec(memory_space=pltpu.HBM)
    planes = rows * mics
    solvers = min(SOLVERS, n)
    deep = -(-planes * (MAIN // solvers) // LANES)
    tall = deep * mics
    stride = -(-groups // 8) * 8
    q_first = (MELS - 3) // 2 + 1
    q_count = q_first * quarter
    features = pl.pallas_call(
        functools.partial(kernel, n),
        out_shape=jax.ShapeDtypeStruct((quarter, model), jnp.float32),
        in_specs=[smem] * 2 + [anywhere] * 5 + [anywhere, anywhere, anywhere, anywhere, anywhere, anywhere],
        out_specs=vmem,
        scratch_shapes=[
            pltpu.VMEM(conv1_w.shape, conv1_w.dtype),
            pltpu.VMEM((1, channels), jnp.float32),
            pltpu.VMEM((1, channels), jnp.float32),
            pltpu.VMEM((1, model), jnp.float32),
            pltpu.VMEM(waveform.shape, waveform.dtype),
            pltpu.VMEM(masks.shape, masks.dtype),
            pltpu.VMEM((NFFT, SPECTRUM), jnp.bfloat16),
            pltpu.VMEM((mics, SPAN + own + reach), jnp.float32),
            pltpu.VMEM((rows, frames, PADDED), jnp.float32),
            pltpu.VMEM((GROUP * groups * mics, SPECTRUM), jnp.float32),
            pltpu.VMEM((mics, SPAN), waveform.dtype),
            pltpu.VMEM((mics, reach), waveform.dtype),
            pltpu.VMEM((PADDED // LANES, planes, mics, LANES), jnp.float32),
            pltpu.VMEM((solvers, tall, LANES), jnp.int16),
            pltpu.VMEM((solvers, rows + 1, LANES), jnp.float32),
            pltpu.VMEM((n, tall, LANES), jnp.int16),
            pltpu.VMEM((n, rows + 1, LANES), jnp.float32),
            pltpu.VMEM((mics, LANES), jnp.float32),
            pltpu.VMEM((solvers, mics, LANES), jnp.float32),
            pltpu.VMEM((4, mics, mics, LANES), jnp.float32),
            pltpu.VMEM((PADDED, LANES), jnp.float32),
            pltpu.VMEM((LANES, MELS * 8), jnp.bfloat16),
            pltpu.VMEM(conv2_w.shape, jnp.bfloat16),
            pltpu.VMEM(proj_w.shape, jnp.bfloat16),
            pltpu.VMEM((2, mics, PADDED), jnp.float32),
            pltpu.VMEM((GROUP * stride, PADDED), jnp.float32),
            pltpu.VMEM((GROUP * stride, MELS * 8), jnp.float32),
            pltpu.VMEM((quarter, MELS * 8 + LANES), jnp.float32),
            pltpu.VMEM((LANES, 3 * channels), jnp.float32),
            pltpu.VMEM((q_count, LANES), jnp.bfloat16),
            pltpu.VMEM((q_count, 3 * channels), jnp.bfloat16),
            pltpu.SemaphoreType.DMA((2,)),
            pltpu.SemaphoreType.DMA((2,)),
            pltpu.SemaphoreType.DMA((n,)),
            pltpu.SemaphoreType.DMA((n,)),
            pltpu.SemaphoreType.DMA((n,)),
            pltpu.SemaphoreType.DMA((n,)),
            pltpu.SemaphoreType.DMA((n,)),
            pltpu.SemaphoreType.DMA((n,)),
            pltpu.SemaphoreType.DMA((11,)),
        ],
        compiler_params=pltpu.CompilerParams(
            collective_id=0, has_side_effects=True, vmem_limit_bytes=16 << 20
        ),
    )(
        valid,
        ref_mic,
        *(
            pltpu.with_memory_space_constraint(held, pltpu.HBM)
            for held in (
                waveform,
                masks,
                jnp.asarray(dft_table()),
                jnp.asarray(mel_bank()),
                jnp.asarray(repeat_table()),
                conv1_w,
                conv1_b[None],
                conv2_w,
                conv2_b[None],
                proj_w,
                proj_b[None],
            )
        ),
    )
    return features.astype(jnp.bfloat16)[None]


def solution(mesh):
    return jax.shard_map(
        functools.partial(per_device, mesh.shape["tm"]),
        mesh=mesh,
        in_specs=(
            P(None, ("meet", "tm")),
            P(None, ("meet", "tm"), None),
            P("meet"),
            P("meet"),
            P(),
            P(),
            P(),
            P(),
            P(),
            P(),
        ),
        out_specs=P(None, ("meet", "tm"), None),
        check_vma=False,
    )
```

```python
import functools
import math

import jax
import jax.numpy as jnp
import numpy as np
from jax import lax
from jax.experimental import pallas as pl
from jax.experimental.pallas import tpu as pltpu
from jax.sharding import PartitionSpec as P

NFFT = 512
HOP = 160
MELS = 80
BINS = NFFT // 2 + 1
LANES = 128
MAIN = BINS - 1
PADDED = MAIN + LANES
SPECTRUM = 2 * MAIN + LANES
GROUP = 4
SPAN = GROUP * HOP
WINDOW = 1024
SOLVERS = 8
LEVEL = 32000.0
TINY = 1e-30

loading = 0.03
epsilon = 1e-06
sample_rate = 16000.0


def dft_table():
    sample_pos = np.arange(NFFT)
    phase = (sample_pos[:, None] * np.arange(BINS)[None, :] % NFFT).astype(np.float32)
    phase = phase * np.float32(2.0 * math.pi / NFFT)
    ramp = sample_pos.astype(np.float32) * np.float32(2.0 * math.pi / NFFT)
    window = np.float32(0.5) - np.float32(0.5) * np.cos(ramp)
    cosines = window[:, None] * np.cos(phase)
    sines = -window[:, None] * np.sin(phase)
    table = np.zeros((NFFT, SPECTRUM), np.float32)
    table[:, :MAIN] = cosines[:, :MAIN]
    table[:, MAIN : 2 * MAIN] = sines[:, :MAIN]
    table[:, 2 * MAIN :] = cosines[:, MAIN:]
    return table.astype(jnp.bfloat16)


def mel_bank():
    mel_top = 2595.0 * math.log10(1.0 + sample_rate / 2.0 / 700.0)
    points = np.arange(MELS + 2) * (mel_top / (MELS + 1))
    edges_hz = 700.0 * (np.power(10.0, points / 2595.0) - 1.0)
    freq_hz = np.arange(BINS) * (sample_rate / 2.0 / (BINS - 1))
    lower, centre, upper = edges_hz[:-2], edges_hz[1:-1], edges_hz[2:]
    rising = (freq_hz[:, None] - lower[None, :]) / (centre - lower)[None, :]
    falling = (upper[None, :] - freq_hz[:, None]) / (upper - centre)[None, :]
    bank = np.zeros((PADDED, LANES), np.float32)
    bank[:BINS, :MELS] = np.maximum(np.minimum(rising, falling), 0.0)
    return bank


def repeat_table():
    table = np.zeros((LANES, MELS * 8), np.float32)
    for mel in range(MELS):
        table[mel, mel * 8 : mel * 8 + 8] = 1.0
    return table.astype(jnp.bfloat16)


def kernel(
    n,
    valid_ref,
    mic_ref,
    wave_hbm,
    masks_hbm,
    table_hbm,
    bank_hbm,
    repeat_hbm,
    conv1_w_hbm,
    conv1_b_hbm,
    conv2_hbm,
    conv2_b_hbm,
    proj_hbm,
    proj_b_hbm,
    out_ref,
    conv1_w,
    conv1_b,
    conv2_b,
    proj_b,
    wave,
    masks,
    table,
    ext,
    weight,
    spec,
    left,
    right,
    cov,
    part,
    notes,
    landed,
    noted,
    packed,
    gathered,
    full,
    bank,
    repeat,
    conv2_w,
    proj_w,
    beam,
    power,
    spread,
    lined,
    kernel_one,
    patches,
    first,
    nearby_send,
    nearby_recv,
    send_one,
    recv_one,
    send_note,
    recv_note,
    send_two,
    recv_two,
    loads,
):
    rows, frames = masks.shape[0], masks.shape[1]
    mics, own = wave.shape
    groups = frames // GROUP + 1
    reach = right.shape[1]
    me = lax.axis_index("tm")
    solvers = part.shape[0]
    base = (n - solvers) // 2
    solving = (me >= base) & (me < base + solvers)
    load_wave = pltpu.make_async_copy(wave_hbm, wave, loads.at[0])
    load_table = pltpu.make_async_copy(table_hbm, table, loads.at[1])
    load_masks = pltpu.make_async_copy(masks_hbm, masks, loads.at[2])
    load_wave.start()
    load_table.start()
    load_masks.start()
    load_conv2 = pltpu.make_async_copy(conv2_hbm, conv2_w, loads.at[3])
    load_proj = pltpu.make_async_copy(proj_hbm, proj_w, loads.at[4])
    load_bank = pltpu.make_async_copy(bank_hbm, bank, loads.at[5])
    load_repeat = pltpu.make_async_copy(repeat_hbm, repeat, loads.at[6])
    barrier = pltpu.get_barrier_semaphore()

    def greet(to):
        pl.semaphore_signal(
            barrier,
            inc=1,
            device_id={"tm": to},
            device_id_type=pl.DeviceIdType.MESH,
        )

    @pl.when(solving)
    def _():
        for j in (1, n - 1, *range(2, n - 1)):
            greet(lax.rem(me + j, n))

    @pl.when((me > 0) & jnp.logical_not(solving))
    def _():
        greet(me - 1)

    @pl.when((me < n - 1) & jnp.logical_not(solving))
    def _():
        greet(me + 1)

    def counted(here):
        return jnp.where(here, 1, 0).astype(jnp.int32)

    greeted = (
        solvers
        - counted(solving)
        + counted((me > 0) & ((me - 1 < base) | (me - 1 >= base + solvers)))
        + counted((me < n - 1) & ((me + 1 < base) | (me + 1 >= base + solvers)))
    )
    to_right = pltpu.make_async_remote_copy(
        src_ref=wave.at[:, own - SPAN :],
        dst_ref=left,
        send_sem=nearby_send.at[0],
        recv_sem=nearby_recv.at[0],
        device_id={"tm": lax.rem(me + 1, n)},
        device_id_type=pl.DeviceIdType.MESH,
    )
    to_left = pltpu.make_async_remote_copy(
        src_ref=wave.at[:, :reach],
        dst_ref=right,
        send_sem=nearby_send.at[1],
        recv_sem=nearby_recv.at[1],
        device_id={"tm": lax.rem(me + n - 1, n)},
        device_id_type=pl.DeviceIdType.MESH,
    )

    def meet():
        pl.semaphore_wait(barrier, greeted)

        @pl.when(me > 0)
        def _():
            to_left.start()

        @pl.when(me < n - 1)
        def _():
            to_right.start()

    late = (me >= n // 2) & (lax.rem(me, 4) >= 2)
    load_wave.wait()

    @pl.when(late)
    def _():
        meet()

    def transform(chosen):
        spans = jnp.concatenate(
            [ext[:, g * SPAN : g * SPAN + WINDOW] for g in chosen], axis=0
        )
        framed = jnp.concatenate(
            [
                (spans if r == 0 else pltpu.roll(spans, WINDOW - r * HOP, axis=1))[:, :NFFT]
                for r in range(GROUP)
            ],
            axis=0,
        ).astype(jnp.bfloat16)
        return jnp.dot(framed, table[...], preferred_element_type=jnp.float32)

    ext[:, SPAN : SPAN + own] = wave[...].astype(jnp.float32)
    load_table.wait()
    inner = list(range(1, groups - 1))
    found = transform(inner)
    width = len(inner) * mics
    for r in range(GROUP):
        spec[(r * groups + 1) * mics : (r * groups + 1) * mics + width, :] = found[
            r * width : (r + 1) * width
        ]

    @pl.when(jnp.logical_not(late) & (me >= base))
    def _():
        meet()

    small = [
        pltpu.make_async_copy(source, held, loads.at[7 + i])
        for i, (source, held) in enumerate(
            (
                (conv1_w_hbm, conv1_w),
                (conv1_b_hbm, conv1_b),
                (conv2_b_hbm, conv2_b),
                (proj_b_hbm, proj_b),
            )
        )
    ]
    for load in small:
        load.start()
    load_bank.start()
    load_repeat.start()
    load_conv2.start()
    load_proj.start()

    load_masks.wait()
    limit = valid_ref[0] - me * frames
    alive = lax.broadcasted_iota(jnp.int32, (frames, MAIN), 0) < limit
    for k in range(rows):
        level = masks[k].astype(jnp.float32) * (1.0 / 255.0)
        weight[k, :, :MAIN] = jnp.where(alive, level[:, :MAIN], 0.0)
        weight[k, :, MAIN:] = jnp.where(
            alive[:, :LANES], jnp.broadcast_to(level[:, MAIN:], (frames, LANES)), 0.0
        )

    half = mics // 2
    low = lax.broadcasted_iota(jnp.int32, (mics, LANES), 0) < half

    def frames_of(h):
        first_row = h * 2 * GROUP
        if not isinstance(h, int):
            first_row = pl.multiple_of(first_row, 2 * GROUP)
        places = []
        for i in range(2 * GROUP):
            at = ((i % GROUP) * groups + 1 + 2 * h + i // GROUP) * mics
            if not isinstance(h, int):
                at = pl.multiple_of(at, mics)
            places.append(pl.ds(at, mics))
        return pl.ds(first_row, 2 * GROUP), places

    def add_block(h, totals, block):
        totals = list(totals)
        lanes = pl.ds(block * LANES, LANES)
        lanes_im = pl.ds(MAIN + block * LANES, LANES)
        span, places = frames_of(h)
        held = [weight[k, span, lanes] for k in range(rows)]
        for i, at in enumerate(places):
            re = spec[at, lanes]
            im = spec[at, lanes_im]
            w = [held[k][i : i + 1] for k in range(rows)]
            place = 0
            for d in range(half + 1):
                if d == 0:
                    products = [re * re + im * im]
                else:
                    re_n = pltpu.roll(re, mics - d, axis=0)
                    im_n = pltpu.roll(im, mics - d, axis=0)
                    real = re * re_n + im * im_n
                    imag = im * re_n - re * im_n
                    products = [real, imag] if d < half else [jnp.where(low, real, imag)]
                for product in products:
                    for k in range(rows):
                        slot = k * mics + place
                        totals[slot] = totals[slot] + w[k] * product
                    place += 1
        return tuple(totals)

    def add_last_bin(h, totals):
        totals = list(totals)
        span, places = frames_of(h)
        held = [weight[k, span, pl.ds(MAIN, LANES)] for k in range(rows)]
        for i, at in enumerate(places):
            re = spec[at, pl.ds(2 * MAIN, LANES)]
            for d in range(half + 1):
                product = re * (re if d == 0 else pltpu.roll(re, mics - d, axis=0))
                for k in range(rows):
                    slot = k * (half + 1) + d
                    totals[slot] = totals[slot] + held[k][i : i + 1] * product
        return tuple(totals)

    blocks = frames // (2 * GROUP)
    tiles = MAIN // LANES
    planes = rows * mics
    extra = rows * (half + 1)
    adders = [functools.partial(add_block, block=block) for block in range(tiles)]
    adders.append(add_last_bin)
    counts = [planes] * tiles + [extra]
    for block in range(tiles + 1):
        zeros = tuple(jnp.zeros((mics, LANES), jnp.float32) for _ in range(counts[block]))
        totals = lax.fori_loop(0, blocks - 1, adders[block], zeros)
        for slot in range(counts[block]):
            cov[block, slot] = totals[slot]

    @pl.when(me < base)
    def _():
        meet()

    @pl.when(me < n - 1)
    def _():
        to_left.wait_recv()
        ext[:, SPAN + own :] = right[...].astype(jnp.float32)

    @pl.when(me == n - 1)
    def _():
        ext[:, SPAN + own :] = jnp.zeros((mics, reach), jnp.float32)

    def transform_edge(g):
        found = transform([g])
        for r in range(GROUP):
            spec[(r * groups + g) * mics : (r * groups + g + 1) * mics, :] = found[
                r * mics : (r + 1) * mics
            ]

    transform_edge(groups - 1)
    lane = lax.broadcasted_iota(jnp.int32, (mics, LANES), 1)
    sub = lax.broadcasted_iota(jnp.int32, (mics, LANES), 0)
    width = MAIN // solvers
    per_tile = LANES // width
    deep = -(-planes // per_tile)

    def turned(value, amount):
        amount = amount % LANES
        return pltpu.roll(value, amount, axis=1) if amount else value

    totals = add_last_bin(blocks - 1, tuple(cov[tiles, slot] for slot in range(extra)))
    line = jnp.zeros((mics, LANES), jnp.float32)
    for slot in range(extra):
        line = jnp.where(lane == mics * slot + sub, totals[slot], line)
    line = jnp.sum(line, axis=0, keepdims=True)
    for to in range(solvers):
        notes[to, rows : rows + 1, :] = line
    group = lane // width

    def packed_for(to, values):
        packing = values[0]
        for i in range(1, per_tile):
            packing = jnp.where(group == (to + i) % per_tile, values[i], packing)
        return packing

    for block in range(tiles):
        totals = adders[block](blocks - 1, tuple(cov[block, slot] for slot in range(planes)))
        turns = []
        for k in range(rows):
            peak = jnp.maximum(jnp.max(totals[k * mics], axis=0, keepdims=True), TINY)
            peak = jnp.broadcast_to(peak, (mics, LANES))
            turns.append([turned(peak * (1.0 / LEVEL), i * width) for i in range(per_tile)])
            scale = LEVEL / peak
            for slot in range(k * mics, (k + 1) * mics):
                cov[block, slot] = turned(totals[slot] * scale, slot % per_tile * width)
        for to in range(block * per_tile, (block + 1) * per_tile):
            for k in range(rows):
                notes[to, k : k + 1, :] = packed_for(to, turns[k])[:1]
            for tile in range(deep):
                values = [cov[block, tile * per_tile + i] for i in range(per_tile)]
                whole = jnp.round(packed_for(to, values)).astype(jnp.int32)
                part[to, tile * mics : (tile + 1) * mics, :] = whole.astype(jnp.int16)

    def parcel(to, offset):
        return pltpu.make_async_remote_copy(
            src_ref=part.at[to],
            dst_ref=landed.at[offset],
            send_sem=send_one.at[to],
            recv_sem=recv_one.at[offset],
            device_id={"tm": base + to},
            device_id_type=pl.DeviceIdType.MESH,
        )

    def note(to, offset):
        return pltpu.make_async_remote_copy(
            src_ref=notes.at[to],
            dst_ref=noted.at[offset],
            send_sem=send_note.at[to],
            recv_sem=recv_note.at[offset],
            device_id={"tm": base + to},
            device_id_type=pl.DeviceIdType.MESH,
        )

    for turn in range(solvers):
        to = jnp.where(me < n // 2, solvers - 1 - turn, turn)

        @pl.when(me != base + to)
        def _():
            offset = lax.rem(base + to + n - me, n)
            parcel(to, offset).start()
            note(to, offset).start()

    @pl.when(me > 0)
    def _():
        to_right.wait_recv()
        ext[:, :SPAN] = left[...].astype(jnp.float32)

    @pl.when(me == 0)
    def _():
        ext[:, :SPAN] = jnp.zeros((mics, SPAN), jnp.float32)

    transform_edge(0)
    for load in small:
        load.wait()
    channels = conv1_w.shape[1]
    kernel_one[...] = jnp.zeros_like(kernel_one)
    for a in range(3):
        for b in range(3):
            tap = conv1_w[3 * a + b : 3 * a + b + 1, :].astype(jnp.float32)
            for late in range(3):
                at = b * 8 + 2 * late + a
                kernel_one[at : at + 1, late * channels : (late + 1) * channels] = tap
    power[...] = jnp.zeros_like(power)
    lined[...] = jnp.zeros_like(lined)

    upper = mics // 2

    def folded(value):
        return jnp.where(
            lane < 2 * width,
            value,
            turned(pltpu.roll(value, mics - upper, axis=0), 2 * width),
        )

    def answer(offset, to, tall):
        return pltpu.make_async_remote_copy(
            src_ref=packed.at[:tall],
            dst_ref=gathered.at[me - base, :tall],
            send_sem=send_two.at[offset],
            recv_sem=recv_two.at[me - base],
            device_id={"tm": to},
            device_id_type=pl.DeviceIdType.MESH,
        )

    def answers(act):
        @pl.when(me == base)
        def _():
            for j in range(1, n):
                act(answer(j, lax.rem(me + j, n), mics))

        @pl.when(solving & (me != base))
        def _():
            for j in range(1, n):
                act(answer(j, lax.rem(me + j, n), upper))

    @pl.when(solving)
    def _():
        def levels(codes, held):
            codes = codes.astype(jnp.int32).astype(jnp.float32)
            return [
                codes[tile * mics : (tile + 1) * mics]
                * held[tile * per_tile // mics : tile * per_tile // mics + 1]
                for tile in range(deep)
            ]

        total = levels(part[me - base], notes[me - base])
        line = notes[me - base, rows : rows + 1]
        for j in range(1, n):
            parcel(0, j).wait_recv()
            note(0, j).wait_recv()
            total = [a + b for a, b in zip(total, levels(landed[j], noted[j]))]
            line = line + noted[j, rows : rows + 1]
        back = lax.rem(per_tile - lax.rem(me - base, per_tile), per_tile) * width
        total = [pltpu.roll(value, back, axis=1) for value in total]
        lasts = [
            jnp.sum(jnp.where(lane == mics * slot + sub, line, 0.0), axis=1, keepdims=True)
            for slot in range(extra)
        ]
        whole = []
        for slot in range(planes):
            tile = slot // per_tile
            plane = turned(total[tile], -(slot % per_tile) * width)
            k, place = slot // mics, slot % mics
            d = (place + 1) // 2
            if place == 0 or (place % 2 == 1 and d < half):
                at_last = lasts[k * (half + 1) + d]
            elif d == half:
                at_last = jnp.where(low, lasts[k * (half + 1) + d], 0.0)
            else:
                at_last = jnp.zeros((mics, LANES), jnp.float32)
            whole.append(jnp.where(lane == width, at_last, plane))
        real, imag = solve(whole, mics, full, mic_ref[0])
        main = folded(jnp.where(lane < width, real, turned(imag, width)))
        rest = folded(jnp.where(lane < width, turned(real, -width), imag))
        sent = jnp.where(sub < upper, main, pltpu.roll(rest, upper, axis=0))
        packed[...] = sent
        gathered[me - base] = sent

    answers(lambda copy: copy.start())

    @pl.when(me < n - 1)
    def _():
        to_right.wait_send()

    @pl.when(me > 0)
    def _():
        to_left.wait_send()

    for to in range(solvers):

        @pl.when(me != base + to)
        def _():
            pltpu.make_async_copy(
                packed.at[: mics if to == 0 else upper],
                gathered.at[to, : mics if to == 0 else upper],
                recv_two.at[to],
            ).wait()

    def unfolded(value):
        return jnp.where(
            sub < upper, value, turned(pltpu.roll(value, upper, axis=0), -2 * width)
        )

    for block in range(tiles):
        joined = [jnp.zeros((mics, LANES), jnp.float32)] * 2
        for t in range(per_tile):
            value = unfolded(gathered[block * per_tile + t])
            for i in range(2):
                moved = turned(value, (t - i) * width)
                joined[i] = moved if t == 0 else jnp.where(lane // width == t, moved, joined[i])
        for i in range(2):
            beam[i, :, block * LANES : (block + 1) * LANES] = joined[i]
    rest = unfolded(pltpu.roll(gathered[0], mics - upper, axis=0))
    for i in range(2):
        at_last = jnp.sum(jnp.where(lane == i * width, rest, 0.0), axis=1, keepdims=True)
        beam[i, :, MAIN:] = jnp.broadcast_to(at_last, (mics, LANES))

    load_bank.wait()
    load_repeat.wait()
    stem(
        valid_ref[0],
        spec,
        bank,
        repeat,
        conv1_b,
        load_conv2,
        conv2_w,
        conv2_b,
        load_proj,
        proj_w,
        proj_b,
        out_ref,
        beam,
        power,
        spread,
        lined,
        kernel_one,
        patches,
        first,
    )
    for to in range(solvers):

        @pl.when(me != base + to)
        def _():
            parcel(to, 0).wait_send()
            note(to, 0).wait_send()

    answers(lambda copy: copy.wait_send())


def solve(planes, mics, full, ref):
    half = mics // 2
    for k in range(2):
        for m in range(mics):
            for d in range(half + 1):
                n = (m + d) % mics
                if d == half and m >= half:
                    continue

                def row(plane, at):
                    return planes[k * mics + plane][at : at + 1]

                if d == 0:
                    full[2 * k, m, m : m + 1, :] = row(0, m)
                    full[2 * k + 1, m, m : m + 1, :] = jnp.zeros((1, LANES), jnp.float32)
                    continue
                if d < half:
                    real, imag = row(2 * d - 1, m), row(2 * d, m)
                else:
                    real, imag = row(2 * d - 1, m), -row(2 * d - 1, m + half)
                full[2 * k, m, n : n + 1, :] = real
                full[2 * k + 1, m, n : n + 1, :] = imag
                full[2 * k, n, m : m + 1, :] = real
                full[2 * k + 1, n, m : m + 1, :] = -imag
    answer_re = [full[0, m] for m in range(mics)]
    answer_im = [full[1, m] for m in range(mics)]
    matrix_re = [full[2, m] for m in range(mics)]
    matrix_im = [full[3, m] for m in range(mics)]
    index = lax.broadcasted_iota(jnp.int32, (mics, LANES), 0)
    spread = matrix_re[0][0:1]
    for m in range(1, mics):
        spread = spread + matrix_re[m][m : m + 1]
    ridge = loading * spread / mics + epsilon
    matrix_re = [
        jnp.where(index == m, matrix_re[m] + ridge, matrix_re[m]) for m in range(mics)
    ]
    for p in range(mics):
        pivot_re, pivot_im = matrix_re[p][p : p + 1], matrix_im[p][p : p + 1]
        scale = 1.0 / (pivot_re * pivot_re + pivot_im * pivot_im)
        inverse_re, inverse_im = pivot_re * scale, -pivot_im * scale
        lead_re = matrix_re[p] * inverse_re - matrix_im[p] * inverse_im
        lead_im = matrix_re[p] * inverse_im + matrix_im[p] * inverse_re
        head_re = answer_re[p] * inverse_re - answer_im[p] * inverse_im
        head_im = answer_re[p] * inverse_im + answer_im[p] * inverse_re
        for m in range(mics):
            if m == p:
                continue
            column_re, column_im = matrix_re[m][p : p + 1], matrix_im[m][p : p + 1]
            matrix_re[m] = matrix_re[m] - (column_re * lead_re - column_im * lead_im)
            matrix_im[m] = matrix_im[m] - (column_re * lead_im + column_im * lead_re)
            answer_re[m] = answer_re[m] - (column_re * head_re - column_im * head_im)
            answer_im[m] = answer_im[m] - (column_re * head_im + column_im * head_re)
        matrix_re[p], matrix_im[p] = lead_re, lead_im
        answer_re[p], answer_im[p] = head_re, head_im
    trace = answer_re[0][0:1]
    for m in range(1, mics):
        trace = trace + answer_re[m][m : m + 1]
    scale = 1.0 / (trace + epsilon)
    picked = index == ref
    beam_re = jnp.zeros((mics, LANES), jnp.float32)
    beam_im = jnp.zeros((mics, LANES), jnp.float32)
    for m in range(mics):
        real = jnp.sum(jnp.where(picked, answer_re[m], 0.0), axis=0, keepdims=True)
        imag = jnp.sum(jnp.where(picked, answer_im[m], 0.0), axis=0, keepdims=True)
        beam_re = jnp.where(index == m, real * scale, beam_re)
        beam_im = jnp.where(index == m, imag * scale, beam_im)
    return beam_re, beam_im


def row_sums(values):
    count = len(values)
    sub = lax.broadcasted_iota(jnp.int32, values[0].shape, 0)
    step = count // 2
    while step:
        upper = sub // step % 2 == 1
        values = [
            jnp.where(
                upper,
                values[i + step] + pltpu.roll(values[i + step], step, axis=0),
                values[i] + pltpu.roll(values[i], count - step, axis=0),
            )
            for i in range(step)
        ]
        step //= 2
    return values[0]


def stem(
    valid,
    spec,
    bank,
    repeat,
    conv1_b,
    load_conv2,
    conv2_w,
    conv2_b,
    load_proj,
    proj_w,
    proj_b,
    out_ref,
    beam,
    power,
    spread,
    lined,
    kernel_one,
    patches,
    first,
):
    mics = beam.shape[1]
    quarter = out_ref.shape[0]
    groups = quarter + 1
    frames = quarter * GROUP
    stride = power.shape[0] // GROUP
    channels = conv2_w.shape[1]
    q_first = (MELS - 3) // 2 + 1
    q_second = (q_first - 3) // 2 + 1
    position = lax.axis_index("tm")
    for block in range(PADDED // LANES):
        lanes = pl.ds(block * LANES, LANES)
        beam_re = beam[0, :, lanes]
        beam_im = beam[1, :, lanes]

        def products(r, g):
            at = slice((r * groups + g) * mics, (r * groups + g + 1) * mics)
            if block < MAIN // LANES:
                re = spec[at, lanes]
                im = spec[at, pl.ds(MAIN + block * LANES, LANES)]
                return beam_re * re + beam_im * im, beam_re * im - beam_im * re
            re = spec[at, pl.ds(2 * MAIN, LANES)]
            return beam_re * re, -beam_im * re

        for r in range(GROUP):
            for g in range(0, groups - mics + 1, mics):
                pairs = [products(r, g + i) for i in range(mics)]
                real = row_sums([pair[0] for pair in pairs])
                imag = row_sums([pair[1] for pair in pairs])
                at = r * stride + g
                power[at : at + mics, lanes] = real * real + imag * imag
            for g in range(groups - groups % mics, groups):
                real, imag = products(r, g)
                real = jnp.sum(real, axis=0, keepdims=True)
                imag = jnp.sum(imag, axis=0, keepdims=True)
                at = r * stride + g
                power[at : at + 1, lanes] = real * real + imag * imag

    melspec = (
        jnp.dot(
            power[:, :MAIN],
            bank[:MAIN, :],
            preferred_element_type=jnp.float32,
            precision=lax.Precision.HIGHEST,
        )
        + power[:, MAIN:] * bank[MAIN : MAIN + 1, :]
    )
    row = lax.broadcasted_iota(jnp.int32, melspec.shape, 0)
    frame = position * frames + (row % stride - 1) * GROUP + row // stride
    alive = (frame >= 0) & (frame < valid)
    logmel = jnp.where(alive, jnp.log(melspec + epsilon), 0.0).astype(jnp.bfloat16)
    spread[...] = jnp.dot(logmel, repeat[...], preferred_element_type=jnp.float32)
    width = spread.shape[1]
    phase = lax.broadcasted_iota(jnp.int32, (quarter, width), 1) % 8
    mixed = jnp.zeros((quarter, width), jnp.float32)
    for u in range(7):
        start = (u + 1) % GROUP * stride + (u + 1) // GROUP
        mixed = jnp.where(phase == u, spread[start : start + quarter, :], mixed)
    lined[:, :width] = mixed
    order = list(range(0, q_first, 2)) + list(range(1, q_first, 2))
    for place, q in enumerate(order):
        base = 16 * q // LANES * LANES
        shift = 16 * q - base
        two = lined[:, base : base + 2 * LANES]
        if shift:
            two = pltpu.roll(two, 2 * LANES - shift, axis=1)
        patches[place * quarter : (place + 1) * quarter, :] = two[:, :LANES].astype(jnp.bfloat16)

    kernel_bf = kernel_one[...].astype(jnp.bfloat16)
    for late in range(3):
        lanes = slice(late * channels, (late + 1) * channels)
        one = jnp.dot(patches[...], kernel_bf[:, lanes], preferred_element_type=jnp.float32)
        one = jnp.maximum(one + conv1_b[...], 0.0)
        if late == 0:
            step = lax.broadcasted_iota(jnp.int32, one.shape, 0) % quarter
            one = jnp.where((step == 0) & (position == 0), 0.0, one)
        first[:, lanes] = one.astype(jnp.bfloat16)

    load_conv2.wait()
    evens = (q_first + 1) // 2
    summed = jnp.zeros((q_second * quarter, channels), jnp.float32)
    for b in range(3):
        start = {0: 0, 1: evens, 2: 1}[b] * quarter
        for late in range(3):
            summed = summed + jnp.dot(
                first[start : start + q_second * quarter, late * channels : (late + 1) * channels],
                conv2_w[3 * late + b],
                preferred_element_type=jnp.float32,
            )
    second = jnp.maximum(summed + conv2_b[...], 0.0).astype(jnp.bfloat16)
    load_proj.wait()
    out = jnp.zeros((quarter, out_ref.shape[1]), jnp.float32)
    for r in range(q_second):
        out = out + jnp.dot(
            second[r * quarter : (r + 1) * quarter],
            proj_w[r * channels : (r + 1) * channels, :],
            preferred_element_type=jnp.float32,
        )
    out_row = lax.broadcasted_iota(jnp.int32, out.shape, 0) + position * quarter
    out = jnp.where(GROUP * out_row < valid, out + proj_b[...], 0.0)
    out_ref[...] = out


def per_device(
    n, waveform, masks, valid, ref_mic, conv1_w, conv1_b, conv2_w, conv2_b, proj_w, proj_b
):
    mics, own = waveform.shape
    rows, frames = masks.shape[0], masks.shape[1]
    groups = frames // GROUP + 1
    quarter = frames // GROUP
    channels = conv1_w.shape[1]
    model = proj_w.shape[1]
    reach = WINDOW - SPAN
    vmem = pl.BlockSpec(memory_space=pltpu.VMEM)
    smem = pl.BlockSpec(memory_space=pltpu.SMEM)
    anywhere = pl.BlockSpec(memory_space=pltpu.HBM)
    planes = rows * mics
    solvers = min(SOLVERS, n)
    deep = -(-planes * (MAIN // solvers) // LANES)
    tall = deep * mics
    stride = -(-groups // 8) * 8
    q_first = (MELS - 3) // 2 + 1
    q_count = q_first * quarter
    features = pl.pallas_call(
        functools.partial(kernel, n),
        out_shape=jax.ShapeDtypeStruct((quarter, model), jnp.float32),
        in_specs=[smem] * 2 + [anywhere] * 5 + [anywhere, anywhere, anywhere, anywhere, anywhere, anywhere],
        out_specs=vmem,
        scratch_shapes=[
            pltpu.VMEM(conv1_w.shape, conv1_w.dtype),
            pltpu.VMEM((1, channels), jnp.float32),
            pltpu.VMEM((1, channels), jnp.float32),
            pltpu.VMEM((1, model), jnp.float32),
            pltpu.VMEM(waveform.shape, waveform.dtype),
            pltpu.VMEM(masks.shape, masks.dtype),
            pltpu.VMEM((NFFT, SPECTRUM), jnp.bfloat16),
            pltpu.VMEM((mics, SPAN + own + reach), jnp.float32),
            pltpu.VMEM((rows, frames, PADDED), jnp.float32),
            pltpu.VMEM((GROUP * groups * mics, SPECTRUM), jnp.float32),
            pltpu.VMEM((mics, SPAN), waveform.dtype),
            pltpu.VMEM((mics, reach), waveform.dtype),
            pltpu.VMEM((PADDED // LANES, planes, mics, LANES), jnp.float32),
            pltpu.VMEM((solvers, tall, LANES), jnp.int16),
            pltpu.VMEM((solvers, rows + 1, LANES), jnp.float32),
            pltpu.VMEM((n, tall, LANES), jnp.int16),
            pltpu.VMEM((n, rows + 1, LANES), jnp.float32),
            pltpu.VMEM((mics, LANES), jnp.float32),
            pltpu.VMEM((solvers, mics, LANES), jnp.float32),
            pltpu.VMEM((4, mics, mics, LANES), jnp.float32),
            pltpu.VMEM((PADDED, LANES), jnp.float32),
            pltpu.VMEM((LANES, MELS * 8), jnp.bfloat16),
            pltpu.VMEM(conv2_w.shape, jnp.bfloat16),
            pltpu.VMEM(proj_w.shape, jnp.bfloat16),
            pltpu.VMEM((2, mics, PADDED), jnp.float32),
            pltpu.VMEM((GROUP * stride, PADDED), jnp.float32),
            pltpu.VMEM((GROUP * stride, MELS * 8), jnp.float32),
            pltpu.VMEM((quarter, MELS * 8 + LANES), jnp.float32),
            pltpu.VMEM((LANES, 3 * channels), jnp.float32),
            pltpu.VMEM((q_count, LANES), jnp.bfloat16),
            pltpu.VMEM((q_count, 3 * channels), jnp.bfloat16),
            pltpu.SemaphoreType.DMA((2,)),
            pltpu.SemaphoreType.DMA((2,)),
            pltpu.SemaphoreType.DMA((n,)),
            pltpu.SemaphoreType.DMA((n,)),
            pltpu.SemaphoreType.DMA((n,)),
            pltpu.SemaphoreType.DMA((n,)),
            pltpu.SemaphoreType.DMA((n,)),
            pltpu.SemaphoreType.DMA((n,)),
            pltpu.SemaphoreType.DMA((11,)),
        ],
        compiler_params=pltpu.CompilerParams(
            collective_id=0, has_side_effects=True, vmem_limit_bytes=16 << 20
        ),
    )(
        valid,
        ref_mic,
        *(
            pltpu.with_memory_space_constraint(held, pltpu.HBM)
            for held in (
                waveform,
                masks,
                jnp.asarray(dft_table()),
                jnp.asarray(mel_bank()),
                jnp.asarray(repeat_table()),
                conv1_w,
                conv1_b[None],
                conv2_w,
                conv2_b[None],
                proj_w,
                proj_b[None],
            )
        ),
    )
    return features.astype(jnp.bfloat16)[None]


def solution(mesh):
    return jax.shard_map(
        functools.partial(per_device, mesh.shape["tm"]),
        mesh=mesh,
        in_specs=(
            P(None, ("meet", "tm")),
            P(None, ("meet", "tm"), None),
            P("meet"),
            P("meet"),
            P(),
            P(),
            P(),
            P(),
            P(),
            P(),
        ),
        out_specs=P(None, ("meet", "tm"), None),
        check_vma=False,
    )
```

```python
import functools
import math

import jax
import jax.numpy as jnp
import numpy as np
from jax import lax
from jax.experimental import pallas as pl
from jax.experimental.pallas import tpu as pltpu
from jax.sharding import PartitionSpec as P

NFFT = 512
HOP = 160
MELS = 80
BINS = NFFT // 2 + 1
LANES = 128
MAIN = BINS - 1
PADDED = MAIN + LANES
SPECTRUM = 2 * MAIN + LANES
GROUP = 4
SPAN = GROUP * HOP
WINDOW = 1024
SOLVERS = 8
LEVEL = 32000.0
TINY = 1e-30

loading = 0.03
epsilon = 1e-06
sample_rate = 16000.0


def dft_table():
    sample_pos = np.arange(NFFT)
    phase = (sample_pos[:, None] * np.arange(BINS)[None, :] % NFFT).astype(np.float32)
    phase = phase * np.float32(2.0 * math.pi / NFFT)
    ramp = sample_pos.astype(np.float32) * np.float32(2.0 * math.pi / NFFT)
    window = np.float32(0.5) - np.float32(0.5) * np.cos(ramp)
    cosines = window[:, None] * np.cos(phase)
    sines = -window[:, None] * np.sin(phase)
    table = np.zeros((NFFT, SPECTRUM), np.float32)
    table[:, :MAIN] = cosines[:, :MAIN]
    table[:, MAIN : 2 * MAIN] = sines[:, :MAIN]
    table[:, 2 * MAIN :] = cosines[:, MAIN:]
    return table.astype(jnp.bfloat16)


def mel_bank():
    mel_top = 2595.0 * math.log10(1.0 + sample_rate / 2.0 / 700.0)
    points = np.arange(MELS + 2) * (mel_top / (MELS + 1))
    edges_hz = 700.0 * (np.power(10.0, points / 2595.0) - 1.0)
    freq_hz = np.arange(BINS) * (sample_rate / 2.0 / (BINS - 1))
    lower, centre, upper = edges_hz[:-2], edges_hz[1:-1], edges_hz[2:]
    rising = (freq_hz[:, None] - lower[None, :]) / (centre - lower)[None, :]
    falling = (upper[None, :] - freq_hz[:, None]) / (upper - centre)[None, :]
    bank = np.zeros((PADDED, LANES), np.float32)
    bank[:BINS, :MELS] = np.maximum(np.minimum(rising, falling), 0.0)
    return bank


def repeat_table():
    table = np.zeros((LANES, MELS * 8), np.float32)
    for mel in range(MELS):
        table[mel, mel * 8 : mel * 8 + 8] = 1.0
    return table.astype(jnp.bfloat16)


def kernel(
    n,
    valid_ref,
    mic_ref,
    wave_hbm,
    masks_hbm,
    table_hbm,
    bank_hbm,
    repeat_hbm,
    conv1_w_hbm,
    conv1_b_hbm,
    conv2_hbm,
    conv2_b_hbm,
    proj_hbm,
    proj_b_hbm,
    out_ref,
    conv1_w,
    conv1_b,
    conv2_b,
    proj_b,
    wave,
    masks,
    table,
    ext,
    weight,
    spec,
    left,
    right,
    cov,
    part,
    notes,
    landed,
    noted,
    packed,
    gathered,
    full,
    bank,
    split,
    repeat,
    conv2_w,
    proj_w,
    beam,
    power,
    spread,
    lined,
    kernel_one,
    patches,
    first,
    nearby_send,
    nearby_recv,
    send_one,
    recv_one,
    send_note,
    recv_note,
    send_two,
    recv_two,
    loads,
    taps,
):
    rows, frames = masks.shape[0], masks.shape[1]
    mics, own = wave.shape
    groups = frames // GROUP + 1
    reach = right.shape[1]
    me = lax.axis_index("tm")
    solvers = part.shape[0]
    base = (n - solvers) // 2
    solving = (me >= base) & (me < base + solvers)
    load_wave = pltpu.make_async_copy(wave_hbm, wave, loads.at[0])
    load_table = pltpu.make_async_copy(table_hbm, table, loads.at[1])
    load_masks = pltpu.make_async_copy(masks_hbm, masks, loads.at[2])
    load_wave.start()
    load_table.start()
    load_masks.start()
    depth = conv2_hbm.shape[1]
    load_conv2 = [
        pltpu.make_async_copy(
            conv2_hbm.at[3 * late + b],
            conv2_w.at[b, late * depth : (late + 1) * depth],
            taps.at[3 * late + b],
        )
        for b in range(3)
        for late in range(3)
    ]
    load_proj = pltpu.make_async_copy(proj_hbm, proj_w, loads.at[4])
    load_bank = pltpu.make_async_copy(bank_hbm, bank, loads.at[5])
    load_repeat = pltpu.make_async_copy(repeat_hbm, repeat, loads.at[6])
    barrier = pltpu.get_barrier_semaphore()

    def greet(to):
        pl.semaphore_signal(
            barrier,
            inc=1,
            device_id={"tm": to},
            device_id_type=pl.DeviceIdType.MESH,
        )

    @pl.when(solving)
    def _():
        for j in (1, n - 1, *range(2, n - 1)):
            greet(lax.rem(me + j, n))

    @pl.when((me > 0) & jnp.logical_not(solving))
    def _():
        greet(me - 1)

    @pl.when((me < n - 1) & jnp.logical_not(solving))
    def _():
        greet(me + 1)

    def counted(here):
        return jnp.where(here, 1, 0).astype(jnp.int32)

    greeted = (
        solvers
        - counted(solving)
        + counted((me > 0) & ((me - 1 < base) | (me - 1 >= base + solvers)))
        + counted((me < n - 1) & ((me + 1 < base) | (me + 1 >= base + solvers)))
    )
    to_right = pltpu.make_async_remote_copy(
        src_ref=wave.at[:, own - SPAN :],
        dst_ref=left,
        send_sem=nearby_send.at[0],
        recv_sem=nearby_recv.at[0],
        device_id={"tm": lax.rem(me + 1, n)},
        device_id_type=pl.DeviceIdType.MESH,
    )
    to_left = pltpu.make_async_remote_copy(
        src_ref=wave.at[:, :reach],
        dst_ref=right,
        send_sem=nearby_send.at[1],
        recv_sem=nearby_recv.at[1],
        device_id={"tm": lax.rem(me + n - 1, n)},
        device_id_type=pl.DeviceIdType.MESH,
    )

    def meet():
        pl.semaphore_wait(barrier, greeted)

        @pl.when(me > 0)
        def _():
            to_left.start()

        @pl.when(me < n - 1)
        def _():
            to_right.start()

    late = (me >= n // 2) & (lax.rem(me, 4) >= 2)
    load_wave.wait()

    @pl.when(late)
    def _():
        meet()

    def transform(chosen):
        spans = jnp.concatenate(
            [ext[:, g * SPAN : g * SPAN + WINDOW] for g in chosen], axis=0
        )
        framed = jnp.concatenate(
            [
                (spans if r == 0 else pltpu.roll(spans, WINDOW - r * HOP, axis=1))[:, :NFFT]
                for r in range(GROUP)
            ],
            axis=0,
        ).astype(jnp.bfloat16)
        return jnp.dot(framed, table[...], preferred_element_type=jnp.float32)

    ext[:, SPAN : SPAN + own] = wave[...].astype(jnp.float32)
    load_table.wait()
    inner = list(range(1, groups - 1))
    found = transform(inner)
    width = len(inner) * mics
    for r in range(GROUP):
        spec[(r * groups + 1) * mics : (r * groups + 1) * mics + width, :] = found[
            r * width : (r + 1) * width
        ]

    @pl.when(jnp.logical_not(late) & (me >= base // 2))
    def _():
        meet()

    small = [
        pltpu.make_async_copy(source, held, loads.at[7 + i])
        for i, (source, held) in enumerate(
            (
                (conv1_w_hbm, conv1_w),
                (conv1_b_hbm, conv1_b),
                (conv2_b_hbm, conv2_b),
                (proj_b_hbm, proj_b),
            )
        )
    ]
    for load in small:
        load.start()
    load_bank.start()
    load_repeat.start()
    for load in load_conv2:
        load.start()
    load_proj.start()

    load_masks.wait()
    limit = valid_ref[0] - me * frames
    alive = lax.broadcasted_iota(jnp.int32, (frames, MAIN), 0) < limit
    for k in range(rows):
        level = masks[k].astype(jnp.float32) * (1.0 / 255.0)
        weight[k, :, :MAIN] = jnp.where(alive, level[:, :MAIN], 0.0)
        weight[k, :, MAIN:] = jnp.where(
            alive[:, :LANES], jnp.broadcast_to(level[:, MAIN:], (frames, LANES)), 0.0
        )

    half = mics // 2
    low = lax.broadcasted_iota(jnp.int32, (mics, LANES), 0) < half

    def frames_of(h):
        first_row = h * 2 * GROUP
        if not isinstance(h, int):
            first_row = pl.multiple_of(first_row, 2 * GROUP)
        places = []
        for i in range(2 * GROUP):
            at = ((i % GROUP) * groups + 1 + 2 * h + i // GROUP) * mics
            if not isinstance(h, int):
                at = pl.multiple_of(at, mics)
            places.append(pl.ds(at, mics))
        return pl.ds(first_row, 2 * GROUP), places

    def add_block(h, totals, block):
        totals = list(totals)
        lanes = pl.ds(block * LANES, LANES)
        lanes_im = pl.ds(MAIN + block * LANES, LANES)
        span, places = frames_of(h)
        held = [weight[k, span, lanes] for k in range(rows)]
        for i, at in enumerate(places):
            re = spec[at, lanes]
            im = spec[at, lanes_im]
            w = [held[k][i : i + 1] for k in range(rows)]
            place = 0
            for d in range(half + 1):
                if d == 0:
                    products = [re * re + im * im]
                else:
                    re_n = pltpu.roll(re, mics - d, axis=0)
                    im_n = pltpu.roll(im, mics - d, axis=0)
                    real = re * re_n + im * im_n
                    imag = im * re_n - re * im_n
                    products = [real, imag] if d < half else [jnp.where(low, real, imag)]
                for product in products:
                    for k in range(rows):
                        slot = k * mics + place
                        totals[slot] = totals[slot] + w[k] * product
                    place += 1
        return tuple(totals)

    def add_last_bin(h, totals):
        totals = list(totals)
        span, places = frames_of(h)
        held = [weight[k, span, pl.ds(MAIN, LANES)] for k in range(rows)]
        for i, at in enumerate(places):
            re = spec[at, pl.ds(2 * MAIN, LANES)]
            for d in range(half + 1):
                product = re * (re if d == 0 else pltpu.roll(re, mics - d, axis=0))
                for k in range(rows):
                    slot = k * (half + 1) + d
                    totals[slot] = totals[slot] + held[k][i : i + 1] * product
        return tuple(totals)

    blocks = frames // (2 * GROUP)
    tiles = MAIN // LANES
    planes = rows * mics
    extra = rows * (half + 1)
    adders = [functools.partial(add_block, block=block) for block in range(tiles)]
    adders.append(add_last_bin)
    counts = [planes] * tiles + [extra]
    for block in range(tiles + 1):
        zeros = tuple(jnp.zeros((mics, LANES), jnp.float32) for _ in range(counts[block]))
        totals = lax.fori_loop(0, blocks - 1, adders[block], zeros)
        for slot in range(counts[block]):
            cov[block, slot] = totals[slot]

    @pl.when(me < base // 2)
    def _():
        meet()

    @pl.when(me < n - 1)
    def _():
        to_left.wait_recv()
        ext[:, SPAN + own :] = right[...].astype(jnp.float32)

    @pl.when(me == n - 1)
    def _():
        ext[:, SPAN + own :] = jnp.zeros((mics, reach), jnp.float32)

    def transform_edge(g):
        found = transform([g])
        for r in range(GROUP):
            spec[(r * groups + g) * mics : (r * groups + g + 1) * mics, :] = found[
                r * mics : (r + 1) * mics
            ]

    transform_edge(groups - 1)
    lane = lax.broadcasted_iota(jnp.int32, (mics, LANES), 1)
    sub = lax.broadcasted_iota(jnp.int32, (mics, LANES), 0)
    width = MAIN // solvers
    per_tile = LANES // width
    deep = -(-planes // per_tile)

    def turned(value, amount):
        amount = amount % LANES
        return pltpu.roll(value, amount, axis=1) if amount else value

    totals = add_last_bin(blocks - 1, tuple(cov[tiles, slot] for slot in range(extra)))
    line = jnp.zeros((mics, LANES), jnp.float32)
    for slot in range(extra):
        line = jnp.where(lane == mics * slot + sub, totals[slot], line)
    line = jnp.sum(line, axis=0, keepdims=True)
    for to in range(solvers):
        notes[to, rows : rows + 1, :] = line
    group = lane // width

    def packed_for(to, values):
        packing = values[0]
        for i in range(1, per_tile):
            packing = jnp.where(group == (to + i) % per_tile, values[i], packing)
        return packing

    def parcel(to, offset):
        return pltpu.make_async_remote_copy(
            src_ref=part.at[to],
            dst_ref=landed.at[offset],
            send_sem=send_one.at[to],
            recv_sem=recv_one.at[offset],
            device_id={"tm": base + to},
            device_id_type=pl.DeviceIdType.MESH,
        )

    def note(to, offset):
        return pltpu.make_async_remote_copy(
            src_ref=notes.at[to],
            dst_ref=noted.at[offset],
            send_sem=send_note.at[to],
            recv_sem=recv_note.at[offset],
            device_id={"tm": base + to},
            device_id_type=pl.DeviceIdType.MESH,
        )

    for block in reversed(range(tiles)):
        totals = adders[block](blocks - 1, tuple(cov[block, slot] for slot in range(planes)))
        turns = []
        for k in range(rows):
            peak = jnp.maximum(jnp.max(totals[k * mics], axis=0, keepdims=True), TINY)
            peak = jnp.broadcast_to(peak, (mics, LANES))
            turns.append([turned(peak * (1.0 / LEVEL), i * width) for i in range(per_tile)])
            scale = LEVEL / peak
            for slot in range(k * mics, (k + 1) * mics):
                cov[block, slot] = turned(totals[slot] * scale, slot % per_tile * width)
        for to in range(block * per_tile, (block + 1) * per_tile):
            for k in range(rows):
                notes[to, k : k + 1, :] = packed_for(to, turns[k])[:1]
            for tile in range(deep):
                values = [cov[block, tile * per_tile + i] for i in range(per_tile)]
                whole = jnp.round(packed_for(to, values)).astype(jnp.int32)
                part[to, tile * mics : (tile + 1) * mics, :] = whole.astype(jnp.int16)
        for to in reversed(range(block * per_tile, (block + 1) * per_tile)):

            @pl.when(me != base + to)
            def _():
                offset = lax.rem(base + to + n - me, n)
                parcel(to, offset).start()
                note(to, offset).start()

    @pl.when(me > 0)
    def _():
        to_right.wait_recv()
        ext[:, :SPAN] = left[...].astype(jnp.float32)

    @pl.when(me == 0)
    def _():
        ext[:, :SPAN] = jnp.zeros((mics, SPAN), jnp.float32)

    transform_edge(0)
    for load in small:
        load.wait()
    channels = conv1_w.shape[1]
    kernel_one[...] = jnp.zeros_like(kernel_one)
    for a in range(3):
        for b in range(3):
            tap = conv1_w[3 * a + b : 3 * a + b + 1, :].astype(jnp.float32)
            for late in range(3):
                at = b * 8 + 2 * late + a
                kernel_one[at : at + 1, late * channels : (late + 1) * channels] = tap
    power[...] = jnp.zeros_like(power)
    lined[...] = jnp.zeros_like(lined)
    load_bank.wait()
    load_repeat.wait()
    coarse = bank[:MAIN, :].astype(jnp.bfloat16)
    split[:MAIN, :] = coarse
    split[MAIN : 2 * MAIN, :] = (bank[:MAIN, :] - coarse.astype(jnp.float32)).astype(jnp.bfloat16)
    split[2 * MAIN :, :] = coarse

    upper = mics // 2

    def folded(value):
        return jnp.where(
            lane < 2 * width,
            value,
            turned(pltpu.roll(value, mics - upper, axis=0), 2 * width),
        )

    def answer(offset, to, tall):
        return pltpu.make_async_remote_copy(
            src_ref=packed.at[:tall],
            dst_ref=gathered.at[me - base, :tall],
            send_sem=send_two.at[offset],
            recv_sem=recv_two.at[me - base],
            device_id={"tm": to},
            device_id_type=pl.DeviceIdType.MESH,
        )

    def answers(act):
        @pl.when(me == base)
        def _():
            for j in range(1, n):
                act(answer(j, lax.rem(me + j, n), mics))

        @pl.when(solving & (me != base))
        def _():
            for j in range(1, n):
                act(answer(j, lax.rem(me + j, n), upper))

    @pl.when(solving)
    def _():
        def levels(codes, held):
            codes = codes.astype(jnp.int32).astype(jnp.float32)
            return [
                codes[tile * mics : (tile + 1) * mics]
                * held[tile * per_tile // mics : tile * per_tile // mics + 1]
                for tile in range(deep)
            ]

        total = levels(part[me - base], notes[me - base])
        line = notes[me - base, rows : rows + 1]
        for j in range(1, n):
            parcel(0, j).wait_recv()
            note(0, j).wait_recv()
            total = [a + b for a, b in zip(total, levels(landed[j], noted[j]))]
            line = line + noted[j, rows : rows + 1]
        back = lax.rem(per_tile - lax.rem(me - base, per_tile), per_tile) * width
        total = [pltpu.roll(value, back, axis=1) for value in total]
        lasts = [
            jnp.sum(jnp.where(lane == mics * slot + sub, line, 0.0), axis=1, keepdims=True)
            for slot in range(extra)
        ]
        whole = []
        for slot in range(planes):
            tile = slot // per_tile
            plane = turned(total[tile], -(slot % per_tile) * width)
            k, place = slot // mics, slot % mics
            d = (place + 1) // 2
            if place == 0 or (place % 2 == 1 and d < half):
                at_last = lasts[k * (half + 1) + d]
            elif d == half:
                at_last = jnp.where(low, lasts[k * (half + 1) + d], 0.0)
            else:
                at_last = jnp.zeros((mics, LANES), jnp.float32)
            whole.append(jnp.where(lane == width, at_last, plane))
        real, imag = solve(whole, mics, full, mic_ref[0])
        main = folded(jnp.where(lane < width, real, turned(imag, width)))
        rest = folded(jnp.where(lane < width, turned(real, -width), imag))
        sent = jnp.where(sub < upper, main, pltpu.roll(rest, upper, axis=0))
        packed[...] = sent
        gathered[me - base] = sent

    answers(lambda copy: copy.start())

    @pl.when(me < n - 1)
    def _():
        to_right.wait_send()

    @pl.when(me > 0)
    def _():
        to_left.wait_send()

    for to in range(solvers):

        @pl.when(me != base + to)
        def _():
            pltpu.make_async_copy(
                packed.at[: mics if to == 0 else upper],
                gathered.at[to, : mics if to == 0 else upper],
                recv_two.at[to],
            ).wait()

    def unfolded(value):
        return jnp.where(
            sub < upper, value, turned(pltpu.roll(value, upper, axis=0), -2 * width)
        )

    for block in range(tiles):
        joined = [jnp.zeros((mics, LANES), jnp.float32)] * 2
        for t in range(per_tile):
            value = unfolded(gathered[block * per_tile + t])
            for i in range(2):
                moved = turned(value, (t - i) * width)
                joined[i] = moved if t == 0 else jnp.where(lane // width == t, moved, joined[i])
        for i in range(2):
            beam[i, :, block * LANES : (block + 1) * LANES] = joined[i]
    rest = unfolded(pltpu.roll(gathered[0], mics - upper, axis=0))
    for i in range(2):
        at_last = jnp.sum(jnp.where(lane == i * width, rest, 0.0), axis=1, keepdims=True)
        beam[i, :, MAIN:] = jnp.broadcast_to(at_last, (mics, LANES))

    stem(
        valid_ref[0],
        spec,
        bank,
        split,
        repeat,
        conv1_b,
        load_conv2,
        conv2_w,
        conv2_b,
        load_proj,
        proj_w,
        proj_b,
        out_ref,
        beam,
        power,
        spread,
        lined,
        kernel_one,
        patches,
        first,
    )
    for to in range(solvers):

        @pl.when(me != base + to)
        def _():
            parcel(to, 0).wait_send()
            note(to, 0).wait_send()

    answers(lambda copy: copy.wait_send())


def solve(planes, mics, full, ref):
    half = mics // 2
    for k in range(2):
        for m in range(mics):
            for d in range(half + 1):
                n = (m + d) % mics
                if d == half and m >= half:
                    continue

                def row(plane, at):
                    return planes[k * mics + plane][at : at + 1]

                if d == 0:
                    full[2 * k, m, m : m + 1, :] = row(0, m)
                    full[2 * k + 1, m, m : m + 1, :] = jnp.zeros((1, LANES), jnp.float32)
                    continue
                if d < half:
                    real, imag = row(2 * d - 1, m), row(2 * d, m)
                else:
                    real, imag = row(2 * d - 1, m), -row(2 * d - 1, m + half)
                full[2 * k, m, n : n + 1, :] = real
                full[2 * k + 1, m, n : n + 1, :] = imag
                full[2 * k, n, m : m + 1, :] = real
                full[2 * k + 1, n, m : m + 1, :] = -imag
    answer_re = [full[0, m] for m in range(mics)]
    answer_im = [full[1, m] for m in range(mics)]
    matrix_re = [full[2, m] for m in range(mics)]
    matrix_im = [full[3, m] for m in range(mics)]
    index = lax.broadcasted_iota(jnp.int32, (mics, LANES), 0)
    spread = matrix_re[0][0:1]
    for m in range(1, mics):
        spread = spread + matrix_re[m][m : m + 1]
    ridge = loading * spread / mics + epsilon
    matrix_re = [
        jnp.where(index == m, matrix_re[m] + ridge, matrix_re[m]) for m in range(mics)
    ]
    for p in range(mics):
        pivot_re, pivot_im = matrix_re[p][p : p + 1], matrix_im[p][p : p + 1]
        scale = 1.0 / (pivot_re * pivot_re + pivot_im * pivot_im)
        inverse_re, inverse_im = pivot_re * scale, -pivot_im * scale
        lead_re = matrix_re[p] * inverse_re - matrix_im[p] * inverse_im
        lead_im = matrix_re[p] * inverse_im + matrix_im[p] * inverse_re
        head_re = answer_re[p] * inverse_re - answer_im[p] * inverse_im
        head_im = answer_re[p] * inverse_im + answer_im[p] * inverse_re
        for m in range(mics):
            if m == p:
                continue
            column_re, column_im = matrix_re[m][p : p + 1], matrix_im[m][p : p + 1]
            matrix_re[m] = matrix_re[m] - (column_re * lead_re - column_im * lead_im)
            matrix_im[m] = matrix_im[m] - (column_re * lead_im + column_im * lead_re)
            answer_re[m] = answer_re[m] - (column_re * head_re - column_im * head_im)
            answer_im[m] = answer_im[m] - (column_re * head_im + column_im * head_re)
        matrix_re[p], matrix_im[p] = lead_re, lead_im
        answer_re[p], answer_im[p] = head_re, head_im
    trace = answer_re[0][0:1]
    for m in range(1, mics):
        trace = trace + answer_re[m][m : m + 1]
    scale = 1.0 / (trace + epsilon)
    picked = index == ref
    beam_re = jnp.zeros((mics, LANES), jnp.float32)
    beam_im = jnp.zeros((mics, LANES), jnp.float32)
    for m in range(mics):
        real = jnp.sum(jnp.where(picked, answer_re[m], 0.0), axis=0, keepdims=True)
        imag = jnp.sum(jnp.where(picked, answer_im[m], 0.0), axis=0, keepdims=True)
        beam_re = jnp.where(index == m, real * scale, beam_re)
        beam_im = jnp.where(index == m, imag * scale, beam_im)
    return beam_re, beam_im


def row_sums(values):
    count = len(values)
    sub = lax.broadcasted_iota(jnp.int32, values[0].shape, 0)
    step = count // 2
    while step:
        upper = sub // step % 2 == 1
        values = [
            jnp.where(
                upper,
                values[i + step] + pltpu.roll(values[i + step], step, axis=0),
                values[i] + pltpu.roll(values[i], count - step, axis=0),
            )
            for i in range(step)
        ]
        step //= 2
    return values[0]


def stem(
    valid,
    spec,
    bank,
    split,
    repeat,
    conv1_b,
    load_conv2,
    conv2_w,
    conv2_b,
    load_proj,
    proj_w,
    proj_b,
    out_ref,
    beam,
    power,
    spread,
    lined,
    kernel_one,
    patches,
    first,
):
    mics = beam.shape[1]
    quarter = out_ref.shape[0]
    groups = quarter + 1
    frames = quarter * GROUP
    stride = power.shape[0] // GROUP
    channels = conv2_w.shape[2]
    q_first = (MELS - 3) // 2 + 1
    q_second = (q_first - 3) // 2 + 1
    position = lax.axis_index("tm")
    for block in range(PADDED // LANES):
        lanes = pl.ds(block * LANES, LANES)
        beam_re = beam[0, :, lanes]
        beam_im = beam[1, :, lanes]

        def products(r, g):
            at = slice((r * groups + g) * mics, (r * groups + g + 1) * mics)
            if block < MAIN // LANES:
                re = spec[at, lanes]
                im = spec[at, pl.ds(MAIN + block * LANES, LANES)]
                return beam_re * re + beam_im * im, beam_re * im - beam_im * re
            re = spec[at, pl.ds(2 * MAIN, LANES)]
            return beam_re * re, -beam_im * re

        for r in range(GROUP):
            for g in range(0, groups - mics + 1, mics):
                pairs = [products(r, g + i) for i in range(mics)]
                real = row_sums([pair[0] for pair in pairs])
                imag = row_sums([pair[1] for pair in pairs])
                at = r * stride + g
                power[at : at + mics, lanes] = real * real + imag * imag
            for g in range(groups - groups % mics, groups):
                real, imag = products(r, g)
                real = jnp.sum(real, axis=0, keepdims=True)
                imag = jnp.sum(imag, axis=0, keepdims=True)
                at = r * stride + g
                power[at : at + 1, lanes] = real * real + imag * imag

    main = power[:, :MAIN]
    coarse = main.astype(jnp.bfloat16)
    fine = (main - coarse.astype(jnp.float32)).astype(jnp.bfloat16)
    melspec = (
        jnp.dot(
            jnp.concatenate([coarse, coarse, fine], axis=1),
            split[...],
            preferred_element_type=jnp.float32,
        )
        + power[:, MAIN:] * bank[MAIN : MAIN + 1, :]
    )
    row = lax.broadcasted_iota(jnp.int32, melspec.shape, 0)
    frame = position * frames + (row % stride - 1) * GROUP + row // stride
    alive = (frame >= 0) & (frame < valid)
    logmel = jnp.where(alive, jnp.log(melspec + epsilon), 0.0).astype(jnp.bfloat16)
    spread[...] = jnp.dot(logmel, repeat[...], preferred_element_type=jnp.float32)
    width = spread.shape[1]
    phase = lax.broadcasted_iota(jnp.int32, (quarter, width), 1) % 8
    mixed = jnp.zeros((quarter, width), jnp.float32)
    for u in range(7):
        start = (u + 1) % GROUP * stride + (u + 1) // GROUP
        mixed = jnp.where(phase == u, spread[start : start + quarter, :], mixed)
    lined[:, :width] = mixed
    order = list(range(0, q_first, 2)) + list(range(1, q_first, 2))
    for place, q in enumerate(order):
        base = 16 * q // LANES * LANES
        shift = 16 * q - base
        two = lined[:, base : base + 2 * LANES]
        if shift:
            two = pltpu.roll(two, 2 * LANES - shift, axis=1)
        patches[place * quarter : (place + 1) * quarter, :] = two[:, :LANES].astype(jnp.bfloat16)

    kernel_bf = kernel_one[...].astype(jnp.bfloat16)
    for late in range(3):
        lanes = slice(late * channels, (late + 1) * channels)
        one = jnp.dot(patches[...], kernel_bf[:, lanes], preferred_element_type=jnp.float32)
        one = jnp.maximum(one + conv1_b[...], 0.0)
        if late == 0:
            step = lax.broadcasted_iota(jnp.int32, one.shape, 0) % quarter
            one = jnp.where((step == 0) & (position == 0), 0.0, one)
        first[:, lanes] = one.astype(jnp.bfloat16)

    for load in load_conv2:
        load.wait()
    evens = (q_first + 1) // 2
    summed = jnp.zeros((q_second * quarter, channels), jnp.float32)
    for b in range(3):
        start = {0: 0, 1: evens, 2: 1}[b] * quarter
        summed = summed + jnp.dot(
            first[start : start + q_second * quarter, :],
            conv2_w[b],
            preferred_element_type=jnp.float32,
        )
    second = jnp.maximum(summed + conv2_b[...], 0.0).astype(jnp.bfloat16)
    load_proj.wait()
    joined = jnp.concatenate(
        [second[r * quarter : (r + 1) * quarter] for r in range(q_second)], axis=1
    )
    out = jnp.dot(joined, proj_w[...], preferred_element_type=jnp.float32)
    out_row = lax.broadcasted_iota(jnp.int32, out.shape, 0) + position * quarter
    out = jnp.where(GROUP * out_row < valid, out + proj_b[...], 0.0)
    out_ref[...] = out


def per_device(
    n, waveform, masks, valid, ref_mic, conv1_w, conv1_b, conv2_w, conv2_b, proj_w, proj_b
):
    mics, own = waveform.shape
    rows, frames = masks.shape[0], masks.shape[1]
    groups = frames // GROUP + 1
    quarter = frames // GROUP
    channels = conv1_w.shape[1]
    model = proj_w.shape[1]
    reach = WINDOW - SPAN
    vmem = pl.BlockSpec(memory_space=pltpu.VMEM)
    smem = pl.BlockSpec(memory_space=pltpu.SMEM)
    anywhere = pl.BlockSpec(memory_space=pltpu.HBM)
    planes = rows * mics
    solvers = min(SOLVERS, n)
    deep = -(-planes * (MAIN // solvers) // LANES)
    tall = deep * mics
    stride = -(-groups // 8) * 8
    q_first = (MELS - 3) // 2 + 1
    q_count = q_first * quarter
    features = pl.pallas_call(
        functools.partial(kernel, n),
        out_shape=jax.ShapeDtypeStruct((quarter, model), jnp.float32),
        in_specs=[smem] * 2 + [anywhere] * 5 + [anywhere, anywhere, anywhere, anywhere, anywhere, anywhere],
        out_specs=vmem,
        scratch_shapes=[
            pltpu.VMEM(conv1_w.shape, conv1_w.dtype),
            pltpu.VMEM((1, channels), jnp.float32),
            pltpu.VMEM((1, channels), jnp.float32),
            pltpu.VMEM((1, model), jnp.float32),
            pltpu.VMEM(waveform.shape, waveform.dtype),
            pltpu.VMEM(masks.shape, masks.dtype),
            pltpu.VMEM((NFFT, SPECTRUM), jnp.bfloat16),
            pltpu.VMEM((mics, SPAN + own + reach), jnp.float32),
            pltpu.VMEM((rows, frames, PADDED), jnp.float32),
            pltpu.VMEM((GROUP * groups * mics, SPECTRUM), jnp.float32),
            pltpu.VMEM((mics, SPAN), waveform.dtype),
            pltpu.VMEM((mics, reach), waveform.dtype),
            pltpu.VMEM((PADDED // LANES, planes, mics, LANES), jnp.float32),
            pltpu.VMEM((solvers, tall, LANES), jnp.int16),
            pltpu.VMEM((solvers, rows + 1, LANES), jnp.float32),
            pltpu.VMEM((n, tall, LANES), jnp.int16),
            pltpu.VMEM((n, rows + 1, LANES), jnp.float32),
            pltpu.VMEM((mics, LANES), jnp.float32),
            pltpu.VMEM((solvers, mics, LANES), jnp.float32),
            pltpu.VMEM((4, mics, mics, LANES), jnp.float32),
            pltpu.VMEM((PADDED, LANES), jnp.float32),
            pltpu.VMEM((3 * MAIN, LANES), jnp.bfloat16),
            pltpu.VMEM((LANES, MELS * 8), jnp.bfloat16),
            pltpu.VMEM((3, 3 * channels, channels), jnp.bfloat16),
            pltpu.VMEM(proj_w.shape, jnp.bfloat16),
            pltpu.VMEM((2, mics, PADDED), jnp.float32),
            pltpu.VMEM((GROUP * stride, PADDED), jnp.float32),
            pltpu.VMEM((GROUP * stride, MELS * 8), jnp.float32),
            pltpu.VMEM((quarter, MELS * 8 + LANES), jnp.float32),
            pltpu.VMEM((LANES, 3 * channels), jnp.float32),
            pltpu.VMEM((q_count, LANES), jnp.bfloat16),
            pltpu.VMEM((q_count, 3 * channels), jnp.bfloat16),
            pltpu.SemaphoreType.DMA((2,)),
            pltpu.SemaphoreType.DMA((2,)),
            pltpu.SemaphoreType.DMA((n,)),
            pltpu.SemaphoreType.DMA((n,)),
            pltpu.SemaphoreType.DMA((n,)),
            pltpu.SemaphoreType.DMA((n,)),
            pltpu.SemaphoreType.DMA((n,)),
            pltpu.SemaphoreType.DMA((n,)),
            pltpu.SemaphoreType.DMA((11,)),
            pltpu.SemaphoreType.DMA((9,)),
        ],
        compiler_params=pltpu.CompilerParams(
            collective_id=0, has_side_effects=True, vmem_limit_bytes=16 << 20
        ),
    )(
        valid,
        ref_mic,
        *(
            pltpu.with_memory_space_constraint(held, pltpu.HBM)
            for held in (
                waveform,
                masks,
                jnp.asarray(dft_table()),
                jnp.asarray(mel_bank()),
                jnp.asarray(repeat_table()),
                conv1_w,
                conv1_b[None],
                conv2_w,
                conv2_b[None],
                proj_w,
                proj_b[None],
            )
        ),
    )
    return features.astype(jnp.bfloat16)[None]


def solution(mesh):
    return jax.shard_map(
        functools.partial(per_device, mesh.shape["tm"]),
        mesh=mesh,
        in_specs=(
            P(None, ("meet", "tm")),
            P(None, ("meet", "tm"), None),
            P("meet"),
            P("meet"),
            P(),
            P(),
            P(),
            P(),
            P(),
            P(),
        ),
        out_specs=P(None, ("meet", "tm"), None),
        check_vma=False,
    )
```

```python
import functools
import math

import jax
import jax.numpy as jnp
import numpy as np
from jax import lax
from jax.experimental import pallas as pl
from jax.experimental.pallas import tpu as pltpu
from jax.sharding import PartitionSpec as P

NFFT = 512
HOP = 160
MELS = 80
BINS = NFFT // 2 + 1
LANES = 128
MAIN = BINS - 1
PADDED = MAIN + LANES
SPECTRUM = 2 * MAIN + LANES
GROUP = 4
SPAN = GROUP * HOP
WINDOW = 1024
SOLVERS = 8
LEVEL = 32000.0
TINY = 1e-30

loading = 0.03
epsilon = 1e-06
sample_rate = 16000.0


def dft_table():
    sample_pos = np.arange(NFFT)
    phase = (sample_pos[:, None] * np.arange(BINS)[None, :] % NFFT).astype(np.float32)
    phase = phase * np.float32(2.0 * math.pi / NFFT)
    ramp = sample_pos.astype(np.float32) * np.float32(2.0 * math.pi / NFFT)
    window = np.float32(0.5) - np.float32(0.5) * np.cos(ramp)
    cosines = window[:, None] * np.cos(phase)
    sines = -window[:, None] * np.sin(phase)
    table = np.zeros((NFFT, SPECTRUM), np.float32)
    table[:, :MAIN] = cosines[:, :MAIN]
    table[:, MAIN : 2 * MAIN] = sines[:, :MAIN]
    table[:, 2 * MAIN :] = cosines[:, MAIN:]
    return table.astype(jnp.bfloat16)


def mel_bank():
    mel_top = 2595.0 * math.log10(1.0 + sample_rate / 2.0 / 700.0)
    points = np.arange(MELS + 2) * (mel_top / (MELS + 1))
    edges_hz = 700.0 * (np.power(10.0, points / 2595.0) - 1.0)
    freq_hz = np.arange(BINS) * (sample_rate / 2.0 / (BINS - 1))
    lower, centre, upper = edges_hz[:-2], edges_hz[1:-1], edges_hz[2:]
    rising = (freq_hz[:, None] - lower[None, :]) / (centre - lower)[None, :]
    falling = (upper[None, :] - freq_hz[:, None]) / (upper - centre)[None, :]
    bank = np.zeros((PADDED, LANES), np.float32)
    bank[:BINS, :MELS] = np.maximum(np.minimum(rising, falling), 0.0)
    return bank


def repeat_table():
    table = np.zeros((LANES, MELS * 8), np.float32)
    for mel in range(MELS):
        table[mel, mel * 8 : mel * 8 + 8] = 1.0
    return table.astype(jnp.bfloat16)


def kernel(
    n,
    valid_ref,
    mic_ref,
    wave_hbm,
    masks_hbm,
    table_hbm,
    bank_hbm,
    repeat_hbm,
    conv1_w_hbm,
    conv1_b_hbm,
    conv2_hbm,
    conv2_b_hbm,
    proj_hbm,
    proj_b_hbm,
    out_ref,
    conv1_w,
    conv1_b,
    conv2_b,
    proj_b,
    wave,
    masks,
    table,
    ext,
    weight,
    spec,
    left,
    right,
    cov,
    part,
    notes,
    landed,
    noted,
    packed,
    gathered,
    full,
    bank,
    split,
    repeat,
    conv2_w,
    proj_w,
    beam,
    power,
    spread,
    lined,
    kernel_one,
    patches,
    first,
    nearby_send,
    nearby_recv,
    send_one,
    recv_one,
    send_note,
    recv_note,
    send_two,
    recv_two,
    loads,
    taps,
):
    rows, frames = masks.shape[0], masks.shape[1]
    mics, own = wave.shape
    groups = frames // GROUP + 1
    reach = right.shape[1]
    me = lax.axis_index("tm")
    solvers = part.shape[0]
    base = (n - solvers) // 2
    solving = (me >= base) & (me < base + solvers)
    load_wave = pltpu.make_async_copy(wave_hbm, wave, loads.at[0])
    load_table = pltpu.make_async_copy(table_hbm, table, loads.at[1])
    load_masks = pltpu.make_async_copy(masks_hbm, masks, loads.at[2])
    load_wave.start()
    load_table.start()
    load_masks.start()
    depth = conv2_hbm.shape[1]
    load_conv2 = [
        pltpu.make_async_copy(
            conv2_hbm.at[3 * late + b],
            conv2_w.at[b, late * depth : (late + 1) * depth],
            taps.at[3 * late + b],
        )
        for b in range(3)
        for late in range(3)
    ]
    load_proj = pltpu.make_async_copy(proj_hbm, proj_w, loads.at[4])
    load_bank = pltpu.make_async_copy(bank_hbm, bank, loads.at[5])
    load_repeat = pltpu.make_async_copy(repeat_hbm, repeat, loads.at[6])
    barrier = pltpu.get_barrier_semaphore()

    def greet(to):
        pl.semaphore_signal(
            barrier,
            inc=1,
            device_id={"tm": to},
            device_id_type=pl.DeviceIdType.MESH,
        )

    @pl.when(solving)
    def _():
        for j in (1, n - 1, *range(2, n - 1)):
            greet(lax.rem(me + j, n))

    @pl.when((me > 0) & jnp.logical_not(solving))
    def _():
        greet(me - 1)

    @pl.when((me < n - 1) & jnp.logical_not(solving))
    def _():
        greet(me + 1)

    def counted(here):
        return jnp.where(here, 1, 0).astype(jnp.int32)

    greeted = (
        solvers
        - counted(solving)
        + counted((me > 0) & ((me - 1 < base) | (me - 1 >= base + solvers)))
        + counted((me < n - 1) & ((me + 1 < base) | (me + 1 >= base + solvers)))
    )
    to_right = pltpu.make_async_remote_copy(
        src_ref=wave.at[:, own - SPAN :],
        dst_ref=left,
        send_sem=nearby_send.at[0],
        recv_sem=nearby_recv.at[0],
        device_id={"tm": lax.rem(me + 1, n)},
        device_id_type=pl.DeviceIdType.MESH,
    )
    to_left = pltpu.make_async_remote_copy(
        src_ref=wave.at[:, :reach],
        dst_ref=right,
        send_sem=nearby_send.at[1],
        recv_sem=nearby_recv.at[1],
        device_id={"tm": lax.rem(me + n - 1, n)},
        device_id_type=pl.DeviceIdType.MESH,
    )

    def meet():
        pl.semaphore_wait(barrier, greeted)

        @pl.when(me > 0)
        def _():
            to_left.start()

        @pl.when(me < n - 1)
        def _():
            to_right.start()

    late = me >= n - 2
    load_wave.wait()

    @pl.when(late)
    def _():
        meet()

    def transform(chosen):
        spans = jnp.concatenate(
            [ext[:, g * SPAN : g * SPAN + WINDOW] for g in chosen], axis=0
        )
        framed = jnp.concatenate(
            [
                (spans if r == 0 else pltpu.roll(spans, WINDOW - r * HOP, axis=1))[:, :NFFT]
                for r in range(GROUP)
            ],
            axis=0,
        ).astype(jnp.bfloat16)
        return jnp.dot(framed, table[...], preferred_element_type=jnp.float32)

    ext[:, SPAN : SPAN + own] = wave[...].astype(jnp.float32)
    load_table.wait()
    inner = list(range(1, groups - 1))
    found = transform(inner)
    width = len(inner) * mics
    for r in range(GROUP):
        spec[(r * groups + 1) * mics : (r * groups + 1) * mics + width, :] = found[
            r * width : (r + 1) * width
        ]

    @pl.when(jnp.logical_not(late) & (me >= base // 2))
    def _():
        meet()

    small = [
        pltpu.make_async_copy(source, held, loads.at[7 + i])
        for i, (source, held) in enumerate(
            (
                (conv1_w_hbm, conv1_w),
                (conv1_b_hbm, conv1_b),
                (conv2_b_hbm, conv2_b),
                (proj_b_hbm, proj_b),
            )
        )
    ]
    for load in small:
        load.start()
    load_bank.start()
    load_repeat.start()
    for load in load_conv2:
        load.start()
    load_proj.start()

    load_masks.wait()
    limit = valid_ref[0] - me * frames
    alive = lax.broadcasted_iota(jnp.int32, (frames, MAIN), 0) < limit
    for k in range(rows):
        level = masks[k].astype(jnp.float32) * (1.0 / 255.0)
        weight[k, :, :MAIN] = jnp.where(alive, level[:, :MAIN], 0.0)
        weight[k, :, MAIN:] = jnp.where(
            alive[:, :LANES], jnp.broadcast_to(level[:, MAIN:], (frames, LANES)), 0.0
        )

    half = mics // 2
    low = lax.broadcasted_iota(jnp.int32, (mics, LANES), 0) < half

    def frames_of(h):
        first_row = h * 2 * GROUP
        if not isinstance(h, int):
            first_row = pl.multiple_of(first_row, 2 * GROUP)
        places = []
        for i in range(2 * GROUP):
            at = ((i % GROUP) * groups + 1 + 2 * h + i // GROUP) * mics
            if not isinstance(h, int):
                at = pl.multiple_of(at, mics)
            places.append(pl.ds(at, mics))
        return pl.ds(first_row, 2 * GROUP), places

    def add_block(h, totals, block):
        totals = list(totals)
        lanes = pl.ds(block * LANES, LANES)
        lanes_im = pl.ds(MAIN + block * LANES, LANES)
        span, places = frames_of(h)
        held = [weight[k, span, lanes] for k in range(rows)]
        for i, at in enumerate(places):
            re = spec[at, lanes]
            im = spec[at, lanes_im]
            w = [held[k][i : i + 1] for k in range(rows)]
            place = 0
            for d in range(half + 1):
                if d == 0:
                    products = [re * re + im * im]
                else:
                    re_n = pltpu.roll(re, mics - d, axis=0)
                    im_n = pltpu.roll(im, mics - d, axis=0)
                    real = re * re_n + im * im_n
                    imag = im * re_n - re * im_n
                    products = [real, imag] if d < half else [jnp.where(low, real, imag)]
                for product in products:
                    for k in range(rows):
                        slot = k * mics + place
                        totals[slot] = totals[slot] + w[k] * product
                    place += 1
        return tuple(totals)

    across = lax.broadcasted_iota(jnp.int32, (mics, LANES), 1)

    def spread_last_bin(chosen, held):
        parts = [held] + [jnp.zeros((mics, LANES), jnp.float32)] * (GROUP - 1)
        for g in chosen:
            for r in range(GROUP):
                value = spec[pl.ds((r * groups + g) * mics, mics), pl.ds(2 * MAIN, LANES)]
                parts[r] = jnp.where(across == (g - 1) * GROUP + r, value, parts[r])
        return (parts[0] + parts[1]) + (parts[2] + parts[3])

    diagonal = lax.broadcasted_iota(jnp.int32, (frames, LANES), 0) == lax.broadcasted_iota(
        jnp.int32, (frames, LANES), 1
    )
    last_weight = [
        jnp.sum(jnp.where(diagonal, weight[k, :, MAIN:], 0.0), axis=0, keepdims=True)
        for k in range(rows)
    ]
    last_bin = spread_last_bin(inner, jnp.zeros((mics, LANES), jnp.float32))

    blocks = frames // (2 * GROUP)
    tiles = MAIN // LANES
    planes = rows * mics
    extra = rows * (half + 1)
    adders = [functools.partial(add_block, block=block) for block in range(tiles)]
    for block in range(tiles):
        zeros = tuple(jnp.zeros((mics, LANES), jnp.float32) for _ in range(planes))
        totals = lax.fori_loop(0, blocks - 1, adders[block], zeros)
        for slot in range(planes):
            cov[block, slot] = totals[slot]

    @pl.when(me < base // 2)
    def _():
        meet()

    @pl.when(me < n - 1)
    def _():
        to_left.wait_recv()
        ext[:, SPAN + own :] = right[...].astype(jnp.float32)

    @pl.when(me == n - 1)
    def _():
        ext[:, SPAN + own :] = jnp.zeros((mics, reach), jnp.float32)

    def transform_edge(g):
        found = transform([g])
        for r in range(GROUP):
            spec[(r * groups + g) * mics : (r * groups + g + 1) * mics, :] = found[
                r * mics : (r + 1) * mics
            ]

    transform_edge(groups - 1)
    lane = lax.broadcasted_iota(jnp.int32, (mics, LANES), 1)
    sub = lax.broadcasted_iota(jnp.int32, (mics, LANES), 0)
    width = MAIN // solvers
    per_tile = LANES // width
    deep = -(-planes // per_tile)

    def turned(value, amount):
        amount = amount % LANES
        return pltpu.roll(value, amount, axis=1) if amount else value

    last_bin = spread_last_bin([groups - 1], last_bin)
    totals = []
    for k in range(rows):
        for d in range(half + 1):
            product = last_bin * (last_bin if d == 0 else pltpu.roll(last_bin, mics - d, axis=0))
            totals.append(jnp.sum(product * last_weight[k], axis=1, keepdims=True))
    line = jnp.zeros((mics, LANES), jnp.float32)
    for slot in range(extra):
        line = jnp.where(lane == mics * slot + sub, totals[slot], line)
    line = jnp.sum(line, axis=0, keepdims=True)
    for to in range(solvers):
        notes[to, rows : rows + 1, :] = line
    group = lane // width

    def packed_for(to, values):
        packing = values[0]
        for i in range(1, per_tile):
            packing = jnp.where(group == (to + i) % per_tile, values[i], packing)
        return packing

    def parcel(to, offset):
        return pltpu.make_async_remote_copy(
            src_ref=part.at[to],
            dst_ref=landed.at[offset],
            send_sem=send_one.at[to],
            recv_sem=recv_one.at[offset],
            device_id={"tm": base + to},
            device_id_type=pl.DeviceIdType.MESH,
        )

    def note(to, offset):
        return pltpu.make_async_remote_copy(
            src_ref=notes.at[to],
            dst_ref=noted.at[offset],
            send_sem=send_note.at[to],
            recv_sem=recv_note.at[offset],
            device_id={"tm": base + to},
            device_id_type=pl.DeviceIdType.MESH,
        )

    for block in reversed(range(tiles)):
        totals = adders[block](blocks - 1, tuple(cov[block, slot] for slot in range(planes)))
        turns = []
        for k in range(rows):
            peak = jnp.maximum(jnp.max(totals[k * mics], axis=0, keepdims=True), TINY)
            peak = jnp.broadcast_to(peak, (mics, LANES))
            turns.append([turned(peak * (1.0 / LEVEL), i * width) for i in range(per_tile)])
            scale = LEVEL / peak
            for slot in range(k * mics, (k + 1) * mics):
                cov[block, slot] = turned(totals[slot] * scale, slot % per_tile * width)
        for to in range(block * per_tile, (block + 1) * per_tile):
            for k in range(rows):
                notes[to, k : k + 1, :] = packed_for(to, turns[k])[:1]
            for tile in range(deep):
                values = [cov[block, tile * per_tile + i] for i in range(per_tile)]
                whole = jnp.round(packed_for(to, values)).astype(jnp.int32)
                part[to, tile * mics : (tile + 1) * mics, :] = whole.astype(jnp.int16)
        for to in reversed(range(block * per_tile, (block + 1) * per_tile)):

            @pl.when(me != base + to)
            def _():
                offset = lax.rem(base + to + n - me, n)
                parcel(to, offset).start()
                note(to, offset).start()

    @pl.when(me > 0)
    def _():
        to_right.wait_recv()
        ext[:, :SPAN] = left[...].astype(jnp.float32)

    @pl.when(me == 0)
    def _():
        ext[:, :SPAN] = jnp.zeros((mics, SPAN), jnp.float32)

    transform_edge(0)
    for load in small:
        load.wait()
    channels = conv1_w.shape[1]
    kernel_one[...] = jnp.zeros_like(kernel_one)
    for a in range(3):
        for b in range(3):
            tap = conv1_w[3 * a + b : 3 * a + b + 1, :].astype(jnp.float32)
            for late in range(3):
                at = b * 8 + 2 * late + a
                kernel_one[at : at + 1, late * channels : (late + 1) * channels] = tap
    power[...] = jnp.zeros_like(power)
    lined[...] = jnp.zeros_like(lined)
    load_bank.wait()
    load_repeat.wait()
    coarse = bank[:MAIN, :].astype(jnp.bfloat16)
    split[:MAIN, :] = coarse
    split[MAIN : 2 * MAIN, :] = (bank[:MAIN, :] - coarse.astype(jnp.float32)).astype(jnp.bfloat16)
    split[2 * MAIN :, :] = coarse

    upper = mics // 2

    def folded(value):
        return jnp.where(
            lane < 2 * width,
            value,
            turned(pltpu.roll(value, mics - upper, axis=0), 2 * width),
        )

    def answer(to, tall):
        return pltpu.make_async_remote_copy(
            src_ref=packed.at[:tall],
            dst_ref=gathered.at[me - base, :tall],
            send_sem=send_two.at[to],
            recv_sem=recv_two.at[me - base],
            device_id={"tm": to},
            device_id_type=pl.DeviceIdType.MESH,
        )

    def answers(act):
        for to in range(n):

            if to != base:

                @pl.when(me == base)
                def _():
                    act(answer(to, mics))

            @pl.when(solving & (me != base) & (me != to))
            def _():
                act(answer(to, upper))

    @pl.when(solving)
    def _():
        def levels(codes, held):
            codes = codes.astype(jnp.int32).astype(jnp.float32)
            return [
                codes[tile * mics : (tile + 1) * mics]
                * held[tile * per_tile // mics : tile * per_tile // mics + 1]
                for tile in range(deep)
            ]

        total = levels(part[me - base], notes[me - base])
        line = notes[me - base, rows : rows + 1]
        for j in range(1, n):
            parcel(0, j).wait_recv()
            note(0, j).wait_recv()
            total = [a + b for a, b in zip(total, levels(landed[j], noted[j]))]
            line = line + noted[j, rows : rows + 1]
        back = lax.rem(per_tile - lax.rem(me - base, per_tile), per_tile) * width
        total = [pltpu.roll(value, back, axis=1) for value in total]
        lasts = [
            jnp.sum(jnp.where(lane == mics * slot + sub, line, 0.0), axis=1, keepdims=True)
            for slot in range(extra)
        ]
        whole = []
        for slot in range(planes):
            tile = slot // per_tile
            plane = turned(total[tile], -(slot % per_tile) * width)
            k, place = slot // mics, slot % mics
            d = (place + 1) // 2
            if place == 0 or (place % 2 == 1 and d < half):
                at_last = lasts[k * (half + 1) + d]
            elif d == half:
                at_last = jnp.where(low, lasts[k * (half + 1) + d], 0.0)
            else:
                at_last = jnp.zeros((mics, LANES), jnp.float32)
            whole.append(jnp.where(lane == width, at_last, plane))
        real, imag = solve(whole, mics, full, mic_ref[0])
        main = folded(jnp.where(lane < width, real, turned(imag, width)))
        rest = folded(jnp.where(lane < width, turned(real, -width), imag))
        sent = jnp.where(sub < upper, main, pltpu.roll(rest, upper, axis=0))
        packed[...] = sent
        gathered[me - base] = sent

    answers(lambda copy: copy.start())

    @pl.when(me < n - 1)
    def _():
        to_right.wait_send()

    @pl.when(me > 0)
    def _():
        to_left.wait_send()

    for to in range(solvers):

        @pl.when(me != base + to)
        def _():
            pltpu.make_async_copy(
                packed.at[: mics if to == 0 else upper],
                gathered.at[to, : mics if to == 0 else upper],
                recv_two.at[to],
            ).wait()

    def unfolded(value):
        return jnp.where(
            sub < upper, value, turned(pltpu.roll(value, upper, axis=0), -2 * width)
        )

    for block in range(tiles):
        joined = [jnp.zeros((mics, LANES), jnp.float32)] * 2
        for t in range(per_tile):
            value = unfolded(gathered[block * per_tile + t])
            for i in range(2):
                moved = turned(value, (t - i) * width)
                joined[i] = moved if t == 0 else jnp.where(lane // width == t, moved, joined[i])
        for i in range(2):
            beam[i, :, block * LANES : (block + 1) * LANES] = joined[i]
    rest = unfolded(pltpu.roll(gathered[0], mics - upper, axis=0))
    for i in range(2):
        at_last = jnp.sum(jnp.where(lane == i * width, rest, 0.0), axis=1, keepdims=True)
        beam[i, :, MAIN:] = jnp.broadcast_to(at_last, (mics, LANES))

    stem(
        valid_ref[0],
        spec,
        bank,
        split,
        repeat,
        conv1_b,
        load_conv2,
        conv2_w,
        conv2_b,
        load_proj,
        proj_w,
        proj_b,
        out_ref,
        beam,
        power,
        spread,
        lined,
        kernel_one,
        patches,
        first,
    )
    for to in range(solvers):

        @pl.when(me != base + to)
        def _():
            parcel(to, 0).wait_send()
            note(to, 0).wait_send()

    answers(lambda copy: copy.wait_send())


def solve(planes, mics, full, ref):
    half = mics // 2
    for k in range(2):
        for m in range(mics):
            for d in range(half + 1):
                n = (m + d) % mics
                if d == half and m >= half:
                    continue

                def row(plane, at):
                    return planes[k * mics + plane][at : at + 1]

                if d == 0:
                    full[2 * k, m, m : m + 1, :] = row(0, m)
                    full[2 * k + 1, m, m : m + 1, :] = jnp.zeros((1, LANES), jnp.float32)
                    continue
                if d < half:
                    real, imag = row(2 * d - 1, m), row(2 * d, m)
                else:
                    real, imag = row(2 * d - 1, m), -row(2 * d - 1, m + half)
                full[2 * k, m, n : n + 1, :] = real
                full[2 * k + 1, m, n : n + 1, :] = imag
                full[2 * k, n, m : m + 1, :] = real
                full[2 * k + 1, n, m : m + 1, :] = -imag
    answer_re = [full[0, m] for m in range(mics)]
    answer_im = [full[1, m] for m in range(mics)]
    matrix_re = [full[2, m] for m in range(mics)]
    matrix_im = [full[3, m] for m in range(mics)]
    index = lax.broadcasted_iota(jnp.int32, (mics, LANES), 0)
    spread = matrix_re[0][0:1]
    for m in range(1, mics):
        spread = spread + matrix_re[m][m : m + 1]
    ridge = loading * spread / mics + epsilon
    matrix_re = [
        jnp.where(index == m, matrix_re[m] + ridge, matrix_re[m]) for m in range(mics)
    ]
    for p in range(mics):
        pivot_re, pivot_im = matrix_re[p][p : p + 1], matrix_im[p][p : p + 1]
        scale = 1.0 / (pivot_re * pivot_re + pivot_im * pivot_im)
        inverse_re, inverse_im = pivot_re * scale, -pivot_im * scale
        lead_re = matrix_re[p] * inverse_re - matrix_im[p] * inverse_im
        lead_im = matrix_re[p] * inverse_im + matrix_im[p] * inverse_re
        head_re = answer_re[p] * inverse_re - answer_im[p] * inverse_im
        head_im = answer_re[p] * inverse_im + answer_im[p] * inverse_re
        for m in range(mics):
            if m == p:
                continue
            column_re, column_im = matrix_re[m][p : p + 1], matrix_im[m][p : p + 1]
            matrix_re[m] = matrix_re[m] - (column_re * lead_re - column_im * lead_im)
            matrix_im[m] = matrix_im[m] - (column_re * lead_im + column_im * lead_re)
            answer_re[m] = answer_re[m] - (column_re * head_re - column_im * head_im)
            answer_im[m] = answer_im[m] - (column_re * head_im + column_im * head_re)
        matrix_re[p], matrix_im[p] = lead_re, lead_im
        answer_re[p], answer_im[p] = head_re, head_im
    trace = answer_re[0][0:1]
    for m in range(1, mics):
        trace = trace + answer_re[m][m : m + 1]
    scale = 1.0 / (trace + epsilon)
    picked = index == ref
    beam_re = jnp.zeros((mics, LANES), jnp.float32)
    beam_im = jnp.zeros((mics, LANES), jnp.float32)
    for m in range(mics):
        real = jnp.sum(jnp.where(picked, answer_re[m], 0.0), axis=0, keepdims=True)
        imag = jnp.sum(jnp.where(picked, answer_im[m], 0.0), axis=0, keepdims=True)
        beam_re = jnp.where(index == m, real * scale, beam_re)
        beam_im = jnp.where(index == m, imag * scale, beam_im)
    return beam_re, beam_im


def row_sums(values):
    count = len(values)
    sub = lax.broadcasted_iota(jnp.int32, values[0].shape, 0)
    step = count // 2
    while step:
        upper = sub // step % 2 == 1
        values = [
            jnp.where(
                upper,
                values[i + step] + pltpu.roll(values[i + step], step, axis=0),
                values[i] + pltpu.roll(values[i], count - step, axis=0),
            )
            for i in range(step)
        ]
        step //= 2
    return values[0]


def stem(
    valid,
    spec,
    bank,
    split,
    repeat,
    conv1_b,
    load_conv2,
    conv2_w,
    conv2_b,
    load_proj,
    proj_w,
    proj_b,
    out_ref,
    beam,
    power,
    spread,
    lined,
    kernel_one,
    patches,
    first,
):
    mics = beam.shape[1]
    quarter = out_ref.shape[0]
    groups = quarter + 1
    frames = quarter * GROUP
    stride = power.shape[0] // GROUP
    channels = conv2_w.shape[2]
    q_first = (MELS - 3) // 2 + 1
    q_second = (q_first - 3) // 2 + 1
    position = lax.axis_index("tm")
    for block in range(PADDED // LANES):
        lanes = pl.ds(block * LANES, LANES)
        beam_re = beam[0, :, lanes]
        beam_im = beam[1, :, lanes]

        def products(r, g):
            at = slice((r * groups + g) * mics, (r * groups + g + 1) * mics)
            if block < MAIN // LANES:
                re = spec[at, lanes]
                im = spec[at, pl.ds(MAIN + block * LANES, LANES)]
                return beam_re * re + beam_im * im, beam_re * im - beam_im * re
            re = spec[at, pl.ds(2 * MAIN, LANES)]
            return beam_re * re, -beam_im * re

        for r in range(GROUP):
            for g in range(0, groups - mics + 1, mics):
                pairs = [products(r, g + i) for i in range(mics)]
                real = row_sums([pair[0] for pair in pairs])
                imag = row_sums([pair[1] for pair in pairs])
                at = r * stride + g
                power[at : at + mics, lanes] = real * real + imag * imag
            for g in range(groups - groups % mics, groups):
                real, imag = products(r, g)
                real = jnp.sum(real, axis=0, keepdims=True)
                imag = jnp.sum(imag, axis=0, keepdims=True)
                at = r * stride + g
                power[at : at + 1, lanes] = real * real + imag * imag

    main = power[:, :MAIN]
    coarse = main.astype(jnp.bfloat16)
    fine = (main - coarse.astype(jnp.float32)).astype(jnp.bfloat16)
    melspec = (
        jnp.dot(
            jnp.concatenate([coarse, coarse, fine], axis=1),
            split[...],
            preferred_element_type=jnp.float32,
        )
        + power[:, MAIN:] * bank[MAIN : MAIN + 1, :]
    )
    row = lax.broadcasted_iota(jnp.int32, melspec.shape, 0)
    frame = position * frames + (row % stride - 1) * GROUP + row // stride
    alive = (frame >= 0) & (frame < valid)
    logmel = jnp.where(alive, jnp.log(melspec + epsilon), 0.0).astype(jnp.bfloat16)
    spread[...] = jnp.dot(logmel, repeat[...], preferred_element_type=jnp.float32)
    width = spread.shape[1]
    phase = lax.broadcasted_iota(jnp.int32, (quarter, width), 1) % 8
    mixed = jnp.zeros((quarter, width), jnp.float32)
    for u in range(7):
        start = (u + 1) % GROUP * stride + (u + 1) // GROUP
        mixed = jnp.where(phase == u, spread[start : start + quarter, :], mixed)
    lined[:, :width] = mixed
    order = list(range(0, q_first, 2)) + list(range(1, q_first, 2))
    for place, q in enumerate(order):
        base = 16 * q // LANES * LANES
        shift = 16 * q - base
        two = lined[:, base : base + 2 * LANES]
        if shift:
            two = pltpu.roll(two, 2 * LANES - shift, axis=1)
        patches[place * quarter : (place + 1) * quarter, :] = two[:, :LANES].astype(jnp.bfloat16)

    kernel_bf = kernel_one[...].astype(jnp.bfloat16)
    for late in range(3):
        lanes = slice(late * channels, (late + 1) * channels)
        one = jnp.dot(patches[...], kernel_bf[:, lanes], preferred_element_type=jnp.float32)
        one = jnp.maximum(one + conv1_b[...], 0.0)
        if late == 0:
            step = lax.broadcasted_iota(jnp.int32, one.shape, 0) % quarter
            one = jnp.where((step == 0) & (position == 0), 0.0, one)
        first[:, lanes] = one.astype(jnp.bfloat16)

    for load in load_conv2:
        load.wait()
    evens = (q_first + 1) // 2
    summed = jnp.zeros((q_second * quarter, channels), jnp.float32)
    for b in range(3):
        start = {0: 0, 1: evens, 2: 1}[b] * quarter
        summed = summed + jnp.dot(
            first[start : start + q_second * quarter, :],
            conv2_w[b],
            preferred_element_type=jnp.float32,
        )
    second = jnp.maximum(summed + conv2_b[...], 0.0).astype(jnp.bfloat16)
    load_proj.wait()
    joined = jnp.concatenate(
        [second[r * quarter : (r + 1) * quarter] for r in range(q_second)], axis=1
    )
    out = jnp.dot(joined, proj_w[...], preferred_element_type=jnp.float32)
    out_row = lax.broadcasted_iota(jnp.int32, out.shape, 0) + position * quarter
    out = jnp.where(GROUP * out_row < valid, out + proj_b[...], 0.0)
    out_ref[...] = out


def per_device(
    n, waveform, masks, valid, ref_mic, conv1_w, conv1_b, conv2_w, conv2_b, proj_w, proj_b
):
    mics, own = waveform.shape
    rows, frames = masks.shape[0], masks.shape[1]
    groups = frames // GROUP + 1
    quarter = frames // GROUP
    channels = conv1_w.shape[1]
    model = proj_w.shape[1]
    reach = WINDOW - SPAN
    vmem = pl.BlockSpec(memory_space=pltpu.VMEM)
    smem = pl.BlockSpec(memory_space=pltpu.SMEM)
    anywhere = pl.BlockSpec(memory_space=pltpu.HBM)
    planes = rows * mics
    solvers = min(SOLVERS, n)
    deep = -(-planes * (MAIN // solvers) // LANES)
    tall = deep * mics
    stride = -(-groups // 8) * 8
    q_first = (MELS - 3) // 2 + 1
    q_count = q_first * quarter
    features = pl.pallas_call(
        functools.partial(kernel, n),
        out_shape=jax.ShapeDtypeStruct((quarter, model), jnp.float32),
        in_specs=[smem] * 2 + [anywhere] * 5 + [anywhere, anywhere, anywhere, anywhere, anywhere, anywhere],
        out_specs=vmem,
        scratch_shapes=[
            pltpu.VMEM(conv1_w.shape, conv1_w.dtype),
            pltpu.VMEM((1, channels), jnp.float32),
            pltpu.VMEM((1, channels), jnp.float32),
            pltpu.VMEM((1, model), jnp.float32),
            pltpu.VMEM(waveform.shape, waveform.dtype),
            pltpu.VMEM(masks.shape, masks.dtype),
            pltpu.VMEM((NFFT, SPECTRUM), jnp.bfloat16),
            pltpu.VMEM((mics, SPAN + own + reach), jnp.float32),
            pltpu.VMEM((rows, frames, PADDED), jnp.float32),
            pltpu.VMEM((GROUP * groups * mics, SPECTRUM), jnp.float32),
            pltpu.VMEM((mics, SPAN), waveform.dtype),
            pltpu.VMEM((mics, reach), waveform.dtype),
            pltpu.VMEM((MAIN // LANES, planes, mics, LANES), jnp.float32),
            pltpu.VMEM((solvers, tall, LANES), jnp.int16),
            pltpu.VMEM((solvers, rows + 1, LANES), jnp.float32),
            pltpu.VMEM((n, tall, LANES), jnp.int16),
            pltpu.VMEM((n, rows + 1, LANES), jnp.float32),
            pltpu.VMEM((mics, LANES), jnp.float32),
            pltpu.VMEM((solvers, mics, LANES), jnp.float32),
            pltpu.VMEM((4, mics, mics, LANES), jnp.float32),
            pltpu.VMEM((PADDED, LANES), jnp.float32),
            pltpu.VMEM((3 * MAIN, LANES), jnp.bfloat16),
            pltpu.VMEM((LANES, MELS * 8), jnp.bfloat16),
            pltpu.VMEM((3, 3 * channels, channels), jnp.bfloat16),
            pltpu.VMEM(proj_w.shape, jnp.bfloat16),
            pltpu.VMEM((2, mics, PADDED), jnp.float32),
            pltpu.VMEM((GROUP * stride, PADDED), jnp.float32),
            pltpu.VMEM((GROUP * stride, MELS * 8), jnp.float32),
            pltpu.VMEM((quarter, MELS * 8 + LANES), jnp.float32),
            pltpu.VMEM((LANES, 3 * channels), jnp.float32),
            pltpu.VMEM((q_count, LANES), jnp.bfloat16),
            pltpu.VMEM((q_count, 3 * channels), jnp.bfloat16),
            pltpu.SemaphoreType.DMA((2,)),
            pltpu.SemaphoreType.DMA((2,)),
            pltpu.SemaphoreType.DMA((n,)),
            pltpu.SemaphoreType.DMA((n,)),
            pltpu.SemaphoreType.DMA((n,)),
            pltpu.SemaphoreType.DMA((n,)),
            pltpu.SemaphoreType.DMA((n,)),
            pltpu.SemaphoreType.DMA((n,)),
            pltpu.SemaphoreType.DMA((11,)),
            pltpu.SemaphoreType.DMA((9,)),
        ],
        compiler_params=pltpu.CompilerParams(
            collective_id=0, has_side_effects=True, vmem_limit_bytes=16 << 20
        ),
    )(
        valid,
        ref_mic,
        *(
            pltpu.with_memory_space_constraint(held, pltpu.HBM)
            for held in (
                waveform,
                masks,
                jnp.asarray(dft_table()),
                jnp.asarray(mel_bank()),
                jnp.asarray(repeat_table()),
                conv1_w,
                conv1_b[None],
                conv2_w,
                conv2_b[None],
                proj_w,
                proj_b[None],
            )
        ),
    )
    return features.astype(jnp.bfloat16)[None]


def solution(mesh):
    return jax.shard_map(
        functools.partial(per_device, mesh.shape["tm"]),
        mesh=mesh,
        in_specs=(
            P(None, ("meet", "tm")),
            P(None, ("meet", "tm"), None),
            P("meet"),
            P("meet"),
            P(),
            P(),
            P(),
            P(),
            P(),
            P(),
        ),
        out_specs=P(None, ("meet", "tm"), None),
        check_vma=False,
    )
```

```python
import functools
import math

import jax
import jax.numpy as jnp
import numpy as np
from jax import lax
from jax.experimental import pallas as pl
from jax.experimental.pallas import tpu as pltpu
from jax.sharding import PartitionSpec as P

NFFT = 512
HOP = 160
MELS = 80
BINS = NFFT // 2 + 1
LANES = 128
MAIN = BINS - 1
PADDED = MAIN + LANES
SPECTRUM = 2 * MAIN + LANES
GROUP = 4
SPAN = GROUP * HOP
WINDOW = 1024
SOLVERS = 8
LEVEL = 32000.0
TINY = 1e-30

loading = 0.03
epsilon = 1e-06
sample_rate = 16000.0


def dft_table():
    sample_pos = np.arange(NFFT)
    phase = (sample_pos[:, None] * np.arange(BINS)[None, :] % NFFT).astype(np.float32)
    phase = phase * np.float32(2.0 * math.pi / NFFT)
    ramp = sample_pos.astype(np.float32) * np.float32(2.0 * math.pi / NFFT)
    window = np.float32(0.5) - np.float32(0.5) * np.cos(ramp)
    cosines = window[:, None] * np.cos(phase)
    sines = -window[:, None] * np.sin(phase)
    table = np.zeros((NFFT, SPECTRUM), np.float32)
    table[:, :MAIN] = cosines[:, :MAIN]
    table[:, MAIN : 2 * MAIN] = sines[:, :MAIN]
    table[:, 2 * MAIN :] = cosines[:, MAIN:]
    return table.astype(jnp.bfloat16)


def mel_bank():
    mel_top = 2595.0 * math.log10(1.0 + sample_rate / 2.0 / 700.0)
    points = np.arange(MELS + 2) * (mel_top / (MELS + 1))
    edges_hz = 700.0 * (np.power(10.0, points / 2595.0) - 1.0)
    freq_hz = np.arange(BINS) * (sample_rate / 2.0 / (BINS - 1))
    lower, centre, upper = edges_hz[:-2], edges_hz[1:-1], edges_hz[2:]
    rising = (freq_hz[:, None] - lower[None, :]) / (centre - lower)[None, :]
    falling = (upper[None, :] - freq_hz[:, None]) / (upper - centre)[None, :]
    bank = np.zeros((PADDED, LANES), np.float32)
    bank[:BINS, :MELS] = np.maximum(np.minimum(rising, falling), 0.0)
    return bank


def repeat_table():
    table = np.zeros((LANES, MELS * 8), np.float32)
    for mel in range(MELS):
        table[mel, mel * 8 : mel * 8 + 8] = 1.0
    return table.astype(jnp.bfloat16)


def kernel(
    n,
    valid_ref,
    mic_ref,
    wave_hbm,
    masks_hbm,
    table_hbm,
    bank_hbm,
    repeat_hbm,
    conv1_w_hbm,
    conv1_b_hbm,
    conv2_hbm,
    conv2_b_hbm,
    proj_hbm,
    proj_b_hbm,
    out_ref,
    conv1_w,
    conv1_b,
    conv2_b,
    proj_b,
    wave,
    masks,
    table,
    ext,
    weight,
    spec,
    left,
    right,
    cov,
    part,
    notes,
    landed,
    noted,
    packed,
    gathered,
    full,
    bank,
    split,
    repeat,
    conv2_w,
    proj_w,
    beam,
    power,
    spread,
    lined,
    kernel_one,
    patches,
    first,
    nearby_send,
    nearby_recv,
    send_one,
    recv_one,
    send_note,
    recv_note,
    send_two,
    recv_two,
    loads,
    taps,
):
    rows, frames = masks.shape[0], masks.shape[1]
    mics, own = wave.shape
    groups = frames // GROUP + 1
    reach = right.shape[1]
    me = lax.axis_index("tm")
    solvers = part.shape[0]
    base = (n - solvers) // 2
    solving = (me >= base) & (me < base + solvers)
    load_wave = pltpu.make_async_copy(wave_hbm, wave, loads.at[0])
    load_table = pltpu.make_async_copy(table_hbm, table, loads.at[1])
    load_masks = pltpu.make_async_copy(masks_hbm, masks, loads.at[2])
    load_wave.start()
    load_table.start()
    load_masks.start()
    depth = conv2_hbm.shape[1]
    load_conv2 = [
        pltpu.make_async_copy(
            conv2_hbm.at[3 * late + b],
            conv2_w.at[b, late * depth : (late + 1) * depth],
            taps.at[3 * late + b],
        )
        for b in range(3)
        for late in range(3)
    ]
    load_proj = pltpu.make_async_copy(proj_hbm, proj_w, loads.at[4])
    load_bank = pltpu.make_async_copy(bank_hbm, bank, loads.at[5])
    load_repeat = pltpu.make_async_copy(repeat_hbm, repeat, loads.at[6])
    barrier = pltpu.get_barrier_semaphore()

    def greet(to):
        pl.semaphore_signal(
            barrier,
            inc=1,
            device_id={"tm": to},
            device_id_type=pl.DeviceIdType.MESH,
        )

    @pl.when(solving)
    def _():
        for j in (1, n - 1, *range(2, n - 1)):
            greet(lax.rem(me + j, n))

    @pl.when((me > 0) & jnp.logical_not(solving))
    def _():
        greet(me - 1)

    @pl.when((me < n - 1) & jnp.logical_not(solving))
    def _():
        greet(me + 1)

    def counted(here):
        return jnp.where(here, 1, 0).astype(jnp.int32)

    greeted = (
        solvers
        - counted(solving)
        + counted((me > 0) & ((me - 1 < base) | (me - 1 >= base + solvers)))
        + counted((me < n - 1) & ((me + 1 < base) | (me + 1 >= base + solvers)))
    )
    to_right = pltpu.make_async_remote_copy(
        src_ref=wave.at[:, own - SPAN :],
        dst_ref=left,
        send_sem=nearby_send.at[0],
        recv_sem=nearby_recv.at[0],
        device_id={"tm": lax.rem(me + 1, n)},
        device_id_type=pl.DeviceIdType.MESH,
    )
    to_left = pltpu.make_async_remote_copy(
        src_ref=wave.at[:, :reach],
        dst_ref=right,
        send_sem=nearby_send.at[1],
        recv_sem=nearby_recv.at[1],
        device_id={"tm": lax.rem(me + n - 1, n)},
        device_id_type=pl.DeviceIdType.MESH,
    )

    def meet():
        pl.semaphore_wait(barrier, greeted)

        @pl.when(me > 0)
        def _():
            to_left.start()

        @pl.when(me < n - 1)
        def _():
            to_right.start()

    late = (me >= n // 2) & (lax.rem(me, 4) >= 2)
    load_wave.wait()

    @pl.when(late)
    def _():
        meet()

    def transform(chosen):
        spans = jnp.concatenate(
            [ext[:, g * SPAN : g * SPAN + WINDOW] for g in chosen], axis=0
        )
        framed = jnp.concatenate(
            [
                (spans if r == 0 else pltpu.roll(spans, WINDOW - r * HOP, axis=1))[:, :NFFT]
                for r in range(GROUP)
            ],
            axis=0,
        ).astype(jnp.bfloat16)
        return jnp.dot(framed, table[...], preferred_element_type=jnp.float32)

    ext[:, SPAN : SPAN + own] = wave[...].astype(jnp.float32)
    load_table.wait()
    inner = list(range(1, groups - 1))
    found = transform(inner)
    width = len(inner) * mics
    for r in range(GROUP):
        spec[(r * groups + 1) * mics : (r * groups + 1) * mics + width, :] = found[
            r * width : (r + 1) * width
        ]

    @pl.when(jnp.logical_not(late) & (me >= base // 2))
    def _():
        meet()

    small = [
        pltpu.make_async_copy(source, held, loads.at[7 + i])
        for i, (source, held) in enumerate(
            (
                (conv1_w_hbm, conv1_w),
                (conv1_b_hbm, conv1_b),
                (conv2_b_hbm, conv2_b),
                (proj_b_hbm, proj_b),
            )
        )
    ]
    for load in small:
        load.start()
    load_bank.start()
    load_repeat.start()
    for load in load_conv2:
        load.start()
    load_proj.start()

    load_masks.wait()
    limit = valid_ref[0] - me * frames
    alive = lax.broadcasted_iota(jnp.int32, (frames, MAIN), 0) < limit
    for k in range(rows):
        level = masks[k].astype(jnp.float32) * (1.0 / 255.0)
        weight[k, :, :MAIN] = jnp.where(alive, level[:, :MAIN], 0.0)
        weight[k, :, MAIN:] = jnp.where(
            alive[:, :LANES], jnp.broadcast_to(level[:, MAIN:], (frames, LANES)), 0.0
        )

    half = mics // 2
    low = lax.broadcasted_iota(jnp.int32, (mics, LANES), 0) < half

    def frames_of(h):
        first_row = h * 2 * GROUP
        if not isinstance(h, int):
            first_row = pl.multiple_of(first_row, 2 * GROUP)
        places = []
        for i in range(2 * GROUP):
            at = ((i % GROUP) * groups + 1 + 2 * h + i // GROUP) * mics
            if not isinstance(h, int):
                at = pl.multiple_of(at, mics)
            places.append(pl.ds(at, mics))
        return pl.ds(first_row, 2 * GROUP), places

    def add_block(h, totals, block):
        totals = list(totals)
        lanes = pl.ds(block * LANES, LANES)
        lanes_im = pl.ds(MAIN + block * LANES, LANES)
        span, places = frames_of(h)
        held = [weight[k, span, lanes] for k in range(rows)]
        for i, at in enumerate(places):
            re = spec[at, lanes]
            im = spec[at, lanes_im]
            w = [held[k][i : i + 1] for k in range(rows)]
            place = 0
            for d in range(half + 1):
                if d == 0:
                    products = [re * re + im * im]
                else:
                    re_n = pltpu.roll(re, mics - d, axis=0)
                    im_n = pltpu.roll(im, mics - d, axis=0)
                    real = re * re_n + im * im_n
                    imag = im * re_n - re * im_n
                    products = [real, imag] if d < half else [jnp.where(low, real, imag)]
                for product in products:
                    for k in range(rows):
                        slot = k * mics + place
                        totals[slot] = totals[slot] + w[k] * product
                    place += 1
        return tuple(totals)

    across = lax.broadcasted_iota(jnp.int32, (mics, LANES), 1)

    def spread_last_bin(chosen, held):
        parts = [held] + [jnp.zeros((mics, LANES), jnp.float32)] * (GROUP - 1)
        for g in chosen:
            for r in range(GROUP):
                value = spec[pl.ds((r * groups + g) * mics, mics), pl.ds(2 * MAIN, LANES)]
                parts[r] = jnp.where(across == (g - 1) * GROUP + r, value, parts[r])
        return (parts[0] + parts[1]) + (parts[2] + parts[3])

    diagonal = lax.broadcasted_iota(jnp.int32, (frames, LANES), 0) == lax.broadcasted_iota(
        jnp.int32, (frames, LANES), 1
    )
    last_weight = [
        jnp.sum(jnp.where(diagonal, weight[k, :, MAIN:], 0.0), axis=0, keepdims=True)
        for k in range(rows)
    ]
    last_bin = spread_last_bin(inner, jnp.zeros((mics, LANES), jnp.float32))

    blocks = frames // (2 * GROUP)
    tiles = MAIN // LANES
    planes = rows * mics
    extra = rows * (half + 1)
    adders = [functools.partial(add_block, block=block) for block in range(tiles)]
    for block in range(tiles):
        zeros = tuple(jnp.zeros((mics, LANES), jnp.float32) for _ in range(planes))
        totals = lax.fori_loop(0, blocks - 1, adders[block], zeros)
        for slot in range(planes):
            cov[block, slot] = totals[slot]

    @pl.when(me < base // 2)
    def _():
        meet()

    @pl.when(me < n - 1)
    def _():
        to_left.wait_recv()
        ext[:, SPAN + own :] = right[...].astype(jnp.float32)

    @pl.when(me == n - 1)
    def _():
        ext[:, SPAN + own :] = jnp.zeros((mics, reach), jnp.float32)

    def transform_edge(g):
        found = transform([g])
        for r in range(GROUP):
            spec[(r * groups + g) * mics : (r * groups + g + 1) * mics, :] = found[
                r * mics : (r + 1) * mics
            ]

    transform_edge(groups - 1)
    lane = lax.broadcasted_iota(jnp.int32, (mics, LANES), 1)
    sub = lax.broadcasted_iota(jnp.int32, (mics, LANES), 0)
    width = MAIN // solvers
    per_tile = LANES // width
    deep = -(-planes // per_tile)

    def turned(value, amount):
        amount = amount % LANES
        return pltpu.roll(value, amount, axis=1) if amount else value

    last_bin = spread_last_bin([groups - 1], last_bin)
    totals = []
    for k in range(rows):
        for d in range(half + 1):
            product = last_bin * (last_bin if d == 0 else pltpu.roll(last_bin, mics - d, axis=0))
            totals.append(jnp.sum(product * last_weight[k], axis=1, keepdims=True))
    line = jnp.zeros((mics, LANES), jnp.float32)
    for slot in range(extra):
        line = jnp.where(lane == mics * slot + sub, totals[slot], line)
    line = jnp.sum(line, axis=0, keepdims=True)
    for to in range(solvers):
        notes[to, rows : rows + 1, :] = line
    group = lane // width

    def packed_for(to, values):
        packing = values[0]
        for i in range(1, per_tile):
            packing = jnp.where(group == (to + i) % per_tile, values[i], packing)
        return packing

    def parcel(to, offset):
        return pltpu.make_async_remote_copy(
            src_ref=part.at[to],
            dst_ref=landed.at[offset],
            send_sem=send_one.at[to],
            recv_sem=recv_one.at[offset],
            device_id={"tm": base + to},
            device_id_type=pl.DeviceIdType.MESH,
        )

    def note(to, offset):
        return pltpu.make_async_remote_copy(
            src_ref=notes.at[to],
            dst_ref=noted.at[offset],
            send_sem=send_note.at[to],
            recv_sem=recv_note.at[offset],
            device_id={"tm": base + to},
            device_id_type=pl.DeviceIdType.MESH,
        )

    for block in reversed(range(tiles)):
        totals = adders[block](blocks - 1, tuple(cov[block, slot] for slot in range(planes)))
        turns = []
        for k in range(rows):
            peak = jnp.maximum(jnp.max(totals[k * mics], axis=0, keepdims=True), TINY)
            peak = jnp.broadcast_to(peak, (mics, LANES))
            turns.append([turned(peak * (1.0 / LEVEL), i * width) for i in range(per_tile)])
            scale = LEVEL / peak
            for slot in range(k * mics, (k + 1) * mics):
                cov[block, slot] = turned(totals[slot] * scale, slot % per_tile * width)
        for to in range(block * per_tile, (block + 1) * per_tile):
            for k in range(rows):
                notes[to, k : k + 1, :] = packed_for(to, turns[k])[:1]
            for tile in range(deep):
                values = [cov[block, tile * per_tile + i] for i in range(per_tile)]
                whole = jnp.round(packed_for(to, values)).astype(jnp.int32)
                part[to, tile * mics : (tile + 1) * mics, :] = whole.astype(jnp.int16)
        for to in reversed(range(block * per_tile, (block + 1) * per_tile)):

            @pl.when(me != base + to)
            def _():
                offset = lax.rem(base + to + n - me, n)
                parcel(to, offset).start()
                note(to, offset).start()

    @pl.when(me > 0)
    def _():
        to_right.wait_recv()
        ext[:, :SPAN] = left[...].astype(jnp.float32)

    @pl.when(me == 0)
    def _():
        ext[:, :SPAN] = jnp.zeros((mics, SPAN), jnp.float32)

    transform_edge(0)
    for load in small:
        load.wait()
    channels = conv1_w.shape[1]
    kernel_one[...] = jnp.zeros_like(kernel_one)
    for a in range(3):
        for b in range(3):
            tap = conv1_w[3 * a + b : 3 * a + b + 1, :].astype(jnp.float32)
            for late in range(3):
                at = b * 8 + 2 * late + a
                kernel_one[at : at + 1, late * channels : (late + 1) * channels] = tap
    power[...] = jnp.zeros_like(power)
    lined[...] = jnp.zeros_like(lined)
    load_bank.wait()
    load_repeat.wait()
    coarse = bank[:MAIN, :].astype(jnp.bfloat16)
    split[:MAIN, :] = coarse
    split[MAIN : 2 * MAIN, :] = (bank[:MAIN, :] - coarse.astype(jnp.float32)).astype(jnp.bfloat16)
    split[2 * MAIN :, :] = coarse

    upper = mics // 2

    def folded(value):
        return jnp.where(
            lane < 2 * width,
            value,
            turned(pltpu.roll(value, mics - upper, axis=0), 2 * width),
        )

    def answer(to, tall):
        return pltpu.make_async_remote_copy(
            src_ref=packed.at[:tall],
            dst_ref=gathered.at[me - base, :tall],
            send_sem=send_two.at[to],
            recv_sem=recv_two.at[me - base],
            device_id={"tm": to},
            device_id_type=pl.DeviceIdType.MESH,
        )

    def answers(act):
        for to in range(n):

            if to != base:

                @pl.when(me == base)
                def _():
                    act(answer(to, mics))

            @pl.when(solving & (me != base) & (me != to))
            def _():
                act(answer(to, upper))

    @pl.when(solving)
    def _():
        def levels(codes, held):
            codes = codes.astype(jnp.int32).astype(jnp.float32)
            return [
                codes[tile * mics : (tile + 1) * mics]
                * held[tile * per_tile // mics : tile * per_tile // mics + 1]
                for tile in range(deep)
            ]

        total = levels(part[me - base], notes[me - base])
        line = notes[me - base, rows : rows + 1]
        for j in range(1, n):
            parcel(0, j).wait_recv()
            note(0, j).wait_recv()
            total = [a + b for a, b in zip(total, levels(landed[j], noted[j]))]
            line = line + noted[j, rows : rows + 1]
        back = lax.rem(per_tile - lax.rem(me - base, per_tile), per_tile) * width
        total = [pltpu.roll(value, back, axis=1) for value in total]
        lasts = [
            jnp.sum(jnp.where(lane == mics * slot + sub, line, 0.0), axis=1, keepdims=True)
            for slot in range(extra)
        ]
        whole = []
        for slot in range(planes):
            tile = slot // per_tile
            plane = turned(total[tile], -(slot % per_tile) * width)
            k, place = slot // mics, slot % mics
            d = (place + 1) // 2
            if place == 0 or (place % 2 == 1 and d < half):
                at_last = lasts[k * (half + 1) + d]
            elif d == half:
                at_last = jnp.where(low, lasts[k * (half + 1) + d], 0.0)
            else:
                at_last = jnp.zeros((mics, LANES), jnp.float32)
            whole.append(jnp.where(lane == width, at_last, plane))
        real, imag = solve(whole, mics, full, mic_ref[0])
        main = folded(jnp.where(lane < width, real, turned(imag, width)))
        rest = folded(jnp.where(lane < width, turned(real, -width), imag))
        sent = jnp.where(sub < upper, main, pltpu.roll(rest, upper, axis=0))
        packed[...] = sent
        gathered[me - base] = sent

    answers(lambda copy: copy.start())

    @pl.when(me < n - 1)
    def _():
        to_right.wait_send()

    @pl.when(me > 0)
    def _():
        to_left.wait_send()

    for to in range(solvers):

        @pl.when(me != base + to)
        def _():
            pltpu.make_async_copy(
                packed.at[: mics if to == 0 else upper],
                gathered.at[to, : mics if to == 0 else upper],
                recv_two.at[to],
            ).wait()

    def unfolded(value):
        return jnp.where(
            sub < upper, value, turned(pltpu.roll(value, upper, axis=0), -2 * width)
        )

    for block in range(tiles):
        joined = [jnp.zeros((mics, LANES), jnp.float32)] * 2
        for t in range(per_tile):
            value = unfolded(gathered[block * per_tile + t])
            for i in range(2):
                moved = turned(value, (t - i) * width)
                joined[i] = moved if t == 0 else jnp.where(lane // width == t, moved, joined[i])
        for i in range(2):
            beam[i, :, block * LANES : (block + 1) * LANES] = joined[i]
    rest = unfolded(pltpu.roll(gathered[0], mics - upper, axis=0))
    for i in range(2):
        at_last = jnp.sum(jnp.where(lane == i * width, rest, 0.0), axis=1, keepdims=True)
        beam[i, :, MAIN:] = jnp.broadcast_to(at_last, (mics, LANES))

    stem(
        valid_ref[0],
        spec,
        bank,
        split,
        repeat,
        conv1_b,
        load_conv2,
        conv2_w,
        conv2_b,
        load_proj,
        proj_w,
        proj_b,
        out_ref,
        beam,
        power,
        spread,
        lined,
        kernel_one,
        patches,
        first,
    )
    for to in range(solvers):

        @pl.when(me != base + to)
        def _():
            parcel(to, 0).wait_send()
            note(to, 0).wait_send()

    answers(lambda copy: copy.wait_send())


def solve(planes, mics, full, ref):
    half = mics // 2
    for k in range(2):
        for m in range(mics):
            for d in range(half + 1):
                n = (m + d) % mics
                if d == half and m >= half:
                    continue

                def row(plane, at):
                    return planes[k * mics + plane][at : at + 1]

                if d == 0:
                    full[2 * k, m, m : m + 1, :] = row(0, m)
                    full[2 * k + 1, m, m : m + 1, :] = jnp.zeros((1, LANES), jnp.float32)
                    continue
                if d < half:
                    real, imag = row(2 * d - 1, m), row(2 * d, m)
                else:
                    real, imag = row(2 * d - 1, m), -row(2 * d - 1, m + half)
                full[2 * k, m, n : n + 1, :] = real
                full[2 * k + 1, m, n : n + 1, :] = imag
                full[2 * k, n, m : m + 1, :] = real
                full[2 * k + 1, n, m : m + 1, :] = -imag
    answer_re = [full[0, m] for m in range(mics)]
    answer_im = [full[1, m] for m in range(mics)]
    matrix_re = [full[2, m] for m in range(mics)]
    matrix_im = [full[3, m] for m in range(mics)]
    index = lax.broadcasted_iota(jnp.int32, (mics, LANES), 0)
    spread = matrix_re[0][0:1]
    for m in range(1, mics):
        spread = spread + matrix_re[m][m : m + 1]
    ridge = loading * spread / mics + epsilon
    matrix_re = [
        jnp.where(index == m, matrix_re[m] + ridge, matrix_re[m]) for m in range(mics)
    ]
    for p in range(mics):
        pivot_re, pivot_im = matrix_re[p][p : p + 1], matrix_im[p][p : p + 1]
        scale = 1.0 / (pivot_re * pivot_re + pivot_im * pivot_im)
        inverse_re, inverse_im = pivot_re * scale, -pivot_im * scale
        lead_re = matrix_re[p] * inverse_re - matrix_im[p] * inverse_im
        lead_im = matrix_re[p] * inverse_im + matrix_im[p] * inverse_re
        head_re = answer_re[p] * inverse_re - answer_im[p] * inverse_im
        head_im = answer_re[p] * inverse_im + answer_im[p] * inverse_re
        for m in range(mics):
            if m == p:
                continue
            column_re, column_im = matrix_re[m][p : p + 1], matrix_im[m][p : p + 1]
            matrix_re[m] = matrix_re[m] - (column_re * lead_re - column_im * lead_im)
            matrix_im[m] = matrix_im[m] - (column_re * lead_im + column_im * lead_re)
            answer_re[m] = answer_re[m] - (column_re * head_re - column_im * head_im)
            answer_im[m] = answer_im[m] - (column_re * head_im + column_im * head_re)
        matrix_re[p], matrix_im[p] = lead_re, lead_im
        answer_re[p], answer_im[p] = head_re, head_im
    trace = answer_re[0][0:1]
    for m in range(1, mics):
        trace = trace + answer_re[m][m : m + 1]
    scale = 1.0 / (trace + epsilon)
    picked = index == ref
    beam_re = jnp.zeros((mics, LANES), jnp.float32)
    beam_im = jnp.zeros((mics, LANES), jnp.float32)
    for m in range(mics):
        real = jnp.sum(jnp.where(picked, answer_re[m], 0.0), axis=0, keepdims=True)
        imag = jnp.sum(jnp.where(picked, answer_im[m], 0.0), axis=0, keepdims=True)
        beam_re = jnp.where(index == m, real * scale, beam_re)
        beam_im = jnp.where(index == m, imag * scale, beam_im)
    return beam_re, beam_im


def row_sums(values):
    count = len(values)
    sub = lax.broadcasted_iota(jnp.int32, values[0].shape, 0)
    step = count // 2
    while step:
        upper = sub // step % 2 == 1
        values = [
            jnp.where(
                upper,
                values[i + step] + pltpu.roll(values[i + step], step, axis=0),
                values[i] + pltpu.roll(values[i], count - step, axis=0),
            )
            for i in range(step)
        ]
        step //= 2
    return values[0]


def stem(
    valid,
    spec,
    bank,
    split,
    repeat,
    conv1_b,
    load_conv2,
    conv2_w,
    conv2_b,
    load_proj,
    proj_w,
    proj_b,
    out_ref,
    beam,
    power,
    spread,
    lined,
    kernel_one,
    patches,
    first,
):
    mics = beam.shape[1]
    quarter = out_ref.shape[0]
    groups = quarter + 1
    frames = quarter * GROUP
    stride = power.shape[0] // GROUP
    channels = conv2_w.shape[2]
    q_first = (MELS - 3) // 2 + 1
    q_second = (q_first - 3) // 2 + 1
    position = lax.axis_index("tm")
    for block in range(PADDED // LANES):
        lanes = pl.ds(block * LANES, LANES)
        beam_re = beam[0, :, lanes]
        beam_im = beam[1, :, lanes]

        def products(r, g):
            at = slice((r * groups + g) * mics, (r * groups + g + 1) * mics)
            if block < MAIN // LANES:
                re = spec[at, lanes]
                im = spec[at, pl.ds(MAIN + block * LANES, LANES)]
                return beam_re * re + beam_im * im, beam_re * im - beam_im * re
            re = spec[at, pl.ds(2 * MAIN, LANES)]
            return beam_re * re, -beam_im * re

        for r in range(GROUP):
            for g in range(0, groups - mics + 1, mics):
                pairs = [products(r, g + i) for i in range(mics)]
                real = row_sums([pair[0] for pair in pairs])
                imag = row_sums([pair[1] for pair in pairs])
                at = r * stride + g
                power[at : at + mics, lanes] = real * real + imag * imag
            for g in range(groups - groups % mics, groups):
                real, imag = products(r, g)
                real = jnp.sum(real, axis=0, keepdims=True)
                imag = jnp.sum(imag, axis=0, keepdims=True)
                at = r * stride + g
                power[at : at + 1, lanes] = real * real + imag * imag

    main = power[:, :MAIN]
    coarse = main.astype(jnp.bfloat16)
    fine = (main - coarse.astype(jnp.float32)).astype(jnp.bfloat16)
    melspec = (
        jnp.dot(
            jnp.concatenate([coarse, coarse, fine], axis=1),
            split[...],
            preferred_element_type=jnp.float32,
        )
        + power[:, MAIN:] * bank[MAIN : MAIN + 1, :]
    )
    row = lax.broadcasted_iota(jnp.int32, melspec.shape, 0)
    frame = position * frames + (row % stride - 1) * GROUP + row // stride
    alive = (frame >= 0) & (frame < valid)
    logmel = jnp.where(alive, jnp.log(melspec + epsilon), 0.0).astype(jnp.bfloat16)
    spread[...] = jnp.dot(logmel, repeat[...], preferred_element_type=jnp.float32)
    width = spread.shape[1]
    phase = lax.broadcasted_iota(jnp.int32, (quarter, width), 1) % 8
    mixed = jnp.zeros((quarter, width), jnp.float32)
    for u in range(7):
        start = (u + 1) % GROUP * stride + (u + 1) // GROUP
        mixed = jnp.where(phase == u, spread[start : start + quarter, :], mixed)
    lined[:, :width] = mixed
    order = list(range(0, q_first, 2)) + list(range(1, q_first, 2))
    for place, q in enumerate(order):
        base = 16 * q // LANES * LANES
        shift = 16 * q - base
        two = lined[:, base : base + 2 * LANES]
        if shift:
            two = pltpu.roll(two, 2 * LANES - shift, axis=1)
        patches[place * quarter : (place + 1) * quarter, :] = two[:, :LANES].astype(jnp.bfloat16)

    kernel_bf = kernel_one[...].astype(jnp.bfloat16)
    for late in range(3):
        lanes = slice(late * channels, (late + 1) * channels)
        one = jnp.dot(patches[...], kernel_bf[:, lanes], preferred_element_type=jnp.float32)
        one = jnp.maximum(one + conv1_b[...], 0.0)
        if late == 0:
            step = lax.broadcasted_iota(jnp.int32, one.shape, 0) % quarter
            one = jnp.where((step == 0) & (position == 0), 0.0, one)
        first[:, lanes] = one.astype(jnp.bfloat16)

    for load in load_conv2:
        load.wait()
    evens = (q_first + 1) // 2
    summed = jnp.zeros((q_second * quarter, channels), jnp.float32)
    for b in range(3):
        start = {0: 0, 1: evens, 2: 1}[b] * quarter
        summed = summed + jnp.dot(
            first[start : start + q_second * quarter, :],
            conv2_w[b],
            preferred_element_type=jnp.float32,
        )
    second = jnp.maximum(summed + conv2_b[...], 0.0).astype(jnp.bfloat16)
    load_proj.wait()
    joined = jnp.concatenate(
        [second[r * quarter : (r + 1) * quarter] for r in range(q_second)], axis=1
    )
    out = jnp.dot(joined, proj_w[...], preferred_element_type=jnp.float32)
    out_row = lax.broadcasted_iota(jnp.int32, out.shape, 0) + position * quarter
    out = jnp.where(GROUP * out_row < valid, out + proj_b[...], 0.0)
    out_ref[...] = out


def per_device(
    n, waveform, masks, valid, ref_mic, conv1_w, conv1_b, conv2_w, conv2_b, proj_w, proj_b
):
    mics, own = waveform.shape
    rows, frames = masks.shape[0], masks.shape[1]
    groups = frames // GROUP + 1
    quarter = frames // GROUP
    channels = conv1_w.shape[1]
    model = proj_w.shape[1]
    reach = WINDOW - SPAN
    vmem = pl.BlockSpec(memory_space=pltpu.VMEM)
    smem = pl.BlockSpec(memory_space=pltpu.SMEM)
    anywhere = pl.BlockSpec(memory_space=pltpu.HBM)
    planes = rows * mics
    solvers = min(SOLVERS, n)
    deep = -(-planes * (MAIN // solvers) // LANES)
    tall = deep * mics
    stride = -(-groups // 8) * 8
    q_first = (MELS - 3) // 2 + 1
    q_count = q_first * quarter
    features = pl.pallas_call(
        functools.partial(kernel, n),
        out_shape=jax.ShapeDtypeStruct((quarter, model), jnp.float32),
        in_specs=[smem] * 2 + [anywhere] * 5 + [anywhere, anywhere, anywhere, anywhere, anywhere, anywhere],
        out_specs=vmem,
        scratch_shapes=[
            pltpu.VMEM(conv1_w.shape, conv1_w.dtype),
            pltpu.VMEM((1, channels), jnp.float32),
            pltpu.VMEM((1, channels), jnp.float32),
            pltpu.VMEM((1, model), jnp.float32),
            pltpu.VMEM(waveform.shape, waveform.dtype),
            pltpu.VMEM(masks.shape, masks.dtype),
            pltpu.VMEM((NFFT, SPECTRUM), jnp.bfloat16),
            pltpu.VMEM((mics, SPAN + own + reach), jnp.float32),
            pltpu.VMEM((rows, frames, PADDED), jnp.float32),
            pltpu.VMEM((GROUP * groups * mics, SPECTRUM), jnp.float32),
            pltpu.VMEM((mics, SPAN), waveform.dtype),
            pltpu.VMEM((mics, reach), waveform.dtype),
            pltpu.VMEM((MAIN // LANES, planes, mics, LANES), jnp.float32),
            pltpu.VMEM((solvers, tall, LANES), jnp.int16),
            pltpu.VMEM((solvers, rows + 1, LANES), jnp.float32),
            pltpu.VMEM((n, tall, LANES), jnp.int16),
            pltpu.VMEM((n, rows + 1, LANES), jnp.float32),
            pltpu.VMEM((mics, LANES), jnp.float32),
            pltpu.VMEM((solvers, mics, LANES), jnp.float32),
            pltpu.VMEM((4, mics, mics, LANES), jnp.float32),
            pltpu.VMEM((PADDED, LANES), jnp.float32),
            pltpu.VMEM((3 * MAIN, LANES), jnp.bfloat16),
            pltpu.VMEM((LANES, MELS * 8), jnp.bfloat16),
            pltpu.VMEM((3, 3 * channels, channels), jnp.bfloat16),
            pltpu.VMEM(proj_w.shape, jnp.bfloat16),
            pltpu.VMEM((2, mics, PADDED), jnp.float32),
            pltpu.VMEM((GROUP * stride, PADDED), jnp.float32),
            pltpu.VMEM((GROUP * stride, MELS * 8), jnp.float32),
            pltpu.VMEM((quarter, MELS * 8 + LANES), jnp.float32),
            pltpu.VMEM((LANES, 3 * channels), jnp.float32),
            pltpu.VMEM((q_count, LANES), jnp.bfloat16),
            pltpu.VMEM((q_count, 3 * channels), jnp.bfloat16),
            pltpu.SemaphoreType.DMA((2,)),
            pltpu.SemaphoreType.DMA((2,)),
            pltpu.SemaphoreType.DMA((n,)),
            pltpu.SemaphoreType.DMA((n,)),
            pltpu.SemaphoreType.DMA((n,)),
            pltpu.SemaphoreType.DMA((n,)),
            pltpu.SemaphoreType.DMA((n,)),
            pltpu.SemaphoreType.DMA((n,)),
            pltpu.SemaphoreType.DMA((11,)),
            pltpu.SemaphoreType.DMA((9,)),
        ],
        compiler_params=pltpu.CompilerParams(
            collective_id=0, has_side_effects=True, vmem_limit_bytes=16 << 20
        ),
    )(
        valid,
        ref_mic,
        *(
            pltpu.with_memory_space_constraint(held, pltpu.HBM)
            for held in (
                waveform,
                masks,
                jnp.asarray(dft_table()),
                jnp.asarray(mel_bank()),
                jnp.asarray(repeat_table()),
                conv1_w,
                conv1_b[None],
                conv2_w,
                conv2_b[None],
                proj_w,
                proj_b[None],
            )
        ),
    )
    return features.astype(jnp.bfloat16)[None]


def solution(mesh):
    return jax.shard_map(
        functools.partial(per_device, mesh.shape["tm"]),
        mesh=mesh,
        in_specs=(
            P(None, ("meet", "tm")),
            P(None, ("meet", "tm"), None),
            P("meet"),
            P("meet"),
            P(),
            P(),
            P(),
            P(),
            P(),
            P(),
        ),
        out_specs=P(None, ("meet", "tm"), None),
        check_vma=False,
    )
```
